32 devices in a mesh: ep: 16 (over z, x, core), vp: 2 (over y).
Axes of the slice: x: 2, y: 2, z: 4, core: 2. Of those that a mesh axis runs over, the one named last changes fastest.
Arguments:
- prefill_tokens: bfloat16 [1024, 2048], P('ep'), may hold values from -6 to 6
- decode_tokens: bfloat16 [64, 2048], P('ep'), may hold values from -6 to 6
- request_order: int32 [64], replicated, may hold values from 0 to 63, each once
- prefill_lengths: int32 [16], P('ep'), may hold values from 1 to 256, 2048 in all
- decode_lengths: int32 [64], P('ep'), may hold values from 1 to 256, 8192 in all
- latent_cache: bfloat16 [80, 256, 576], P('ep'), may hold values from -6 to 6
- attn_gain: float32 [2048], replicated, may hold values from 0.1 to 1.9
- w_query: bfloat16 [2048, 1536], P(None, 'vp'), may hold values from -0.125 to 0.125
- w_latent: bfloat16 [2048, 576], replicated, may hold values from -0.125 to 0.125
- latent_gain: float32 [512], replicated, may hold values from 0.1 to 1.9
- key_up: bfloat16 [512, 1024], P(None, 'vp'), may hold values from -0.5 to 0.5
- value_up: bfloat16 [512, 1024], P(None, 'vp'), may hold values from -0.25 to 0.25
- w_out: bfloat16 [1024, 2048], P('vp'), may hold values from -0.1875 to 0.1875
- ffn_gain: float32 [2048], replicated, may hold values from 0.1 to 1.9
- expert_ids: int32 [1088, 6], P('ep'), may hold values from 0 to 15, all different within a row; in each aligned block of 68 rows (0 to 67, 68 to 135, ...) at most 51 rows name the same one
- expert_weights: float32 [1088, 6], P('ep'), may hold values from 0.05 to 0.45
- w_gate: bfloat16 [16, 2048, 1408], P('ep', None, 'vp'), may hold values from -0.125 to 0.125
- w_up: bfloat16 [16, 2048, 1408], P('ep', None, 'vp'), may hold values from -0.125 to 0.125
- w_down: bfloat16 [16, 1408, 2048], P('ep', 'vp'), may hold values from -0.15625 to 0.15625
- final_gain: float32 [2048], replicated, may hold values from 0.1 to 1.9
- head_weight: bfloat16 [2048, 51200], P(None, ('ep', 'vp')), may hold values from -0.375 to 0.375
Outputs:
- layer_out: bfloat16 [1088, 2048], P('ep', 'vp')
- logits: float32 [80, 51200], P(None, ('ep', 'vp'))
The draws below stay inside these ranges and needn't reach their ends.
Inputs may be any that keep to these rules, and one draw needn't show every extreme that they name: `request_order`: each decode request appears in exactly one batch slot. `prefill_lengths`: some prefill request has 256 cached positions. `decode_lengths`: some decode request has 256 cached positions. `expert_ids`: each row names 6 different experts. Among the rows of one owner no expert is named more than 51 times, and in some owner's rows one expert is named exactly 51 times.
All inputs are finite; a program needn't handle non-finite values. No bound on the sum of `prefill_lengths` or of `decode_lengths` on one device may be relied on, other than what follows from the above.
Results may differ from the reference program's by a relative error of at most 0.0086.
Values may be sent and summed in bfloat16 or wider, within the bound.
A program may use at most 128 MiB of HBM per device.

```python
import math
import jax
import jax.numpy as jnp
import numpy as np
from jax import lax

D = 2048
H = 8
NOPE = 128
ROPE = 64
VD = 128
LAT = 512
FFE = 1408
TOPK = 6
VOCAB = 51200
CTX = 256
PREFILL = 64
DECODE = 4
ROWS_DEV = 68
TOKENS = 1088
EXPERTS = 16
CAP = 51
N_EP = 16


def steps_of(own_key, shape, cuts, smallest, largest):
    level, own = 1.0, jax.random.fold_in(own_key, 6)
    for axis_at, parts in cuts:
        heights = jnp.exp(jax.random.uniform(jax.random.fold_in(own, axis_at), (parts,), jnp.float32, smallest / len(cuts), largest / len(cuts)))
        level = level * jnp.repeat(heights, shape[axis_at] // parts).reshape([-1 if axis == axis_at else 1 for axis in range(len(shape))])
    return level


def length_profile(amount, total, most, slope):
    loads = [(1 << 20) // math.isqrt(rank ** slope) + 1 for rank in range(2, amount + 1)]
    surplus, holding = total - most - (amount - 1), [1] * (amount - 1)
    while surplus > 0:
        movable = [i for i in range(amount - 1) if holding[i] < most]
        pool, remaining = sum([loads[i] for i in movable]), surplus
        for i in movable:
            more = min(most - holding[i], max(1, remaining * loads[i] // pool), surplus)
            holding[i] = holding[i] + more
            surplus = surplus - more
    return np.array([most] + holding)


def ragged(own_key, amount, total, limit, skew):
    if amount == 2:
        one = jax.random.randint(own_key, (), max(1, total - limit), min(limit, total - 1) + 1)
        return jnp.stack([one, total - one])
    sizes = jnp.asarray(length_profile(amount, total, limit, skew), jnp.int32)
    pairs = (amount - 1) // 2
    source_of, taker = sizes[1:1 + 2 * pairs:2], sizes[2:2 + 2 * pairs:2]
    slack = jnp.minimum(source_of - 1, limit - taker)
    moved = jax.random.randint(jax.random.fold_in(own_key, 1), (pairs,), 0, 1 << 20) % (slack + 1)
    sizes = sizes.at[1:1 + 2 * pairs:2].set(source_of - moved).at[2:2 + 2 * pairs:2].set(taker + moved)
    return sizes[jax.random.permutation(jax.random.fold_in(own_key, 2), amount)]


def routed_block(rng, own, number, rows, count, top, most, lean):
    order = jax.random.permutation(rng, count)
    heavy_load, common = shares(count, rows * top, most, lean, True), shares(count, rows * top, most, lean, False)
    places = jnp.arange(count)

    def named(sizes, rotation):
        used = int((sizes > 0).sum())
        fixed = max(1, used // 4)
        shifted = fixed + (places - fixed + rotation * (used - fixed)) % max(1, count - fixed)
        return jnp.zeros((count,), jnp.int32).at[order[jnp.where(places < fixed, places, shifted)]].set(jnp.asarray(sizes, jnp.int32))

    sizes = jnp.where(number % 4 == 0, named(heavy_load, number // 4), named(common, number - number // 4 - 1))
    mixed = jax.random.permutation(jax.random.fold_in(own, 3), count)
    donor, receiver = mixed[0:count // 2 * 2:2], mixed[1:count // 2 * 2:2]
    margin = jnp.minimum(sizes[donor] - 1, most - sizes[receiver]) // 2
    margin = jnp.where((donor == order[0]) | (receiver == order[0]) | (sizes[receiver] == 0), 0, jnp.maximum(margin, 0))
    shifted = jax.random.randint(jax.random.fold_in(own, 4), (count // 2,), 0, 1 << 20) % (margin + 1)
    sizes = sizes.at[donor].add(-shifted).at[receiver].add(shifted)
    items = jnp.searchsorted(jnp.cumsum(sizes), jnp.arange(rows * top), side="right").astype(jnp.int32)
    listing = items.reshape(top, rows).T
    listing = listing[jax.random.permutation(jax.random.fold_in(own, 1), rows)]
    rotation = jax.random.randint(jax.random.fold_in(own, 2), (rows, 1), 0, top)
    return jnp.take_along_axis(listing, (jnp.arange(top)[None, :] + rotation) % top, axis=1)


def shares(amount, total, reach, lean, full):
    portions = [(1 << 20) // math.isqrt(grade ** lean) + 1 for grade in range(1, amount + 1)]
    largest = reach if full else min(reach, max(-(-total // amount), total * portions[0] // sum(portions)))
    least = 1 if total - largest >= amount - 1 else 0
    counts, surplus = [largest] + [least] * (amount - 1), total - largest - least * (amount - 1)
    while surplus > 0:
        movable = [i for i in range(1, amount) if counts[i] < largest] or [i for i in range(1, amount) if counts[i] < reach]
        whole, remaining = sum([portions[i] for i in movable]), surplus
        for i in movable:
            extra = min(reach - counts[i], max(1, remaining * portions[i] // whole), surplus)
            counts[i] = counts[i] + extra
            surplus = surplus - extra
    return np.array(counts)


def scatter_about(key, dims, width, most, split=(), kind=jnp.bfloat16):
    result = jax.random.normal(key, dims, jnp.float32) * width
    if len(split) > 0:
        result = steps_of(key, dims, split, -0.22, 0.18) * result
    return jnp.clip(result, min=-most, max=most).astype(kind)


def setup_inputs(seed: int = 0) -> dict:
    key_of = jax.random.split(jax.random.key(seed), 22)
    prefill_tokens = scatter_about(key_of[0], (N_EP * PREFILL, D), 1.0, 6.0, ((0, 16),))
    decode_tokens = scatter_about(key_of[1], (N_EP * DECODE, D), 1.0, 6.0, ((0, 16),))
    request_order = jax.random.permutation(key_of[2], N_EP * DECODE).astype(jnp.int32)
    prefill_lengths = ragged(key_of[3], N_EP, N_EP * CTX // 2, CTX, 1).astype(jnp.int32)
    decode_lengths = ragged(key_of[4], N_EP * DECODE, N_EP * DECODE * CTX // 2, CTX, 1).astype(jnp.int32)
    latent_cache = scatter_about(key_of[5], (N_EP * (1 + DECODE), CTX, LAT + ROPE), 1.0, 6.0, ((0, 16),))
    attn_gain = jnp.clip(1.0 + 0.18 * jax.random.normal(key_of[6], (D,), jnp.float32), 0.1, 1.9)
    w_query = scatter_about(key_of[7], (D, H * (NOPE + ROPE)), D ** -0.5, 0.125, ((1, 2),))
    w_latent = scatter_about(key_of[8], (D, LAT + ROPE), D ** -0.5, 0.125)
    latent_gain = jnp.clip(1.0 + 0.18 * jax.random.normal(key_of[9], (LAT,), jnp.float32), 0.1, 1.9)
    key_up = scatter_about(key_of[10], (LAT, H * NOPE), NOPE ** -0.5, 0.5, ((1, 2),))
    value_up = scatter_about(key_of[11], (LAT, H * VD), LAT ** -0.5, 0.25, ((1, 2),))
    w_out = scatter_about(key_of[12], (H * VD, D), (H * VD) ** -0.5, 0.1875, ((0, 2),))
    ffn_gain = jnp.clip(1.0 + 0.18 * jax.random.normal(key_of[13], (D,), jnp.float32), 0.1, 1.9)
    expert_ids_keys = jax.random.split(jax.random.fold_in(key_of[14], 1), TOKENS // ROWS_DEV)
    expert_ids_turns = jax.random.permutation(jax.random.fold_in(key_of[14], 3), TOKENS // ROWS_DEV)
    expert_ids = jax.vmap(lambda own, number: routed_block(jax.random.fold_in(key_of[14], 2), own, number, ROWS_DEV, EXPERTS, TOPK, CAP, 2))(expert_ids_keys, expert_ids_turns).reshape((TOKENS, TOPK))
    expert_weights = jnp.clip(0.05 + 0.39999999 * jax.random.uniform(key_of[15], (TOKENS, TOPK), jnp.float32) ** steps_of(key_of[15], (TOKENS, TOPK), ((0, 16),), -0.2, 0.2), 0.05, 0.45)
    w_gate = scatter_about(key_of[16], (EXPERTS, D, FFE), D ** -0.5, 0.125, ((0, 16), (2, 2)))
    w_up = scatter_about(key_of[17], (EXPERTS, D, FFE), D ** -0.5, 0.125, ((0, 16), (2, 2)))
    w_down = scatter_about(key_of[18], (EXPERTS, FFE, D), FFE ** -0.5, 0.15625, ((0, 16), (1, 2)))
    final_gain = jnp.clip(1.0 + 0.18 * jax.random.normal(key_of[19], (D,), jnp.float32), 0.1, 1.9)
    head_weight = scatter_about(key_of[20], (D, VOCAB), (D // 9) ** -0.5, 0.375, ((1, 32),))
    return {"prefill_tokens": prefill_tokens, "decode_tokens": decode_tokens, "request_order": request_order, "prefill_lengths": prefill_lengths, "decode_lengths": decode_lengths, "latent_cache": latent_cache, "attn_gain": attn_gain, "w_query": w_query, "w_latent": w_latent, "latent_gain": latent_gain, "key_up": key_up, "value_up": value_up, "w_out": w_out, "ffn_gain": ffn_gain, "expert_ids": expert_ids, "expert_weights": expert_weights, "w_gate": w_gate, "w_up": w_up, "w_down": w_down, "final_gain": final_gain, "head_weight": head_weight}


epsilon = 1e-06
rope_base = 10000.0

def rms_norm(values, gain):
    return values * lax.rsqrt(lax.optimization_barrier(jnp.mean(values * values, axis=-1, keepdims=True)) + epsilon) * gain

def rotate(values, positions):
    half_width = values.shape[-1] // 2
    frequency = rope_base ** (-jnp.arange(half_width, dtype=jnp.float32) * 2.0 / values.shape[-1])
    angles = positions.astype(jnp.float32)[..., None] * frequency
    cosines = jnp.cos(angles)
    sines = jnp.sin(angles)
    lower_half = values[..., :half_width]
    upper_half = values[..., half_width:]
    return jnp.concatenate([lower_half * cosines - upper_half * sines, lower_half * sines + upper_half * cosines], axis=-1)

def attend(prefill_rows, decode_rows, cached, prefill_len, decode_len, attn_gain, w_query, w_latent, latent_gain, key_up, value_up, w_out):
    tokens = jnp.concatenate([prefill_rows, decode_rows], axis=0)
    prefill_count = prefill_rows.shape[0]
    row_count = tokens.shape[0]
    head_count = w_query.shape[1] // (NOPE + ROPE)
    positions = jnp.concatenate([prefill_len[0] + jnp.arange(prefill_count, dtype=jnp.int32), decode_len.astype(jnp.int32)])
    normed = rms_norm(tokens.astype(jnp.float32), attn_gain).astype(jnp.bfloat16)
    queries = jnp.dot(normed, w_query, preferred_element_type=jnp.float32).reshape(row_count, head_count, NOPE + ROPE)
    query_nope = queries[..., :NOPE].astype(jnp.bfloat16)
    query_rope = rotate(queries[..., NOPE:], positions[:, None]).astype(jnp.bfloat16)
    latent = jnp.dot(normed, w_latent, preferred_element_type=jnp.float32)
    latent_normed = rms_norm(latent[:, :LAT], latent_gain)
    new_keys = jnp.concatenate([latent_normed, rotate(latent[:, LAT:], positions)], axis=1).astype(jnp.bfloat16)
    key_heads = key_up.reshape(LAT, head_count, NOPE)
    absorbed = jnp.einsum('rhn,lhn->rhl', query_nope.astype(jnp.float32), key_heads.astype(jnp.float32)).astype(jnp.bfloat16)
    query_all = jnp.concatenate([absorbed, query_rope], axis=-1).astype(jnp.float32)
    factor = 1.0 / jnp.sqrt(jnp.float32(NOPE + ROPE))
    cache_len = cached.shape[1]
    prefill_keys = jnp.concatenate([cached[0], new_keys[:prefill_count]], axis=0).astype(jnp.float32)
    scores = jnp.einsum('chk,jk->chj', query_all[:prefill_count], prefill_keys) * factor
    key_index = jnp.arange(cache_len + prefill_count, dtype=jnp.int32)
    row_index = jnp.arange(prefill_count, dtype=jnp.int32)
    visible = jnp.where(key_index[None, :] < cache_len, key_index[None, :] < prefill_len[0], key_index[None, :] - cache_len <= row_index[:, None])
    expo = jnp.exp(jnp.where(visible[:, None, :], scores, -jnp.inf))
    attn_probs = (expo / lax.optimization_barrier(jnp.sum(expo, axis=-1, keepdims=True))).astype(jnp.bfloat16)
    prefill_context = jnp.einsum('chj,jl->chl', attn_probs.astype(jnp.float32), prefill_keys[:, :LAT]).astype(jnp.bfloat16)
    decode_query = query_all[prefill_count:]
    decode_cache = cached[1:].astype(jnp.float32)
    own_keys = new_keys[prefill_count:].astype(jnp.float32)
    cache_scores = jnp.einsum('dhk,dsk->dhs', decode_query, decode_cache) * factor
    self_scores = jnp.einsum('dhk,dk->dh', decode_query, own_keys) * factor
    cache_visible = jnp.arange(cache_len, dtype=jnp.int32)[None, :] < decode_len[:, None]
    cache_expo = jnp.exp(jnp.where(cache_visible[:, None, :], cache_scores, -jnp.inf))
    self_expo = jnp.exp(self_scores)
    totals = lax.optimization_barrier(jnp.sum(cache_expo, axis=-1)) + self_expo
    cache_probs = (cache_expo / totals[..., None]).astype(jnp.bfloat16)
    self_probs = (self_expo / totals).astype(jnp.bfloat16)
    decode_context = jnp.einsum('dhs,dsl->dhl', cache_probs.astype(jnp.float32), decode_cache[..., :LAT])
    decode_context = (decode_context + self_probs.astype(jnp.float32)[..., None] * own_keys[:, None, :LAT]).astype(jnp.bfloat16)
    context = jnp.concatenate([prefill_context, decode_context], axis=0)
    value_heads = value_up.reshape(LAT, head_count, VD)
    head_out = jnp.einsum('rhl,lhv->rhv', context.astype(jnp.float32), value_heads.astype(jnp.float32)).astype(jnp.bfloat16)
    return jnp.dot(head_out.reshape(row_count, head_count * VD), w_out, preferred_element_type=jnp.float32)

def reference(prefill_tokens, decode_tokens, request_order, prefill_lengths, decode_lengths, latent_cache, attn_gain, w_query, w_latent, latent_gain, key_up, value_up, w_out, ffn_gain, expert_ids, expert_weights, w_gate, w_up, w_down, final_gain, head_weight):
    prefill_blocks = prefill_tokens.reshape(N_EP, PREFILL, D)
    decode_blocks = decode_tokens.reshape(N_EP, DECODE, D)
    cache_blocks = latent_cache.reshape(N_EP, 1 + DECODE, CTX, LAT + ROPE)
    prefill_len_blocks = prefill_lengths.reshape(N_EP, 1)
    decode_len_blocks = decode_lengths.reshape(N_EP, DECODE)

    def per_owner(pieces):
        return attend(pieces[0], pieces[1], pieces[2], pieces[3], pieces[4], attn_gain, w_query, w_latent, latent_gain, key_up, value_up, w_out)
    attn = lax.map(per_owner, (prefill_blocks, decode_blocks, cache_blocks, prefill_len_blocks, decode_len_blocks))
    tokens = jnp.concatenate([prefill_blocks, decode_blocks], axis=1).reshape(TOKENS, D)
    resid = (tokens.astype(jnp.float32) + attn.reshape(TOKENS, D)).astype(jnp.bfloat16)
    ffn_in = rms_norm(resid.astype(jnp.float32), ffn_gain).astype(jnp.bfloat16)
    flat_ids = expert_ids.reshape(-1)
    flat_weights = expert_weights.reshape(-1)
    assignments = TOKENS * TOPK
    room = N_EP * CAP

    def one_expert(carry, expert_index):
        picks = jnp.nonzero(flat_ids == expert_index, size=room, fill_value=assignments)[0].astype(jnp.int32)
        valid = picks < assignments
        token_rows = jnp.minimum(picks // TOPK, TOKENS - 1)
        weight = jnp.where(valid, flat_weights[jnp.minimum(picks, assignments - 1)], 0.0)
        inputs = ffn_in[token_rows]
        gated = jnp.dot(inputs, w_gate[expert_index], preferred_element_type=jnp.float32)
        upward = jnp.dot(inputs, w_up[expert_index], preferred_element_type=jnp.float32)
        hidden_act = (jax.nn.silu(gated) * upward).astype(jnp.bfloat16)
        expert_out = jnp.dot(hidden_act, w_down[expert_index], preferred_element_type=jnp.float32)
        return (carry.at[token_rows].add(weight[:, None] * expert_out), None)
    routed, _ = lax.scan(one_expert, jnp.zeros((TOKENS, D), jnp.float32), jnp.arange(EXPERTS, dtype=jnp.int32))
    layer_out = (resid.astype(jnp.float32) + routed).astype(jnp.bfloat16)
    out_blocks = layer_out.reshape(N_EP, PREFILL + DECODE, D)
    prefill_last = out_blocks[:, PREFILL - 1]
    decode_rows = out_blocks[:, PREFILL:].reshape(N_EP * DECODE, D)[request_order]
    final_rows = jnp.concatenate([prefill_last, decode_rows], axis=0)
    final_normed = rms_norm(final_rows.astype(jnp.float32), final_gain).astype(jnp.bfloat16)
    logits = jnp.dot(final_normed, head_weight, preferred_element_type=jnp.float32)
    return (layer_out, logits)
```

```python
import functools

import jax
import jax.numpy as jnp
from jax import lax
from jax.experimental import pallas as pl
from jax.experimental.pallas import tpu as pltpu
from jax.sharding import PartitionSpec as P

NOPE = 128
ROPE = 64
VD = 128
LAT = 512
TOPK = 6


epsilon = 1e-06
rope_base = 10000.0


def rms_norm(values, gain):
    return values * lax.rsqrt(jnp.mean(values * values, axis=-1, keepdims=True) + epsilon) * gain


def rotate(values, positions):
    half_width = values.shape[-1] // 2
    frequency = rope_base ** (-jnp.arange(half_width, dtype=jnp.float32) * 2.0 / values.shape[-1])
    angles = positions.astype(jnp.float32)[..., None] * frequency
    cosines = jnp.cos(angles)
    sines = jnp.sin(angles)
    lower_half = values[..., :half_width]
    upper_half = values[..., half_width:]
    return jnp.concatenate(
        [lower_half * cosines - upper_half * sines, lower_half * sines + upper_half * cosines],
        axis=-1,
    )


def attend(
    prefill_rows,
    decode_rows,
    cached,
    prefill_len,
    decode_len,
    attn_gain,
    w_query,
    w_latent,
    latent_gain,
    key_up,
    value_up,
    w_out,
):
    tokens = jnp.concatenate([prefill_rows, decode_rows], axis=0)
    prefill_count = prefill_rows.shape[0]
    row_count = tokens.shape[0]
    head_count = w_query.shape[1] // (NOPE + ROPE)
    positions = jnp.concatenate(
        [prefill_len[0] + jnp.arange(prefill_count, dtype=jnp.int32), decode_len]
    )
    normed = rms_norm(tokens.astype(jnp.float32), attn_gain).astype(jnp.bfloat16)
    queries = jnp.dot(normed, w_query, preferred_element_type=jnp.float32).reshape(
        row_count, head_count, NOPE + ROPE
    )
    query_nope = queries[..., :NOPE].astype(jnp.bfloat16)
    query_rope = rotate(queries[..., NOPE:], positions[:, None]).astype(jnp.bfloat16)
    latent = jnp.dot(normed, w_latent, preferred_element_type=jnp.float32)
    latent_normed = rms_norm(latent[:, :LAT], latent_gain)
    new_keys = jnp.concatenate([latent_normed, rotate(latent[:, LAT:], positions)], axis=1).astype(
        jnp.bfloat16
    )
    key_heads = key_up.reshape(LAT, head_count, NOPE)
    absorbed = jnp.einsum(
        "rhn,lhn->rhl", query_nope, key_heads, preferred_element_type=jnp.float32
    ).astype(jnp.bfloat16)
    query_all = jnp.concatenate([absorbed, query_rope], axis=-1)
    factor = 1.0 / jnp.sqrt(jnp.float32(NOPE + ROPE))
    cache_len = cached.shape[1]
    prefill_keys = jnp.concatenate([cached[0], new_keys[:prefill_count]], axis=0)
    scores = (
        jnp.einsum(
            "chk,jk->chj",
            query_all[:prefill_count],
            prefill_keys,
            preferred_element_type=jnp.float32,
        )
        * factor
    )
    key_index = jnp.arange(cache_len + prefill_count, dtype=jnp.int32)
    row_index = jnp.arange(prefill_count, dtype=jnp.int32)
    visible = jnp.where(
        key_index[None, :] < cache_len,
        key_index[None, :] < prefill_len[0],
        key_index[None, :] - cache_len <= row_index[:, None],
    )
    expo = jnp.exp(jnp.where(visible[:, None, :], scores, -jnp.inf))
    attn_probs = (expo / jnp.sum(expo, axis=-1, keepdims=True)).astype(jnp.bfloat16)
    prefill_context = jnp.einsum(
        "chj,jl->chl", attn_probs, prefill_keys[:, :LAT], preferred_element_type=jnp.float32
    ).astype(jnp.bfloat16)
    decode_query = query_all[prefill_count:]
    decode_cache = cached[1:]
    own_keys = new_keys[prefill_count:]
    cache_scores = (
        jnp.einsum("dhk,dsk->dhs", decode_query, decode_cache, preferred_element_type=jnp.float32)
        * factor
    )
    self_scores = (
        jnp.einsum("dhk,dk->dh", decode_query, own_keys, preferred_element_type=jnp.float32)
        * factor
    )
    cache_visible = jnp.arange(cache_len, dtype=jnp.int32)[None, :] < decode_len[:, None]
    cache_expo = jnp.exp(jnp.where(cache_visible[:, None, :], cache_scores, -jnp.inf))
    self_expo = jnp.exp(self_scores)
    totals = jnp.sum(cache_expo, axis=-1) + self_expo
    cache_probs = (cache_expo / totals[..., None]).astype(jnp.bfloat16)
    self_probs = (self_expo / totals).astype(jnp.bfloat16)
    decode_context = jnp.einsum(
        "dhs,dsl->dhl", cache_probs, decode_cache[..., :LAT], preferred_element_type=jnp.float32
    )
    decode_context = (
        decode_context
        + self_probs.astype(jnp.float32)[..., None] * own_keys[:, None, :LAT].astype(jnp.float32)
    ).astype(jnp.bfloat16)
    context = jnp.concatenate([prefill_context, decode_context], axis=0)
    value_heads = value_up.reshape(LAT, head_count, VD)
    head_out = jnp.einsum(
        "rhl,lhv->rhv", context, value_heads, preferred_element_type=jnp.float32
    ).astype(jnp.bfloat16)
    return jnp.dot(
        head_out.reshape(row_count, head_count * VD), w_out, preferred_element_type=jnp.float32
    )


MESH = pl.DeviceIdType.MESH
SLAB = 80
PF = 64
FINAL = 8
HALF = 1024
CODE = 256


def place():
    e = lax.axis_index("ep")
    return e // 4, (e // 2) % 2, e % 2, lax.axis_index("vp")


def at(z, x, c, y):
    return {"ep": z * 4 + x * 2 + c, "vp": y}


def remote(src, dst, send, recv, target):
    return pltpu.make_async_remote_copy(
        src_ref=src, dst_ref=dst, send_sem=send, recv_sem=recv, device_id=target, device_id_type=MESH
    )


def moe_kernel(part, tok, gain, last_gain, code, slots, wg_hbm, wu_hbm, wd_hbm, hw_hbm, out, logits, *scratch):
    (wg, wu, wd, hw, got, slab, prod, cin, xin, yin, t0, t1, y2, x2, s3, zin) = scratch[:16]
    (xn, hid, fb, pf, fcin, fxin, f2, fyin, f3, fzin, fg, rf, fn) = scratch[16:29]
    (w_sem, sw_s, sw_r, gz_s, gz_r, fz_s, fz_r, g_s, g_r, o_s, o_r, one_s, one_r) = scratch[29:42]
    (r_s, r_r, rz_s, rz_r, fr_s, fr_r, lz_s, lz_r) = scratch[42:]
    f32, bf16 = jnp.float32, jnp.bfloat16
    nt = lambda a, b: lax.dot_general(a, b, (((1,), (1,)), ((), ())), preferred_element_type=f32)
    z, x, c, y = place()
    mine = z * 4 + x * 2 + c
    near = z + 1 - 2 * (z % 2)
    planes = [z, near, 2 - z // 2, 3 - 3 * (z // 2)]
    to_x, to_y, to_c = at(z, 1 - x, c, y), at(z, x, c, 1 - y), at(z, x, 1 - c, y)

    def along(zo):
        return at(zo, x, c, y)

    pairs = [(wg_hbm, wg), (wu_hbm, wu), (wd_hbm, wd), (hw_hbm, hw)]
    loads = [pltpu.make_async_copy(a, b, w_sem.at[i]) for i, (a, b) in enumerate(pairs)]
    for load in loads:
        load.start()
    barrier = pltpu.get_barrier_semaphore()
    for target in [to_x, to_y, to_c] + [along(zo) for zo in planes[1:]]:
        pl.semaphore_signal(barrier, inc=1, device_id=target, device_id_type=MESH)
    pl.semaphore_wait(barrier, 6)
    sent = []

    def send(copy):
        copy.start()
        sent.append(copy)

    def cols(h):
        return pl.ds(pl.multiple_of(h * HALF, HALF), HALF)

    def swap(i, h_out, h_in):
        if i == 0:
            s = part.at[PF:SLAB, :]
            g = got.at[PF:SLAB, :]
            return remote(s, g, sw_s.at[0], sw_r.at[0], to_y), remote(s, g, sw_s.at[0], sw_r.at[0], to_y)
        leave = part.at[0:PF, cols(h_out)]
        return (
            remote(leave, got.at[0:PF, cols(h_out)], sw_s.at[i], sw_r.at[i], to_y),
            remote(leave, got.at[0:PF, cols(h_in)], sw_s.at[i], sw_r.at[i], to_y),
        )

    swaps = [swap(0, y, y), swap(1, 1 - y, y), swap(2, y, 1 - y)]
    for s in swaps:
        send(s[0])

    def same(ref_out, ref_in, s, r, target):
        return remote(ref_out, ref_out, s, r, target), remote(ref_in, ref_in, s, r, target)

    def gz(i):
        zo = planes[i]
        a, b = slab.at[z, c, x, y], slab.at[zo, c, x, y]
        return remote(a, a, gz_s.at[i - 1], gz_r.at[z], along(zo)), remote(b, b, gz_s.at[i - 1], gz_r.at[zo], along(zo))

    def fz(i):
        zo = planes[i]
        a, b = fb.at[c, x, z], fb.at[c, x, zo]
        return remote(a, a, fz_s.at[i - 1], fz_r.at[z], along(zo)), remote(b, b, fz_s.at[i - 1], fz_r.at[zo], along(zo))

    def own(i):
        h = y if i == 0 else 1 - y
        return same(slab.at[z, c, x, h], slab.at[z, c, 1 - x, h], o_s.at[i], o_r.at[i], to_x)

    def gx(i):
        zo = planes[i]
        return same(slab.at[zo, c, x, y], slab.at[zo, c, 1 - x, y], g_s.at[0, i], g_r.at[0, i], to_x)

    def gy(i):
        zo = planes[i]
        return same(slab.at[zo, c, x, y], slab.at[zo, c, x, 1 - y], g_s.at[1, i], g_r.at[1, i], to_y)

    def dx(i):
        zo = planes[i]
        return same(
            slab.at[zo, c, x, 1 - y, 32:64], slab.at[zo, c, 1 - x, 1 - y, 32:64], g_s.at[2, i], g_r.at[2, i], to_x
        )

    def dy(i):
        zo = planes[i]
        return same(
            slab.at[zo, c, 1 - x, y, 0:32], slab.at[zo, c, 1 - x, 1 - y, 0:32], g_s.at[3, i], g_r.at[3, i], to_y
        )

    def gc(i):
        zo = planes[i]
        return same(slab.at[zo, c], slab.at[zo, 1 - c], g_s.at[4, i], g_r.at[4, i], to_c)

    def fx():
        return same(fb.at[c, x], fb.at[c, 1 - x], one_s.at[0], one_r.at[0], to_x)

    def fc():
        return same(fb.at[c], fb.at[1 - c], one_s.at[1], one_r.at[1], to_c)

    swaps[0][1].wait_recv()
    rows = tok[PF : PF + FINAL, :].astype(f32) + (
        part[PF:SLAB, :].astype(f32)[:FINAL] + got[PF:SLAB, :].astype(f32)[:FINAL]
    )
    fb[c, x, z, :, 0:HALF] = jnp.concatenate([rows[:, :HALF], rows[:, HALF:]], axis=0).astype(bf16)
    fb[c, x, z, :, HALF : HALF + CODE] = code[...]
    for i in range(1, 4):
        send(fz(i)[0])

    def fill(h):
        attn = part[0:PF, cols(h)].astype(f32) + got[0:PF, cols(h)].astype(f32)
        slab[z, c, x, h] = (tok[0:PF, cols(h)].astype(f32) + attn).astype(bf16)

    swaps[1][1].wait_recv()
    fill(y)
    for i in range(1, 4):
        send(gz(i)[0])
    send(own(0)[0])
    swaps[2][1].wait_recv()
    fill(1 - y)
    send(own(1)[0])

    def take(pair):
        pair[1].wait_recv()

    def spread(i):
        take(gz(i))
        send(gx(i)[0])
        send(gy(i)[0])

    def corner(i):
        take(gx(i))
        send(dy(i)[0])
        take(gy(i))
        send(dx(i)[0])

    def close(i):
        take(dx(i))
        take(dy(i))
        send(gc(i)[0])

    width = 2 * HALF

    def normalize(top, first, second):
        total = jnp.sum(first * first, axis=1, keepdims=True) + jnp.sum(second * second, axis=1, keepdims=True)
        scale = lax.rsqrt(total * (1.0 / width) + epsilon)
        count = first.shape[0]
        xn[top : top + count, 0:HALF] = (first * scale * gain[:, 0:HALF]).astype(bf16)
        xn[top : top + count, HALF:width] = (second * scale * gain[:, HALF:width]).astype(bf16)

    def gates_of(co, xo, zo, first, count):
        block = fb[co, xo, zo, :, HALF : HALF + CODE].astype(f32)
        expert = lax.broadcasted_iota(jnp.int32, block.shape, 0)
        row = jnp.sum(jnp.where(expert == mine, block, 0.0), axis=0, keepdims=True)
        row = row[:, 0:128] + row[:, 128:256]
        lane = lax.broadcasted_iota(jnp.int32, (count, 128), 1)
        index = lax.broadcasted_iota(jnp.int32, (count, 128), 0)
        return jnp.sum(jnp.where(lane == index + first, row, 0.0), axis=1, keepdims=True)

    units = wg.shape[0]

    def expand(count):
        lo = 0
        while lo < units:
            n = min(256, units - lo)
            gated = nt(xn[0:count, :], wg[lo : lo + n, :])
            upward = nt(xn[0:count, :], wu[lo : lo + n, :])
            hid[0:count, lo : lo + n] = (jax.nn.silu(gated) * upward).astype(bf16)
            lo += n

    def contract(count, gates, store):
        for lo in range(0, width, 512):
            result = jnp.dot(hid[0:count, :], wd[:, lo : lo + 512], preferred_element_type=f32) * gates
            store(lo, result.astype(bf16))

    def enter(i):
        zo = planes[i]
        for s, (co, xo) in enumerate([(0, 0), (0, 1), (1, 0), (1, 1)]):
            normalize(s * PF, slab[zo, co, xo, 0].astype(f32), slab[zo, co, xo, 1].astype(f32))
        expand(4 * PF)

    def leave(i):
        zo = planes[i]
        gates = jnp.concatenate([gates_of(co, xo, zo, 0, PF) for co in range(2) for xo in range(2)], axis=0)

        def store(lo, result):
            h, at_col = lo // HALF, lo % HALF
            for s in range(4):
                prod[zo, s // 2, s % 2, h, :, at_col : at_col + 512] = result[s * PF : (s + 1) * PF]

        contract(4 * PF, gates, store)

    def add(a, b):
        return (a.astype(f32) + b.astype(f32)).astype(bf16)

    def rc(i):
        zo = planes[i]
        a = prod.at[zo, 1 - c]
        p = remote(a, cin.at[i], r_s.at[0, i], r_r.at[0, i], to_c)
        return p, p

    def rx1(i):
        p = remote(prod.at[planes[i], c, 1 - x, :, 0:32], xin.at[i], r_s.at[1, i], r_r.at[1, i], to_x)
        return p, p

    def ry1(i):
        p = remote(prod.at[planes[i], c, :, 1 - y, 32:64], yin.at[i], r_s.at[2, i], r_r.at[2, i], to_y)
        return p, p

    def ry2(i):
        p = remote(t0.at[i, 1 - y], y2.at[i], r_s.at[3, i], r_r.at[3, i], to_y)
        return p, p

    def rx2(i):
        p = remote(t1.at[i, 1 - x], x2.at[i], r_s.at[4, i], r_r.at[4, i], to_x)
        return p, p

    def rz(i):
        zo = planes[i]
        return (
            remote(s3.at[i], zin.at[z], rz_s.at[i - 1], rz_r.at[z], along(zo)),
            remote(s3.at[i], zin.at[zo], rz_s.at[i - 1], rz_r.at[zo], along(zo)),
        )

    def r0(i):
        send(rc(i)[0])

    def r1(i):
        zo = planes[i]
        take(rc(i))
        for xo in range(2):
            for h in range(2):
                prod[zo, c, xo, h] = add(prod[zo, c, xo, h], cin[i, xo, h])
        send(rx1(i)[0])
        send(ry1(i)[0])

    def r2(i):
        zo = planes[i]
        take(rx1(i))
        for h in range(2):
            t0[i, h] = add(prod[zo, c, x, h, 0:32], xin[i, h])
        send(ry2(i)[0])
        take(ry1(i))
        for xo in range(2):
            t1[i, xo] = add(prod[zo, c, xo, y, 32:64], yin[i, xo])
        send(rx2(i)[0])

    def r3(i):
        take(ry2(i))
        s3[i, 0:32] = add(t0[i, y], y2[i])
        take(rx2(i))
        s3[i, 32:64] = add(t1[i, x], x2[i])
        if i > 0:
            send(rz(i)[0])

    def enter_last():
        rows = fb[:, :, :, :, 0:HALF].astype(f32).reshape(16, 2 * FINAL, HALF)
        normalize(0, rows[:, :FINAL].reshape(16 * FINAL, HALF), rows[:, FINAL:].reshape(16 * FINAL, HALF))
        expand(16 * FINAL)

    def leave_last():
        gates = jnp.concatenate(
            [gates_of(co, xo, zo, PF, FINAL) for co in range(2) for xo in range(2) for zo in range(4)], axis=0
        )

        def store(lo, result):
            h, at_col = lo // HALF, lo % HALF
            for s in range(4):
                pf[s // 2, h, s % 2, :, at_col : at_col + 512] = result[s * 32 : (s + 1) * 32]

        contract(16 * FINAL, gates, store)

    def fr(k):
        src, dst, target = [
            (pf.at[1 - c], fcin, to_c),
            (pf.at[c, :, 1 - x], fxin, to_x),
            (f2.at[1 - y], fyin, to_y),
        ][k]
        p = remote(src, dst, fr_s.at[k], fr_r.at[k], target)
        return p, p

    def frz(i):
        zo = planes[i]
        return (
            remote(f3.at[zo], fzin.at[z], fr_s.at[2 + i], fr_r.at[3 + z], along(zo)),
            remote(f3.at[zo], fzin.at[zo], fr_s.at[2 + i], fr_r.at[3 + zo], along(zo)),
        )

    def lz(i):
        zo = planes[i]
        a, b = fg.at[y, c, x, z], fg.at[y, c, x, zo]
        return remote(a, a, lz_s.at[i], lz_r.at[z], along(zo)), remote(b, b, lz_s.at[i], lz_r.at[zo], along(zo))

    def lx():
        return same(fg.at[y, c, x], fg.at[y, c, 1 - x], lz_s.at[4], lz_r.at[4], to_x)

    def ly():
        return same(fg.at[y, c], fg.at[1 - y, c], lz_s.at[5], lz_r.at[5], to_y)

    def lc():
        return same(fg.at[:, c], fg.at[:, 1 - c], lz_s.at[6], lz_r.at[6], to_c)

    def f_core():
        take(fr(0))
        for h in range(2):
            for xo in range(2):
                pf[c, h, xo] = add(pf[c, h, xo], fcin[h, xo])
        send(fr(1)[0])

    def f_x():
        take(fr(1))
        for h in range(2):
            f2[h] = add(pf[c, h, x], fxin[h])
        send(fr(2)[0])

    def f_y():
        take(fr(2))
        f3[...] = (f2[y].astype(f32) + fyin[...].astype(f32)).reshape(4, FINAL, HALF)
        for i in range(1, 4):
            send(frz(i)[0])

    def f_z():
        rows = fb[c, x, z, :, 0:HALF].astype(f32)
        rf[...] = rows.reshape(2, FINAL, HALF)
        total = f3[z]
        for i in range(1, 4):
            take(frz(i))
            total = total + fzin[planes[i]]
        rows = rf[y] + total
        out[PF : out.shape[0], :] = rows[: out.shape[0] - PF].astype(bf16)
        fg[y, c, x, z] = jnp.concatenate([rows[:, :512], rows[:, 512:]], axis=0).astype(bf16)
        for i in range(1, 4):
            send(lz(i)[0])

    def l_z():
        for i in range(1, 4):
            take(lz(i))
        send(lx()[0])

    def l_x():
        take(lx())
        send(ly()[0])

    def l_y():
        take(ly())
        send(lc()[0])

    def head_rows():
        take(lc())
        rows = fg[...].astype(f32).reshape(2, 16, 2 * FINAL, 512)
        blocks = [rows[yo, :, q * FINAL : (q + 1) * FINAL].reshape(16 * FINAL, 512) for yo in range(2) for q in range(2)]
        total = sum(jnp.sum(b * b, axis=1, keepdims=True) for b in blocks)
        scale = lax.rsqrt(total * (1.0 / width) + epsilon)
        spots = lax.broadcasted_iota(jnp.int32, (slots.shape[0], 16 * FINAL), 1)
        chosen = jnp.where(slots[...] == spots, 1.0, 0.0).astype(bf16)
        for k, b in enumerate(blocks):
            lo = k * 512
            normed = (b * scale * last_gain[:, lo : lo + 512]).astype(bf16)
            fn[:, lo : lo + 512] = jnp.dot(chosen, normed, preferred_element_type=f32).astype(bf16)

    def head_columns():
        loads[3].wait()
        lo = 0
        while lo < hw.shape[0]:
            n = min(256, hw.shape[0] - lo)
            logits[:, lo : lo + n] = nt(fn[...], hw[lo : lo + n, :])
            lo += n

    for i in range(1, 4):
        take(fz(i))
    send(fx()[0])
    spread(1)
    take(fx())
    send(fc()[0])
    take(own(0))
    take(own(1))
    send(gc(0)[0])
    spread(2)
    corner(1)
    spread(3)
    take(fc())
    loads[0].wait()
    loads[1].wait()
    enter_last()
    corner(2)
    loads[2].wait()
    leave_last()
    send(fr(0)[0])
    take(gc(0))
    close(1)
    enter(0)
    f_core()
    corner(3)
    leave(0)
    r0(0)
    close(2)
    take(gc(1))
    enter(1)
    r1(0)
    f_x()
    close(3)
    leave(1)
    r0(1)
    r2(0)
    f_y()
    take(gc(2))
    enter(2)
    r1(1)
    r3(0)
    f_z()
    leave(2)
    r0(2)
    r2(1)
    l_z()
    take(gc(3))
    enter(3)
    r1(2)
    l_x()
    r3(1)
    leave(3)
    r0(3)
    r2(2)
    l_y()
    r1(3)
    r3(2)
    head_rows()
    r2(3)
    head_columns()
    r3(3)
    total = slab[z, c, x, y].astype(f32) + s3[0].astype(f32)
    for i in range(1, 4):
        take(rz(i))
        total = total + zin[planes[i]].astype(f32)
    out[0:PF, :] = total.astype(bf16)
    for copy in sent:
        copy.wait_send()


def moe(part, tokens, gain, last_gain, code, slots, w_gate, w_up, w_down, head_weight, row_count):
    width = tokens.shape[1]
    units, vocab = w_gate.shape[0], head_weight.shape[0]
    dma = pltpu.SemaphoreType.DMA
    buf = lambda *shape: pltpu.VMEM(shape, jnp.bfloat16)
    wide = lambda *shape: pltpu.VMEM(shape, jnp.float32)
    vmem = pl.BlockSpec(memory_space=pltpu.VMEM)
    hbm = pl.BlockSpec(memory_space=pltpu.HBM)
    return pl.pallas_call(
        moe_kernel,
        name="moe",
        out_shape=(
            jax.ShapeDtypeStruct((row_count, HALF), jnp.bfloat16),
            jax.ShapeDtypeStruct((slots.shape[0], vocab), jnp.float32),
        ),
        in_specs=[vmem] * 6 + [hbm] * 4,
        out_specs=(vmem,) * 2,
        scratch_shapes=[
            buf(units, width),
            buf(units, width),
            buf(units, width),
            buf(vocab, width),
            buf(SLAB, width),
            buf(4, 2, 2, 2, PF, HALF),
            buf(4, 2, 2, 2, PF, HALF),
            buf(4, 2, 2, PF, HALF),
            buf(4, 2, 32, HALF),
            buf(4, 2, 32, HALF),
            buf(4, 2, 32, HALF),
            buf(4, 2, 32, HALF),
            buf(4, 32, HALF),
            buf(4, 32, HALF),
            buf(4, PF, HALF),
            buf(4, PF, HALF),
            buf(4 * PF, width),
            buf(4 * PF, units),
            buf(2, 2, 4, 2 * FINAL, HALF + CODE),
            buf(2, 2, 2, 32, HALF),
            buf(2, 2, 32, HALF),
            buf(2, 32, HALF),
            buf(2, 32, HALF),
            buf(32, HALF),
            wide(4, FINAL, HALF),
            wide(4, FINAL, HALF),
            buf(2, 2, 2, 4, 2 * FINAL, 512),
            wide(2, FINAL, HALF),
            buf(slots.shape[0], width),
            dma((4,)),
            dma((3,)),
            dma((3,)),
            dma((3,)),
            dma((4,)),
            dma((3,)),
            dma((4,)),
            dma((5, 4)),
            dma((5, 4)),
            dma((2,)),
            dma((2,)),
            dma((2,)),
            dma((2,)),
            dma((5, 4)),
            dma((5, 4)),
            dma((3,)),
            dma((4,)),
            dma((7,)),
            dma((7,)),
            dma((7,)),
            dma((7,)),
        ],
        compiler_params=pltpu.CompilerParams(
            collective_id=0, has_side_effects=True, vmem_limit_bytes=58 * 1024 * 1024
        ),
    )(part, tokens, gain, last_gain, code, slots, w_gate, w_up, w_down, head_weight)


def attention_kernel(heads, pf, rows_of, tok_ref, gain_ref, cos_ref, sin_ref, len_ref, lgain_ref, wq_hbm, wl_hbm, cache_hbm, ku_hbm, vu_hbm, wo_hbm, out_ref, wq, wl, cache, ku, vu, wo, sems):
    pairs = [(wq_hbm, wq), (wl_hbm, wl), (cache_hbm, cache), (ku_hbm, ku), (vu_hbm, vu), (wo_hbm, wo)]
    loads = [pltpu.make_async_copy(a, b, sems.at[i]) for i, (a, b) in enumerate(pairs)]
    for load in loads:
        load.start()
    rows = tok_ref.shape[0]
    f32, bf16 = jnp.float32, jnp.bfloat16
    dot = functools.partial(jnp.dot, preferred_element_type=f32)
    nt = lambda a, b: lax.dot_general(a, b, (((1,), (1,)), ((), ())), preferred_element_type=f32)
    normed = rms_norm(tok_ref[...].astype(f32), gain_ref[...]).astype(bf16)
    cosines, sines = cos_ref[...], sin_ref[...]

    def turn(v):
        half = ROPE // 2
        return v * cosines + jnp.concatenate([v[:, half:], v[:, :half]], axis=1) * sines

    loads[0].wait()
    queries = dot(normed, wq[...])
    loads[1].wait()
    latent = nt(normed, wl[...])
    key_lat = rms_norm(latent[:, :LAT], lgain_ref[...]).astype(bf16)
    key_rope = turn(latent[:, LAT:]).astype(bf16)
    loads[2].wait()
    entries, cache_len = cache.shape[0], cache.shape[2]
    old_lat = [cache[e, :LAT, :] for e in range(entries)]
    old_rope = [cache[e, LAT:, :] for e in range(entries)]
    row = lax.broadcasted_iota(jnp.int32, (rows, 1), 0)
    entry = jnp.where(row < pf, 0, jnp.where(row < rows_of, row - pf + 1, entries))
    start = entry * cache_len
    key = lax.broadcasted_iota(jnp.int32, (rows, entries * cache_len), 1)
    old_seen = (key >= start) & (key < start + len_ref[...])
    col = lax.broadcasted_iota(jnp.int32, (rows, rows), 1)
    new_seen = (col == row) | ((row < pf) & (col <= row))
    factor = 1.0 / jnp.sqrt(jnp.float32(NOPE + ROPE))
    loads[3].wait()
    outs = []
    for h in range(heads):
        base = h * (NOPE + ROPE)
        q_nope = queries[:, base : base + NOPE].astype(bf16)
        q_rope = turn(queries[:, base + NOPE : base + NOPE + ROPE]).astype(bf16)
        absorbed = nt(q_nope, ku[:, h * NOPE : (h + 1) * NOPE]).astype(bf16)
        old = [dot(absorbed, old_lat[e]) + dot(q_rope, old_rope[e]) for e in range(entries)]
        old = jnp.concatenate(old, axis=1) * factor
        new = (nt(absorbed, key_lat) + nt(q_rope, key_rope)) * factor
        old = jnp.exp(jnp.where(old_seen, old, -jnp.inf))
        new = jnp.exp(jnp.where(new_seen, new, -jnp.inf))
        total = jnp.sum(old, axis=1, keepdims=True) + jnp.sum(new, axis=1, keepdims=True)
        old = (old / total).astype(bf16)
        new = (new / total).astype(bf16)
        context = dot(new, key_lat)
        for e in range(entries):
            context = context + nt(old[:, e * cache_len : (e + 1) * cache_len], old_lat[e])
        context = context.astype(bf16)
        if h == 0:
            loads[4].wait()
        value = dot(context, vu[:, h * VD : (h + 1) * VD])
        outs.append(jnp.where(row == rows_of, value[pf - 1 : pf], value).astype(bf16))
    loads[5].wait()
    out_ref[...] = dot(jnp.concatenate(outs, axis=1), wo[...]).astype(bf16)


def attention(tokens, pf, nd, prefill_len, decode_len, cached, attn_gain, w_query, w_latent, latent_gain, key_up, value_up, w_out):
    rows, width = tokens.shape
    spare = rows - pf - nd
    steps = jnp.arange(pf, dtype=jnp.int32)
    none = jnp.zeros((spare,), jnp.int32)
    positions = jnp.concatenate([prefill_len[0] + steps, decode_len, none])
    lengths = jnp.concatenate([prefill_len[0] + 0 * steps, decode_len, none])[:, None]
    half = ROPE // 2
    frequency = rope_base ** (-jnp.arange(half, dtype=jnp.float32) * 2.0 / ROPE)
    angles = positions.astype(jnp.float32)[:, None] * frequency
    cosines, sines = jnp.cos(angles), jnp.sin(angles)
    vmem = pl.BlockSpec(memory_space=pltpu.VMEM)
    hbm = pl.BlockSpec(memory_space=pltpu.HBM)
    large = (w_query, w_latent.T, jnp.swapaxes(cached, 1, 2), key_up, value_up, w_out)
    return pl.pallas_call(
        functools.partial(attention_kernel, w_query.shape[1] // (NOPE + ROPE), pf, pf + nd),
        name="attention",
        out_shape=jax.ShapeDtypeStruct((rows, width), jnp.bfloat16),
        in_specs=[vmem] * 6 + [hbm] * 6,
        out_specs=vmem,
        scratch_shapes=[pltpu.VMEM(a.shape, a.dtype) for a in large] + [pltpu.SemaphoreType.DMA((6,))],
        compiler_params=pltpu.CompilerParams(vmem_limit_bytes=60 * 1024 * 1024),
    )(
        tokens,
        attn_gain.reshape(1, width),
        jnp.concatenate([cosines, cosines], axis=1),
        jnp.concatenate([-sines, sines], axis=1),
        lengths,
        latent_gain.reshape(1, LAT),
        *large,
    )


def gate_code(expert_ids, expert_weights, owners):
    named = expert_ids[:, :, None] == jnp.arange(owners, dtype=jnp.int32)
    dense = jnp.sum(jnp.where(named, expert_weights[:, :, None], 0.0), axis=1)
    dense = jnp.concatenate([dense, dense[PF - 1 : PF]], axis=0).T
    flat = jnp.pad(dense, ((0, 0), (0, 128 - dense.shape[1])))
    high = lax.reduce_precision(flat, 8, 7)
    return jnp.concatenate([high, flat - high], axis=1).astype(jnp.bfloat16)


def head_slots(request_order, owners, decode_count):
    def spot(owner, row):
        return ((owner % 2 * 2 + owner // 2 % 2) * 4 + owner // 4) * FINAL + row

    every = jnp.arange(owners, dtype=jnp.int32)
    return jnp.concatenate(
        [spot(every, decode_count), spot(request_order // decode_count, request_order % decode_count)]
    )[:, None]


def on_block(
    prefill_tokens,
    decode_tokens,
    request_order,
    prefill_lengths,
    decode_lengths,
    latent_cache,
    attn_gain,
    w_query,
    w_latent,
    latent_gain,
    key_up,
    value_up,
    w_out,
    ffn_gain,
    expert_ids,
    expert_weights,
    w_gate,
    w_up,
    w_down,
    final_gain,
    head_weight,
):
    owners = lax.axis_size("ep")
    prefill_count, decode_count = prefill_tokens.shape[0], decode_tokens.shape[0]
    row_count, width = prefill_count + decode_count, prefill_tokens.shape[1]
    tokens = jnp.concatenate([prefill_tokens, decode_tokens, prefill_tokens[prefill_count - 1 :]], axis=0)
    tokens = jnp.pad(tokens, ((0, SLAB - row_count - 1), (0, 0)))
    partial_attn = attention(
        tokens,
        prefill_count,
        decode_count,
        prefill_lengths,
        decode_lengths,
        latent_cache,
        attn_gain,
        w_query,
        w_latent,
        latent_gain,
        key_up,
        value_up,
        w_out,
    )
    return moe(
        partial_attn,
        tokens,
        ffn_gain.reshape(1, width),
        final_gain.reshape(1, width),
        gate_code(expert_ids, expert_weights, owners),
        head_slots(request_order, owners, decode_count),
        w_gate[0].T,
        w_up[0].T,
        w_down[0],
        head_weight.T,
        row_count,
    )


def on_device(
    prefill_tokens,
    decode_tokens,
    request_order,
    prefill_lengths,
    decode_lengths,
    latent_cache,
    attn_gain,
    w_query,
    w_latent,
    latent_gain,
    key_up,
    value_up,
    w_out,
    ffn_gain,
    expert_ids,
    expert_weights,
    w_gate,
    w_up,
    w_down,
    final_gain,
    head_weight,
):
    owners = lax.axis_size("ep")
    shards = lax.axis_size("vp")
    partial_attn = attend(
        prefill_tokens,
        decode_tokens,
        latent_cache,
        prefill_lengths,
        decode_lengths,
        attn_gain,
        w_query,
        w_latent,
        latent_gain,
        key_up,
        value_up,
        w_out,
    )
    attn = lax.psum(partial_attn, "vp")
    tokens = jnp.concatenate([prefill_tokens, decode_tokens], axis=0)
    resid = (tokens.astype(jnp.float32) + attn).astype(jnp.bfloat16)
    ffn_in = rms_norm(resid.astype(jnp.float32), ffn_gain).astype(jnp.bfloat16)
    row_count = tokens.shape[0]
    model_width = tokens.shape[1]
    share_width = model_width // shards
    capacity = max(2, min(row_count, row_count * TOPK * 2 // owners))
    flat_ids = expert_ids.reshape(-1)
    onehot = (flat_ids[:, None] == jnp.arange(owners, dtype=jnp.int32)[None, :]).astype(jnp.float32)
    entry = jnp.arange(flat_ids.shape[0], dtype=jnp.int32)
    before = (entry[:, None] > entry[None, :]).astype(jnp.bfloat16)
    earlier = jnp.dot(before, onehot.astype(jnp.bfloat16), preferred_element_type=jnp.float32)
    slot_index = jnp.sum(earlier * onehot, axis=1).astype(jnp.int32)
    target = flat_ids * capacity + slot_index
    source_rows = jnp.arange(row_count * TOPK, dtype=jnp.int32) // TOPK
    outgoing = (
        jnp.zeros((owners * capacity, model_width), jnp.bfloat16)
        .at[target]
        .set(ffn_in[source_rows])
    )
    outgoing = outgoing.reshape(owners, capacity, model_width)
    arrived = lax.all_to_all(outgoing, "ep", split_axis=0, concat_axis=0, tiled=True)
    item_count = arrived.shape[1]
    flattened = arrived.reshape(owners * item_count, model_width)
    gated = jnp.dot(flattened, w_gate[0], preferred_element_type=jnp.float32)
    upward = jnp.dot(flattened, w_up[0], preferred_element_type=jnp.float32)
    hidden_act = (jax.nn.silu(gated) * upward).astype(jnp.bfloat16)
    result = jnp.dot(hidden_act, w_down[0], preferred_element_type=jnp.float32).reshape(
        owners, item_count, model_width
    )
    summed = lax.psum_scatter(result, "vp", scatter_dimension=2, tiled=True)
    sent_back = lax.all_to_all(summed, "ep", split_axis=0, concat_axis=0, tiled=True)
    picked = sent_back.reshape(owners * capacity, sent_back.shape[2])[target]
    picked = picked.reshape(row_count, TOPK, sent_back.shape[2])
    routed_sum = jnp.sum(expert_weights[:, :, None] * picked, axis=1)
    column = lax.axis_index("vp") * share_width
    resid_share = lax.dynamic_slice_in_dim(resid, column, share_width, 1)
    layer_out = (resid_share.astype(jnp.float32) + routed_sum).astype(jnp.bfloat16)
    prefill_count = prefill_tokens.shape[0]
    decode_count = decode_tokens.shape[0]
    own_rows = layer_out[prefill_count - 1 :]
    everyone = lax.all_gather(own_rows, ("ep", "vp"), axis=0, tiled=True)
    everyone = everyone.reshape(owners, shards, 1 + decode_count, share_width)
    everyone = jnp.transpose(everyone, (0, 2, 1, 3)).reshape(owners, 1 + decode_count, model_width)
    prefill_last = everyone[:, 0]
    decode_rows = everyone[:, 1:].reshape(owners * decode_count, model_width)[request_order]
    final_rows = jnp.concatenate([prefill_last, decode_rows], axis=0)
    final_normed = rms_norm(final_rows.astype(jnp.float32), final_gain).astype(jnp.bfloat16)
    logits = jnp.dot(final_normed, head_weight, preferred_element_type=jnp.float32)
    return (layer_out, logits)


def solution(mesh):
    block = mesh.shape["vp"] == 2 and mesh.shape["ep"] == 16
    return jax.shard_map(
        on_block if block else on_device,
        mesh=mesh,
        in_specs=(
            P("ep", None),
            P("ep", None),
            P(),
            P("ep"),
            P("ep"),
            P("ep", None, None),
            P(),
            P(None, "vp"),
            P(),
            P(),
            P(None, "vp"),
            P(None, "vp"),
            P("vp", None),
            P(),
            P("ep", None),
            P("ep", None),
            P("ep", None, "vp"),
            P("ep", None, "vp"),
            P("ep", "vp", None),
            P(),
            P(None, ("ep", "vp")),
        ),
        out_specs=(P("ep", "vp"), P(None, ("ep", "vp"))),
        check_vma=False,
    )
```

```python
import functools
import math

import jax
import jax.numpy as jnp
from jax import lax
from jax.experimental import pallas as pl
from jax.experimental.pallas import tpu as pltpu
from jax.sharding import PartitionSpec as P

NOPE = 128
ROPE = 64
VD = 128
LAT = 512
TOPK = 6


epsilon = 1e-06
rope_base = 10000.0


def rms_norm(values, gain):
    return values * lax.rsqrt(jnp.mean(values * values, axis=-1, keepdims=True) + epsilon) * gain


def rotate(values, positions):
    half_width = values.shape[-1] // 2
    frequency = rope_base ** (-jnp.arange(half_width, dtype=jnp.float32) * 2.0 / values.shape[-1])
    angles = positions.astype(jnp.float32)[..., None] * frequency
    cosines = jnp.cos(angles)
    sines = jnp.sin(angles)
    lower_half = values[..., :half_width]
    upper_half = values[..., half_width:]
    return jnp.concatenate(
        [lower_half * cosines - upper_half * sines, lower_half * sines + upper_half * cosines],
        axis=-1,
    )


def attend(
    prefill_rows,
    decode_rows,
    cached,
    prefill_len,
    decode_len,
    attn_gain,
    w_query,
    w_latent,
    latent_gain,
    key_up,
    value_up,
    w_out,
):
    tokens = jnp.concatenate([prefill_rows, decode_rows], axis=0)
    prefill_count = prefill_rows.shape[0]
    row_count = tokens.shape[0]
    head_count = w_query.shape[1] // (NOPE + ROPE)
    positions = jnp.concatenate(
        [prefill_len[0] + jnp.arange(prefill_count, dtype=jnp.int32), decode_len]
    )
    normed = rms_norm(tokens.astype(jnp.float32), attn_gain).astype(jnp.bfloat16)
    queries = jnp.dot(normed, w_query, preferred_element_type=jnp.float32).reshape(
        row_count, head_count, NOPE + ROPE
    )
    query_nope = queries[..., :NOPE].astype(jnp.bfloat16)
    query_rope = rotate(queries[..., NOPE:], positions[:, None]).astype(jnp.bfloat16)
    latent = jnp.dot(normed, w_latent, preferred_element_type=jnp.float32)
    latent_normed = rms_norm(latent[:, :LAT], latent_gain)
    new_keys = jnp.concatenate([latent_normed, rotate(latent[:, LAT:], positions)], axis=1).astype(
        jnp.bfloat16
    )
    key_heads = key_up.reshape(LAT, head_count, NOPE)
    absorbed = jnp.einsum(
        "rhn,lhn->rhl", query_nope, key_heads, preferred_element_type=jnp.float32
    ).astype(jnp.bfloat16)
    query_all = jnp.concatenate([absorbed, query_rope], axis=-1)
    factor = 1.0 / jnp.sqrt(jnp.float32(NOPE + ROPE))
    cache_len = cached.shape[1]
    prefill_keys = jnp.concatenate([cached[0], new_keys[:prefill_count]], axis=0)
    scores = (
        jnp.einsum(
            "chk,jk->chj",
            query_all[:prefill_count],
            prefill_keys,
            preferred_element_type=jnp.float32,
        )
        * factor
    )
    key_index = jnp.arange(cache_len + prefill_count, dtype=jnp.int32)
    row_index = jnp.arange(prefill_count, dtype=jnp.int32)
    visible = jnp.where(
        key_index[None, :] < cache_len,
        key_index[None, :] < prefill_len[0],
        key_index[None, :] - cache_len <= row_index[:, None],
    )
    expo = jnp.exp(jnp.where(visible[:, None, :], scores, -jnp.inf))
    attn_probs = (expo / jnp.sum(expo, axis=-1, keepdims=True)).astype(jnp.bfloat16)
    prefill_context = jnp.einsum(
        "chj,jl->chl", attn_probs, prefill_keys[:, :LAT], preferred_element_type=jnp.float32
    ).astype(jnp.bfloat16)
    decode_query = query_all[prefill_count:]
    decode_cache = cached[1:]
    own_keys = new_keys[prefill_count:]
    cache_scores = (
        jnp.einsum("dhk,dsk->dhs", decode_query, decode_cache, preferred_element_type=jnp.float32)
        * factor
    )
    self_scores = (
        jnp.einsum("dhk,dk->dh", decode_query, own_keys, preferred_element_type=jnp.float32)
        * factor
    )
    cache_visible = jnp.arange(cache_len, dtype=jnp.int32)[None, :] < decode_len[:, None]
    cache_expo = jnp.exp(jnp.where(cache_visible[:, None, :], cache_scores, -jnp.inf))
    self_expo = jnp.exp(self_scores)
    totals = jnp.sum(cache_expo, axis=-1) + self_expo
    cache_probs = (cache_expo / totals[..., None]).astype(jnp.bfloat16)
    self_probs = (self_expo / totals).astype(jnp.bfloat16)
    decode_context = jnp.einsum(
        "dhs,dsl->dhl", cache_probs, decode_cache[..., :LAT], preferred_element_type=jnp.float32
    )
    decode_context = (
        decode_context
        + self_probs.astype(jnp.float32)[..., None] * own_keys[:, None, :LAT].astype(jnp.float32)
    ).astype(jnp.bfloat16)
    context = jnp.concatenate([prefill_context, decode_context], axis=0)
    value_heads = value_up.reshape(LAT, head_count, VD)
    head_out = jnp.einsum(
        "rhl,lhv->rhv", context, value_heads, preferred_element_type=jnp.float32
    ).astype(jnp.bfloat16)
    return jnp.dot(
        head_out.reshape(row_count, head_count * VD), w_out, preferred_element_type=jnp.float32
    )


MESH = pl.DeviceIdType.MESH
SLAB = 80
PF = 64
FINAL = 8
HALF = 1024
CODE = 256


def place():
    e = lax.axis_index("ep")
    return e // 4, (e // 2) % 2, e % 2, lax.axis_index("vp")


def at(z, x, c, y):
    return {"ep": z * 4 + x * 2 + c, "vp": y}


def remote(src, dst, send, recv, target):
    return pltpu.make_async_remote_copy(
        src_ref=src, dst_ref=dst, send_sem=send, recv_sem=recv, device_id=target, device_id_type=MESH
    )


def layer_kernel(heads, prefill, decode, again, gain, last_gain, lgain, ids, mix, order, plen, dlen, wq_hbm, wl_hbm, cache_hbm, ku_hbm, vu_hbm, wo_hbm, wg_hbm, wu_hbm, wd_hbm, hw_hbm, out, logits, *scratch):
    (wg, wu, wd, hw, got, slab, prod, cin, xin, yin, t0, t1, y2, x2, s3, zin) = scratch[:16]
    (xn, hid, fb, cb, pf, fcin, fxin, f2, fyin, f3, fzin, fg, rf, fn) = scratch[16:30]
    (w_sem, sw_s, sw_r, gz_s, gz_r, g_s, g_r) = scratch[30:37]
    (r_s, r_r, rz_s, rz_r, fr_s, fr_r, tree_s, tree_r) = scratch[37:45]
    (wq, wl, cache, ku, vu, wo, tok, tail, part, dense) = scratch[45:]
    f32, bf16 = jnp.float32, jnp.bfloat16
    nt = lambda a, b: lax.dot_general(a, b, (((1,), (1,)), ((), ())), preferred_element_type=f32)
    z, x, c, y = place()
    mine = z * 4 + x * 2 + c
    near = z + 1 - 2 * (z % 2)
    planes = [z, near, 3 - 3 * (z // 2), 2 - z // 2]
    to_x, to_y, to_c = at(z, 1 - x, c, y), at(z, x, c, 1 - y), at(z, x, 1 - c, y)

    def along(zo):
        return at(zo, x, c, y)

    pairs = [(wg_hbm, wg), (wu_hbm, wu), (wd_hbm, wd), (hw_hbm, hw)]
    pairs += [(wq_hbm, wq), (wl_hbm, wl), (cache_hbm, cache), (ku_hbm, ku), (vu_hbm, vu), (wo_hbm, wo)]
    loads = [pltpu.make_async_copy(a, b, w_sem.at[i]) for i, (a, b) in enumerate(pairs)]
    for load in loads[4:] + loads[:4]:
        load.start()
    barrier = pltpu.get_barrier_semaphore()
    for target in [to_x, to_y, to_c] + [along(zo) for zo in planes[1:]]:
        pl.semaphore_signal(barrier, inc=1, device_id=target, device_id_type=MESH)
    sent = []

    def send(copy):
        copy.start()
        sent.append(copy)

    def cols(h):
        return pl.ds(pl.multiple_of(h * HALF, HALF), HALF)

    def swap(i):
        rows = pl.ds(PF, SLAB - PF) if i == 0 else pl.ds(0, PF)
        p = remote(part.at[rows, cols(1 - y)], got.at[rows, :], sw_s.at[i], sw_r.at[i], to_y)
        return p, p

    def same(ref_out, ref_in, s, r, target):
        return remote(ref_out, ref_out, s, r, target), remote(ref_in, ref_in, s, r, target)

    def gz(i):
        zo = planes[i]
        a, b = slab.at[z, c, x, y], slab.at[zo, c, x, y]
        return remote(a, a, gz_s.at[i - 1], gz_r.at[z], along(zo)), remote(b, b, gz_s.at[i - 1], gz_r.at[zo], along(zo))

    def gx(i):
        zo = planes[i]
        return same(slab.at[zo, c, x, y], slab.at[zo, c, 1 - x, y], g_s.at[0, i], g_r.at[0, i], to_x)

    def gy(i):
        zo = planes[i]
        return same(slab.at[zo, c, x, y], slab.at[zo, c, x, 1 - y], g_s.at[1, i], g_r.at[1, i], to_y)

    def dx(i):
        zo = planes[i]
        return same(
            slab.at[zo, c, x, 1 - y, 32:64], slab.at[zo, c, 1 - x, 1 - y, 32:64], g_s.at[2, i], g_r.at[2, i], to_x
        )

    def dy(i):
        zo = planes[i]
        return same(
            slab.at[zo, c, 1 - x, y, 0:32], slab.at[zo, c, 1 - x, 1 - y, 0:32], g_s.at[3, i], g_r.at[3, i], to_y
        )

    def gc(i):
        zo = planes[i]
        return same(slab.at[zo, c], slab.at[zo, 1 - c], g_s.at[4, i], g_r.at[4, i], to_c)

    def tree(k, block):
        def hop_z(i):
            zo = planes[i]
            return (
                remote(block(c, x, z), block(c, x, z), tree_s.at[k, i], tree_r.at[k, z], along(zo)),
                remote(block(c, x, zo), block(c, x, zo), tree_s.at[k, i], tree_r.at[k, zo], along(zo)),
            )

        return hop_z

    def hop(k, j, leaves, lands, target):
        return same(leaves, lands, tree_s.at[k, 4 + j], tree_r.at[k, 4 + j], target)

    code_z = tree(0, lambda co, xo, zo: cb.at[co, xo, zo])
    code_x = lambda: hop(0, 0, cb.at[c, x], cb.at[c, 1 - x], to_x)
    code_c = lambda: hop(0, 2, cb.at[c], cb.at[1 - c], to_c)
    first_z = tree(1, lambda co, xo, zo: fb.at[y, co, xo, zo])
    first_x = lambda: hop(1, 0, fb.at[y, c, x], fb.at[y, c, 1 - x], to_x)
    first_y = lambda: hop(1, 1, fb.at[y, c], fb.at[1 - y, c], to_y)
    first_c = lambda: hop(1, 2, fb.at[:, c], fb.at[:, 1 - c], to_c)
    lz = tree(2, lambda co, xo, zo: fg.at[y, co, xo, zo])
    lx = lambda: hop(2, 0, fg.at[y, c, x], fg.at[y, c, 1 - x], to_x)
    ly = lambda: hop(2, 1, fg.at[y, c], fg.at[1 - y, c], to_y)
    lc = lambda: hop(2, 2, fg.at[:, c], fg.at[:, 1 - c], to_c)

    tail[...] = jnp.zeros_like(tail)
    tail[0 : decode.shape[0], :] = decode[...].astype(f32)
    tail[decode.shape[0] : decode.shape[0] + 1, :] = prefill[PF - 16 : PF, :].astype(f32)[15:16]
    tok[0:PF, :] = prefill[...]
    tok[PF:SLAB, :] = tail[...].astype(bf16)
    dense[...] = jnp.zeros_like(dense)
    expert = lax.broadcasted_iota(jnp.int32, (16, ids.shape[1]), 0)
    named = jnp.zeros((16, ids.shape[1]), f32)
    for k in range(TOPK):
        named = named + jnp.where(ids[k : k + 1, :] == expert, mix[k : k + 1, :], 0.0)
    dense[:, 0 : ids.shape[1]] = named
    high = dense[...].astype(bf16)
    cb[c, x, z, :, 0:128] = high
    cb[c, x, z, :, 128:256] = (dense[...] - high.astype(f32)).astype(bf16)
    row = lax.broadcasted_iota(jnp.int32, (SLAB, 1), 0)
    length = jnp.where(row < PF, plen[0], 0)
    for j in range(decode.shape[0]):
        length = jnp.where(row == PF + j, dlen[j], length)
    position = jnp.where(row < PF, length + row, length).astype(f32)
    lane = lax.broadcasted_iota(jnp.int32, (1, ROPE), 1)
    upper = lane >= ROPE // 2
    power = jnp.where(upper, lane - ROPE // 2, lane).astype(f32)
    angles = position * jnp.exp(power * (-2.0 / ROPE * math.log(rope_base)))
    cosines = jnp.cos(angles)
    sines = jnp.where(upper, 1.0, -1.0) * jnp.sin(angles)
    pl.semaphore_wait(barrier, 6)
    for i in range(1, 4):
        send(code_z(i)[0])

    def turn(v):
        half = ROPE // 2
        return v * cosines + jnp.concatenate([v[:, half:], v[:, :half]], axis=1) * sines

    dot = functools.partial(jnp.dot, preferred_element_type=f32)
    normed = rms_norm(tok[...].astype(f32), again[...]).astype(bf16)
    loads[4].wait()
    queries = dot(normed, wq[...])
    loads[5].wait()
    latent = nt(normed, wl[...])
    key_lat = rms_norm(latent[:, :LAT], lgain[...]).astype(bf16)
    key_rope = turn(latent[:, LAT:]).astype(bf16)
    loads[6].wait()
    entries, cache_len = cache.shape[0], cache.shape[2]
    old_lat = [cache[e, :LAT, :] for e in range(entries)]
    old_rope = [cache[e, LAT:, :] for e in range(entries)]
    rows_of = PF + decode.shape[0]
    entry = jnp.where(row < PF, 0, jnp.where(row < rows_of, row - PF + 1, entries))
    start = entry * cache_len
    key = lax.broadcasted_iota(jnp.int32, (SLAB, entries * cache_len), 1)
    old_seen = (key >= start) & (key < start + length)
    col = lax.broadcasted_iota(jnp.int32, (SLAB, SLAB), 1)
    new_seen = (col == row) | ((row < PF) & (col <= row))
    factor = 1.0 / jnp.sqrt(jnp.float32(NOPE + ROPE))
    loads[7].wait()
    values = []
    for h in range(heads):
        base = h * (NOPE + ROPE)
        q_nope = queries[:, base : base + NOPE].astype(bf16)
        q_rope = turn(queries[:, base + NOPE : base + NOPE + ROPE]).astype(bf16)
        absorbed = nt(q_nope, ku[:, h * NOPE : (h + 1) * NOPE]).astype(bf16)
        old = [dot(absorbed, old_lat[e]) + dot(q_rope, old_rope[e]) for e in range(entries)]
        old = jnp.concatenate(old, axis=1) * factor
        new = (nt(absorbed, key_lat) + nt(q_rope, key_rope)) * factor
        old = jnp.exp(jnp.where(old_seen, old, -jnp.inf))
        new = jnp.exp(jnp.where(new_seen, new, -jnp.inf))
        total = jnp.sum(old, axis=1, keepdims=True) + jnp.sum(new, axis=1, keepdims=True)
        old = (old / total).astype(bf16)
        new = (new / total).astype(bf16)
        context = dot(new, key_lat)
        for e in range(entries):
            context = context + nt(old[:, e * cache_len : (e + 1) * cache_len], old_lat[e])
        context = context.astype(bf16)
        if h == 0:
            loads[8].wait()
        value = dot(context, vu[:, h * VD : (h + 1) * VD])
        values.append(jnp.where(row == rows_of, value[PF - 1 : PF], value).astype(bf16))
    values = jnp.concatenate(values, axis=1)
    loads[9].wait()
    part[:, cols(1 - y)] = dot(values, wo[:, cols(1 - y)]).astype(bf16)
    send(swap(0)[0])
    send(swap(1)[0])
    part[:, cols(y)] = dot(values, wo[:, cols(y)]).astype(bf16)

    def fold(rows):
        return jnp.concatenate([rows[:, : HALF // 2], rows[:, HALF // 2 :]], axis=0).astype(bf16)

    swap(0)[1].wait_recv()
    rows = part[PF:SLAB, cols(y)].astype(f32) + got[PF:SLAB, :].astype(f32)
    rows = tok[PF:SLAB, cols(y)].astype(f32) + rows
    rf[...] = rows[:FINAL].astype(bf16).astype(f32)
    fb[y, c, x, z] = fold(rows[:FINAL])
    for i in range(1, 4):
        send(first_z(i)[0])
    swap(1)[1].wait_recv()
    rows = part[0:PF, cols(y)].astype(f32) + got[0:PF, :].astype(f32)
    slab[z, c, x, y] = (tok[0:PF, cols(y)].astype(f32) + rows).astype(bf16)

    def take(pair):
        pair[1].wait_recv()

    def spread(i):
        if i > 0:
            take(gz(i))
        send(gx(i)[0])
        send(gy(i)[0])

    def corner(i):
        take(gx(i))
        send(dy(i)[0])
        take(gy(i))
        send(dx(i)[0])

    def close(i):
        take(dx(i))
        take(dy(i))
        send(gc(i)[0])

    width = 2 * HALF

    def normalize(top, blocks):
        total = sum(jnp.sum(b * b, axis=1, keepdims=True) for b in blocks)
        scale = lax.rsqrt(total * (1.0 / width) + epsilon)
        count, wide = blocks[0].shape
        for k, b in enumerate(blocks):
            lo = k * wide
            xn[top : top + count, lo : lo + wide] = (b * scale * gain[:, lo : lo + wide]).astype(bf16)

    def unfold(ref):
        rows = ref[...].astype(f32).reshape(2, 16, 2 * FINAL, HALF // 2)
        return [
            rows[yo, :, q * FINAL : (q + 1) * FINAL].reshape(16 * FINAL, HALF // 2) for yo in range(2) for q in range(2)
        ]

    def gates_of(co, xo, zo, first, count):
        block = cb[co, xo, zo].astype(f32)
        expert = lax.broadcasted_iota(jnp.int32, block.shape, 0)
        row = jnp.sum(jnp.where(expert == mine, block, 0.0), axis=0, keepdims=True)
        row = row[:, 0:128] + row[:, 128:256]
        lane = lax.broadcasted_iota(jnp.int32, (count, 128), 1)
        index = lax.broadcasted_iota(jnp.int32, (count, 128), 0)
        spot = index + first
        spot = jnp.where(spot == PF + decode.shape[0], PF - 1, spot)
        return jnp.sum(jnp.where(lane == spot, row, 0.0), axis=1, keepdims=True)

    units = wg.shape[0]

    def expand(count):
        lo = 0
        while lo < units:
            n = min(256, units - lo)
            gated = nt(xn[0:count, :], wg[lo : lo + n, :])
            upward = nt(xn[0:count, :], wu[lo : lo + n, :])
            hid[0:count, lo : lo + n] = (jax.nn.silu(gated) * upward).astype(bf16)
            lo += n

    def contract(count, gates, store):
        for lo in range(0, width, 512):
            result = jnp.dot(hid[0:count, :], wd[:, lo : lo + 512], preferred_element_type=f32) * gates
            store(lo, result.astype(bf16))

    def enter(i):
        zo = planes[i]
        for s, (co, xo) in enumerate([(0, 0), (0, 1), (1, 0), (1, 1)]):
            normalize(s * PF, [slab[zo, co, xo, h].astype(f32) for h in range(2)])
        expand(4 * PF)

    def leave(i):
        zo = planes[i]
        gates = jnp.concatenate([gates_of(co, xo, zo, 0, PF) for co in range(2) for xo in range(2)], axis=0)

        def store(lo, result):
            h, at_col = lo // HALF, lo % HALF
            for s in range(4):
                prod[zo, s // 2, s % 2, h, :, at_col : at_col + 512] = result[s * PF : (s + 1) * PF]

        contract(4 * PF, gates, store)

    def add(a, b):
        return (a.astype(f32) + b.astype(f32)).astype(bf16)

    def rc(i):
        zo = planes[i]
        a = prod.at[zo, 1 - c]
        p = remote(a, cin.at[i], r_s.at[0, i], r_r.at[0, i], to_c)
        return p, p

    def rx1(i):
        p = remote(prod.at[planes[i], c, 1 - x, :, 0:32], xin.at[i], r_s.at[1, i], r_r.at[1, i], to_x)
        return p, p

    def ry1(i):
        p = remote(prod.at[planes[i], c, :, 1 - y, 32:64], yin.at[i], r_s.at[2, i], r_r.at[2, i], to_y)
        return p, p

    def ry2(i):
        p = remote(t0.at[i, 1 - y], y2.at[i], r_s.at[3, i], r_r.at[3, i], to_y)
        return p, p

    def rx2(i):
        p = remote(t1.at[i, 1 - x], x2.at[i], r_s.at[4, i], r_r.at[4, i], to_x)
        return p, p

    def rz(i, k):
        zo = planes[i]
        return (
            remote(s3.at[i, 32 * k : 32 * k + 32], zin.at[z, 32 * k : 32 * k + 32], rz_s.at[k, i - 1], rz_r.at[k, z], along(zo)),
            remote(s3.at[i, 32 * k : 32 * k + 32], zin.at[zo, 32 * k : 32 * k + 32], rz_s.at[k, i - 1], rz_r.at[k, zo], along(zo)),
        )

    def r0(i):
        send(rc(i)[0])

    def r1(i):
        zo = planes[i]
        take(rc(i))
        for xo in range(2):
            for h in range(2):
                prod[zo, c, xo, h] = add(prod[zo, c, xo, h], cin[i, xo, h])
        send(rx1(i)[0])
        send(ry1(i)[0])

    def r2(i):
        zo = planes[i]
        take(rx1(i))
        for h in range(2):
            t0[i, h] = add(prod[zo, c, x, h, 0:32], xin[i, h])
        send(ry2(i)[0])
        take(ry1(i))
        for xo in range(2):
            t1[i, xo] = add(prod[zo, c, xo, y, 32:64], yin[i, xo])
        send(rx2(i)[0])

    def r3(i):
        take(ry2(i))
        s3[i, 0:32] = add(t0[i, y], y2[i])
        if i > 0:
            send(rz(i, 0)[0])
        take(rx2(i))
        s3[i, 32:64] = add(t1[i, x], x2[i])
        if i > 0:
            send(rz(i, 1)[0])

    def enter_last():
        normalize(0, unfold(fb))
        expand(16 * FINAL)

    def leave_last():
        gates = jnp.concatenate(
            [gates_of(co, xo, zo, PF, FINAL) for co in range(2) for xo in range(2) for zo in range(4)], axis=0
        )

        def store(lo, result):
            h, at_col = lo // HALF, lo % HALF
            for s in range(4):
                pf[s // 2, h, s % 2, :, at_col : at_col + 512] = result[s * 32 : (s + 1) * 32]

        contract(16 * FINAL, gates, store)

    def fr(k):
        src, dst, target = [
            (pf.at[1 - c], fcin, to_c),
            (pf.at[c, :, 1 - x], fxin, to_x),
            (f2.at[1 - y], fyin, to_y),
        ][k]
        p = remote(src, dst, fr_s.at[k], fr_r.at[k], target)
        return p, p

    def frz(i):
        zo = planes[i]
        return (
            remote(f3.at[zo], fzin.at[z], fr_s.at[2 + i], fr_r.at[3 + z], along(zo)),
            remote(f3.at[zo], fzin.at[zo], fr_s.at[2 + i], fr_r.at[3 + zo], along(zo)),
        )

    def f_core():
        take(fr(0))
        for h in range(2):
            for xo in range(2):
                pf[c, h, xo] = add(pf[c, h, xo], fcin[h, xo])
        send(fr(1)[0])

    def f_x():
        take(fr(1))
        for h in range(2):
            f2[h] = add(pf[c, h, x], fxin[h])
        send(fr(2)[0])

    def f_y():
        take(fr(2))
        f3[...] = (f2[y].astype(f32) + fyin[...].astype(f32)).reshape(4, FINAL, HALF)
        for i in range(1, 4):
            send(frz(i)[0])

    def f_z():
        total = f3[z]
        for i in range(1, 4):
            take(frz(i))
            total = total + fzin[planes[i]]
        rows = rf[...] + total
        out[PF : out.shape[0], :] = rows[: out.shape[0] - PF].astype(bf16)
        fg[y, c, x, z] = fold(rows)
        for i in range(1, 4):
            send(lz(i)[0])

    def l_z():
        for i in range(1, 4):
            take(lz(i))
        send(lx()[0])

    def l_x():
        take(lx())
        send(ly()[0])

    def l_y():
        take(ly())
        send(lc()[0])

    def head_rows():
        take(lc())
        blocks = unfold(fg)
        total = sum(jnp.sum(b * b, axis=1, keepdims=True) for b in blocks)
        scale = lax.rsqrt(total * (1.0 / width) + epsilon)
        asked = order.shape[1]
        count = decode.shape[0]

        def spot(owner, row):
            return ((owner % 2 * 2 + owner // 2 % 2) * 4 + owner // 4) * FINAL + row

        last = spot(lax.broadcasted_iota(jnp.int32, (1, 16), 1), count)
        ordered = spot(order[...] // count, order[...] % count)
        picks = [
            jnp.where(lax.broadcasted_iota(jnp.int32, (16 * FINAL, n), 0) == s, 1.0, 0.0).astype(bf16)
            for s, n in [(last, 16), (ordered, asked)]
        ]
        tn = lambda a, b: lax.dot_general(a, b, (((0,), (0,)), ((), ())), preferred_element_type=f32)
        for k, b in enumerate(blocks):
            lo = k * (HALF // 2)
            normed = (b * scale * last_gain[:, lo : lo + HALF // 2]).astype(bf16)
            fn[0:16, lo : lo + HALF // 2] = tn(picks[0], normed).astype(bf16)
            fn[16 : 16 + asked, lo : lo + HALF // 2] = tn(picks[1], normed).astype(bf16)

    def head_columns():
        loads[3].wait()
        lo = 0
        while lo < hw.shape[0]:
            n = min(256, hw.shape[0] - lo)
            logits[:, lo : lo + n] = nt(fn[...], hw[lo : lo + n, :])
            lo += n

    spread(0)
    for i in range(1, 4):
        send(gz(i)[0])
    for i in range(1, 4):
        take(code_z(i))
    send(code_x()[0])
    for i in range(1, 4):
        take(first_z(i))
    send(first_x()[0])
    take(code_x())
    send(code_c()[0])
    take(first_x())
    send(first_y()[0])
    corner(0)
    spread(1)
    take(first_y())
    send(first_c()[0])
    close(0)
    spread(2)
    take(code_c())
    take(first_c())
    loads[0].wait()
    loads[1].wait()
    enter_last()
    corner(1)
    loads[2].wait()
    leave_last()
    send(fr(0)[0])
    spread(3)
    take(gc(0))
    enter(0)
    close(1)
    corner(2)
    leave(0)
    r0(0)
    take(gc(1))
    enter(1)
    close(2)
    f_core()
    r1(0)
    leave(1)
    r0(1)
    corner(3)
    take(gc(2))
    enter(2)
    r1(1)
    f_x()
    close(3)
    leave(2)
    r0(2)
    r2(0)
    f_y()
    r1(2)
    take(gc(3))
    enter(3)
    r2(1)
    r3(0)
    f_z()
    leave(3)
    r0(3)
    r2(2)
    r3(1)
    l_z()
    r1(3)
    l_x()
    r3(2)
    l_y()
    r2(3)
    head_rows()
    r3(3)
    head_columns()
    total = slab[z, c, x, y].astype(f32) + s3[0].astype(f32)
    for i in [1, 2, 3]:
        take(rz(i, 0))
        take(rz(i, 1))
        total = total + zin[planes[i]].astype(f32)
    out[0:PF, :] = total.astype(bf16)
    for copy in sent:
        copy.wait_send()


def layer(small, lengths, attn_weights, expert_weights, row_count):
    width = small[0].shape[1]
    units, vocab = expert_weights[0].shape[0], expert_weights[3].shape[0]
    slots = 16 + small[8].shape[1]
    heads = attn_weights[0].shape[1] // (NOPE + ROPE)
    dma = pltpu.SemaphoreType.DMA
    buf = lambda *shape: pltpu.VMEM(shape, jnp.bfloat16)
    wide = lambda *shape: pltpu.VMEM(shape, jnp.float32)
    vmem = pl.BlockSpec(memory_space=pltpu.VMEM)
    hbm = pl.BlockSpec(memory_space=pltpu.HBM)
    smem = pl.BlockSpec(memory_space=pltpu.SMEM)
    return pl.pallas_call(
        functools.partial(layer_kernel, heads),
        name="layer",
        out_shape=(
            pltpu.VMEM((row_count, HALF), jnp.bfloat16),
            pltpu.VMEM((slots, vocab), jnp.float32),
        ),
        in_specs=[vmem] * 9 + [smem] * 2 + [hbm] * 10,
        out_specs=(vmem,) * 2,
        scratch_shapes=[
            buf(units, width),
            buf(units, width),
            buf(units, width),
            buf(vocab, width),
            buf(SLAB, HALF),
            buf(4, 2, 2, 2, PF, HALF),
            buf(4, 2, 2, 2, PF, HALF),
            buf(4, 2, 2, PF, HALF),
            buf(4, 2, 32, HALF),
            buf(4, 2, 32, HALF),
            buf(4, 2, 32, HALF),
            buf(4, 2, 32, HALF),
            buf(4, 32, HALF),
            buf(4, 32, HALF),
            buf(4, PF, HALF),
            buf(4, PF, HALF),
            buf(4 * PF, width),
            buf(4 * PF, units),
            buf(2, 2, 2, 4, 2 * FINAL, HALF // 2),
            buf(2, 2, 4, 16, CODE),
            buf(2, 2, 2, 32, HALF),
            buf(2, 2, 32, HALF),
            buf(2, 32, HALF),
            buf(2, 32, HALF),
            buf(32, HALF),
            wide(4, FINAL, HALF),
            wide(4, FINAL, HALF),
            buf(2, 2, 2, 4, 2 * FINAL, HALF // 2),
            wide(FINAL, HALF),
            buf(slots, width),
            dma((10,)),
            dma((2,)),
            dma((2,)),
            dma((3,)),
            dma((4,)),
            dma((5, 4)),
            dma((5, 4)),
            dma((5, 4)),
            dma((5, 4)),
            dma((2, 3)),
            dma((2, 4)),
            dma((7,)),
            dma((7,)),
            dma((3, 7)),
            dma((3, 7)),
        ]
        + [pltpu.VMEM(a.shape, a.dtype) for a in attn_weights]
        + [buf(SLAB, width), wide(SLAB - PF, width), buf(SLAB, width), wide(16, 128)],
        compiler_params=pltpu.CompilerParams(
            collective_id=0, has_side_effects=True, vmem_limit_bytes=60 * 1024 * 1024
        ),
    )(*small, *lengths, *attn_weights, *expert_weights)


def on_block(
    prefill_tokens,
    decode_tokens,
    request_order,
    prefill_lengths,
    decode_lengths,
    latent_cache,
    attn_gain,
    w_query,
    w_latent,
    latent_gain,
    key_up,
    value_up,
    w_out,
    ffn_gain,
    expert_ids,
    expert_weights,
    w_gate,
    w_up,
    w_down,
    final_gain,
    head_weight,
):
    width = prefill_tokens.shape[1]
    small = (
        prefill_tokens,
        decode_tokens,
        attn_gain.reshape(1, width),
        ffn_gain.reshape(1, width),
        final_gain.reshape(1, width),
        latent_gain.reshape(1, LAT),
        expert_ids.T,
        expert_weights.T,
        request_order.reshape(1, -1),
    )
    return layer(
        small,
        (prefill_lengths, decode_lengths),
        (w_query, w_latent.T, jnp.swapaxes(latent_cache, 1, 2), key_up, value_up, w_out),
        (w_gate[0].T, w_up[0].T, w_down[0], head_weight.T),
        prefill_tokens.shape[0] + decode_tokens.shape[0],
    )


def on_device(
    prefill_tokens,
    decode_tokens,
    request_order,
    prefill_lengths,
    decode_lengths,
    latent_cache,
    attn_gain,
    w_query,
    w_latent,
    latent_gain,
    key_up,
    value_up,
    w_out,
    ffn_gain,
    expert_ids,
    expert_weights,
    w_gate,
    w_up,
    w_down,
    final_gain,
    head_weight,
):
    owners = lax.axis_size("ep")
    shards = lax.axis_size("vp")
    partial_attn = attend(
        prefill_tokens,
        decode_tokens,
        latent_cache,
        prefill_lengths,
        decode_lengths,
        attn_gain,
        w_query,
        w_latent,
        latent_gain,
        key_up,
        value_up,
        w_out,
    )
    attn = lax.psum(partial_attn, "vp")
    tokens = jnp.concatenate([prefill_tokens, decode_tokens], axis=0)
    resid = (tokens.astype(jnp.float32) + attn).astype(jnp.bfloat16)
    ffn_in = rms_norm(resid.astype(jnp.float32), ffn_gain).astype(jnp.bfloat16)
    row_count = tokens.shape[0]
    model_width = tokens.shape[1]
    share_width = model_width // shards
    capacity = max(2, min(row_count, row_count * TOPK * 2 // owners))
    flat_ids = expert_ids.reshape(-1)
    onehot = (flat_ids[:, None] == jnp.arange(owners, dtype=jnp.int32)[None, :]).astype(jnp.float32)
    entry = jnp.arange(flat_ids.shape[0], dtype=jnp.int32)
    before = (entry[:, None] > entry[None, :]).astype(jnp.bfloat16)
    earlier = jnp.dot(before, onehot.astype(jnp.bfloat16), preferred_element_type=jnp.float32)
    slot_index = jnp.sum(earlier * onehot, axis=1).astype(jnp.int32)
    target = flat_ids * capacity + slot_index
    source_rows = jnp.arange(row_count * TOPK, dtype=jnp.int32) // TOPK
    outgoing = (
        jnp.zeros((owners * capacity, model_width), jnp.bfloat16)
        .at[target]
        .set(ffn_in[source_rows])
    )
    outgoing = outgoing.reshape(owners, capacity, model_width)
    arrived = lax.all_to_all(outgoing, "ep", split_axis=0, concat_axis=0, tiled=True)
    item_count = arrived.shape[1]
    flattened = arrived.reshape(owners * item_count, model_width)
    gated = jnp.dot(flattened, w_gate[0], preferred_element_type=jnp.float32)
    upward = jnp.dot(flattened, w_up[0], preferred_element_type=jnp.float32)
    hidden_act = (jax.nn.silu(gated) * upward).astype(jnp.bfloat16)
    result = jnp.dot(hidden_act, w_down[0], preferred_element_type=jnp.float32).reshape(
        owners, item_count, model_width
    )
    summed = lax.psum_scatter(result, "vp", scatter_dimension=2, tiled=True)
    sent_back = lax.all_to_all(summed, "ep", split_axis=0, concat_axis=0, tiled=True)
    picked = sent_back.reshape(owners * capacity, sent_back.shape[2])[target]
    picked = picked.reshape(row_count, TOPK, sent_back.shape[2])
    routed_sum = jnp.sum(expert_weights[:, :, None] * picked, axis=1)
    column = lax.axis_index("vp") * share_width
    resid_share = lax.dynamic_slice_in_dim(resid, column, share_width, 1)
    layer_out = (resid_share.astype(jnp.float32) + routed_sum).astype(jnp.bfloat16)
    prefill_count = prefill_tokens.shape[0]
    decode_count = decode_tokens.shape[0]
    own_rows = layer_out[prefill_count - 1 :]
    everyone = lax.all_gather(own_rows, ("ep", "vp"), axis=0, tiled=True)
    everyone = everyone.reshape(owners, shards, 1 + decode_count, share_width)
    everyone = jnp.transpose(everyone, (0, 2, 1, 3)).reshape(owners, 1 + decode_count, model_width)
    prefill_last = everyone[:, 0]
    decode_rows = everyone[:, 1:].reshape(owners * decode_count, model_width)[request_order]
    final_rows = jnp.concatenate([prefill_last, decode_rows], axis=0)
    final_normed = rms_norm(final_rows.astype(jnp.float32), final_gain).astype(jnp.bfloat16)
    logits = jnp.dot(final_normed, head_weight, preferred_element_type=jnp.float32)
    return (layer_out, logits)


def solution(mesh):
    block = mesh.shape["vp"] == 2 and mesh.shape["ep"] == 16
    return jax.shard_map(
        on_block if block else on_device,
        mesh=mesh,
        in_specs=(
            P("ep", None),
            P("ep", None),
            P(),
            P("ep"),
            P("ep"),
            P("ep", None, None),
            P(),
            P(None, "vp"),
            P(),
            P(),
            P(None, "vp"),
            P(None, "vp"),
            P("vp", None),
            P(),
            P("ep", None),
            P("ep", None),
            P("ep", None, "vp"),
            P("ep", None, "vp"),
            P("ep", "vp", None),
            P(),
            P(None, ("ep", "vp")),
        ),
        out_specs=(P("ep", "vp"), P(None, ("ep", "vp"))),
        check_vma=False,
    )
```

```python
import functools
import math

import jax
import jax.numpy as jnp
from jax import lax
from jax.experimental import pallas as pl
from jax.experimental.pallas import tpu as pltpu
from jax.sharding import PartitionSpec as P

NOPE = 128
ROPE = 64
VD = 128
LAT = 512
TOPK = 6


epsilon = 1e-06
rope_base = 10000.0


def rms_norm(values, gain):
    return values * lax.rsqrt(jnp.mean(values * values, axis=-1, keepdims=True) + epsilon) * gain


def rotate(values, positions):
    half_width = values.shape[-1] // 2
    frequency = rope_base ** (-jnp.arange(half_width, dtype=jnp.float32) * 2.0 / values.shape[-1])
    angles = positions.astype(jnp.float32)[..., None] * frequency
    cosines = jnp.cos(angles)
    sines = jnp.sin(angles)
    lower_half = values[..., :half_width]
    upper_half = values[..., half_width:]
    return jnp.concatenate(
        [lower_half * cosines - upper_half * sines, lower_half * sines + upper_half * cosines],
        axis=-1,
    )


def attend(
    prefill_rows,
    decode_rows,
    cached,
    prefill_len,
    decode_len,
    attn_gain,
    w_query,
    w_latent,
    latent_gain,
    key_up,
    value_up,
    w_out,
):
    tokens = jnp.concatenate([prefill_rows, decode_rows], axis=0)
    prefill_count = prefill_rows.shape[0]
    row_count = tokens.shape[0]
    head_count = w_query.shape[1] // (NOPE + ROPE)
    positions = jnp.concatenate(
        [prefill_len[0] + jnp.arange(prefill_count, dtype=jnp.int32), decode_len]
    )
    normed = rms_norm(tokens.astype(jnp.float32), attn_gain).astype(jnp.bfloat16)
    queries = jnp.dot(normed, w_query, preferred_element_type=jnp.float32).reshape(
        row_count, head_count, NOPE + ROPE
    )
    query_nope = queries[..., :NOPE].astype(jnp.bfloat16)
    query_rope = rotate(queries[..., NOPE:], positions[:, None]).astype(jnp.bfloat16)
    latent = jnp.dot(normed, w_latent, preferred_element_type=jnp.float32)
    latent_normed = rms_norm(latent[:, :LAT], latent_gain)
    new_keys = jnp.concatenate([latent_normed, rotate(latent[:, LAT:], positions)], axis=1).astype(
        jnp.bfloat16
    )
    key_heads = key_up.reshape(LAT, head_count, NOPE)
    absorbed = jnp.einsum(
        "rhn,lhn->rhl", query_nope, key_heads, preferred_element_type=jnp.float32
    ).astype(jnp.bfloat16)
    query_all = jnp.concatenate([absorbed, query_rope], axis=-1)
    factor = 1.0 / jnp.sqrt(jnp.float32(NOPE + ROPE))
    cache_len = cached.shape[1]
    prefill_keys = jnp.concatenate([cached[0], new_keys[:prefill_count]], axis=0)
    scores = (
        jnp.einsum(
            "chk,jk->chj",
            query_all[:prefill_count],
            prefill_keys,
            preferred_element_type=jnp.float32,
        )
        * factor
    )
    key_index = jnp.arange(cache_len + prefill_count, dtype=jnp.int32)
    row_index = jnp.arange(prefill_count, dtype=jnp.int32)
    visible = jnp.where(
        key_index[None, :] < cache_len,
        key_index[None, :] < prefill_len[0],
        key_index[None, :] - cache_len <= row_index[:, None],
    )
    expo = jnp.exp(jnp.where(visible[:, None, :], scores, -jnp.inf))
    attn_probs = (expo / jnp.sum(expo, axis=-1, keepdims=True)).astype(jnp.bfloat16)
    prefill_context = jnp.einsum(
        "chj,jl->chl", attn_probs, prefill_keys[:, :LAT], preferred_element_type=jnp.float32
    ).astype(jnp.bfloat16)
    decode_query = query_all[prefill_count:]
    decode_cache = cached[1:]
    own_keys = new_keys[prefill_count:]
    cache_scores = (
        jnp.einsum("dhk,dsk->dhs", decode_query, decode_cache, preferred_element_type=jnp.float32)
        * factor
    )
    self_scores = (
        jnp.einsum("dhk,dk->dh", decode_query, own_keys, preferred_element_type=jnp.float32)
        * factor
    )
    cache_visible = jnp.arange(cache_len, dtype=jnp.int32)[None, :] < decode_len[:, None]
    cache_expo = jnp.exp(jnp.where(cache_visible[:, None, :], cache_scores, -jnp.inf))
    self_expo = jnp.exp(self_scores)
    totals = jnp.sum(cache_expo, axis=-1) + self_expo
    cache_probs = (cache_expo / totals[..., None]).astype(jnp.bfloat16)
    self_probs = (self_expo / totals).astype(jnp.bfloat16)
    decode_context = jnp.einsum(
        "dhs,dsl->dhl", cache_probs, decode_cache[..., :LAT], preferred_element_type=jnp.float32
    )
    decode_context = (
        decode_context
        + self_probs.astype(jnp.float32)[..., None] * own_keys[:, None, :LAT].astype(jnp.float32)
    ).astype(jnp.bfloat16)
    context = jnp.concatenate([prefill_context, decode_context], axis=0)
    value_heads = value_up.reshape(LAT, head_count, VD)
    head_out = jnp.einsum(
        "rhl,lhv->rhv", context, value_heads, preferred_element_type=jnp.float32
    ).astype(jnp.bfloat16)
    return jnp.dot(
        head_out.reshape(row_count, head_count * VD), w_out, preferred_element_type=jnp.float32
    )


MESH = pl.DeviceIdType.MESH
SLAB = 80
PF = 64
FINAL = 8
HALF = 1024
CODE = 256


def place():
    e = lax.axis_index("ep")
    return e // 4, (e // 2) % 2, e % 2, lax.axis_index("vp")


def at(z, x, c, y):
    return {"ep": z * 4 + x * 2 + c, "vp": y}


def remote(src, dst, send, recv, target):
    return pltpu.make_async_remote_copy(
        src_ref=src, dst_ref=dst, send_sem=send, recv_sem=recv, device_id=target, device_id_type=MESH
    )


def layer_kernel(heads, prefill, decode, again, gain, last_gain, lgain, ids, mix, order, plen, dlen, wq_hbm, wl_hbm, cache_hbm, ku_hbm, vu_hbm, wo_hbm, wg_hbm, wu_hbm, wd_hbm, hw_hbm, out, logits, *scratch):
    (wg, wu, wd, hw, got, slab, prod, cin, xin, yin, t0, t1, y2, x2, s3, zin) = scratch[:16]
    (xn, hid, fb, cb, pf, fcin, fxin, f3, fzin, fg, rf, fn) = scratch[16:28]
    (w_sem, sw_s, sw_r, gz_s, gz_r, g_s, g_r) = scratch[28:35]
    (r_s, r_r, rz_s, rz_r, fr_s, fr_r, tree_s, tree_r) = scratch[35:43]
    (wq, wl, cache, ku, vu, wo, tok, tail, part, dense) = scratch[43:]
    f32, bf16 = jnp.float32, jnp.bfloat16
    nt = lambda a, b: lax.dot_general(a, b, (((1,), (1,)), ((), ())), preferred_element_type=f32)
    z, x, c, y = place()
    mine = z * 4 + x * 2 + c
    near = z + 1 - 2 * (z % 2)
    planes = [z, near, 3 - 3 * (z // 2), 2 - z // 2]
    to_x, to_y, to_c = at(z, 1 - x, c, y), at(z, x, c, 1 - y), at(z, x, 1 - c, y)
    to_d = at(z, 1 - x, c, 1 - y)
    square = [(1 - x, y, to_x), (x, 1 - y, to_y), (1 - x, 1 - y, to_d)]

    def along(zo):
        return at(zo, x, c, y)

    pairs = [(wg_hbm, wg), (wu_hbm, wu), (wd_hbm, wd), (hw_hbm, hw)]
    pairs += [(wq_hbm, wq), (wl_hbm, wl), (cache_hbm, cache), (ku_hbm, ku), (vu_hbm, vu), (wo_hbm, wo)]
    loads = [pltpu.make_async_copy(a, b, w_sem.at[i]) for i, (a, b) in enumerate(pairs)]
    for load in loads[4:] + loads[:4]:
        load.start()
    barrier = pltpu.get_barrier_semaphore()
    for target in [to_x, to_y, to_c, to_d] + [along(zo) for zo in planes[1:]]:
        pl.semaphore_signal(barrier, inc=1, device_id=target, device_id_type=MESH)
    sent = []

    def send(copy):
        copy.start()
        sent.append(copy)

    def cols(h):
        return pl.ds(pl.multiple_of(h * HALF, HALF), HALF)

    def swap(i):
        rows = pl.ds(PF, SLAB - PF) if i == 0 else pl.ds(0, PF)
        p = remote(part.at[rows, cols(1 - y)], got.at[rows, :], sw_s.at[i], sw_r.at[i], to_y)
        return p, p

    def same(ref_out, ref_in, s, r, target):
        return remote(ref_out, ref_out, s, r, target), remote(ref_in, ref_in, s, r, target)

    def gz(i):
        zo = planes[i]
        a, b = slab.at[z, c, x, y], slab.at[zo, c, x, y]
        return remote(a, a, gz_s.at[i - 1], gz_r.at[z], along(zo)), remote(b, b, gz_s.at[i - 1], gz_r.at[zo], along(zo))

    def gx(i):
        zo = planes[i]
        return same(slab.at[zo, c, x, y], slab.at[zo, c, 1 - x, y], g_s.at[0, i], g_r.at[0, i], to_x)

    def gy(i):
        zo = planes[i]
        return same(slab.at[zo, c, x, y], slab.at[zo, c, x, 1 - y], g_s.at[1, i], g_r.at[1, i], to_y)

    def dx(i):
        zo = planes[i]
        return same(
            slab.at[zo, c, x, 1 - y, 32:64], slab.at[zo, c, 1 - x, 1 - y, 32:64], g_s.at[2, i], g_r.at[2, i], to_x
        )

    def dy(i):
        zo = planes[i]
        return same(
            slab.at[zo, c, 1 - x, y, 0:32], slab.at[zo, c, 1 - x, 1 - y, 0:32], g_s.at[3, i], g_r.at[3, i], to_y
        )

    def gc(i):
        zo = planes[i]
        return same(slab.at[zo, c], slab.at[zo, 1 - c], g_s.at[4, i], g_r.at[4, i], to_c)

    def tree(k, block):
        def hop_z(i):
            zo = planes[i]
            return (
                remote(block(c, x, z), block(c, x, z), tree_s.at[k, i], tree_r.at[k, z], along(zo)),
                remote(block(c, x, zo), block(c, x, zo), tree_s.at[k, i], tree_r.at[k, zo], along(zo)),
            )

        return hop_z

    def hop(k, j, leaves, lands, target):
        return same(leaves, lands, tree_s.at[k, 4 + j], tree_r.at[k, 4 + j], target)

    code_z = tree(0, lambda co, xo, zo: cb.at[co, xo, zo])
    code_x = lambda: hop(0, 0, cb.at[c, x], cb.at[c, 1 - x], to_x)
    code_c = lambda: hop(0, 2, cb.at[c], cb.at[1 - c], to_c)
    first_z = tree(1, lambda co, xo, zo: fb.at[y, co, xo, zo])
    def around(k, ref):
        return [hop(k, j, ref.at[y, c, x], ref.at[yo, c, xo], to) for j, (xo, yo, to) in enumerate(square)]

    first_c = lambda: hop(1, 3, fb.at[:, c], fb.at[:, 1 - c], to_c)
    lz = tree(2, lambda co, xo, zo: fg.at[y, co, xo, zo])
    lc = lambda: hop(2, 3, fg.at[:, c], fg.at[:, 1 - c], to_c)

    tail[...] = jnp.zeros_like(tail)
    tail[0 : decode.shape[0], :] = decode[...].astype(f32)
    tail[decode.shape[0] : decode.shape[0] + 1, :] = prefill[PF - 16 : PF, :].astype(f32)[15:16]
    tok[0:PF, :] = prefill[...]
    tok[PF:SLAB, :] = tail[...].astype(bf16)
    dense[...] = jnp.zeros_like(dense)
    expert = lax.broadcasted_iota(jnp.int32, (16, ids.shape[1]), 0)
    named = jnp.zeros((16, ids.shape[1]), f32)
    for k in range(TOPK):
        named = named + jnp.where(ids[k : k + 1, :] == expert, mix[k : k + 1, :], 0.0)
    dense[:, 0 : ids.shape[1]] = named
    high = dense[...].astype(bf16)
    cb[c, x, z, :, 0:128] = high
    cb[c, x, z, :, 128:256] = (dense[...] - high.astype(f32)).astype(bf16)
    row = lax.broadcasted_iota(jnp.int32, (SLAB, 1), 0)
    length = jnp.where(row < PF, plen[0], 0)
    for j in range(decode.shape[0]):
        length = jnp.where(row == PF + j, dlen[j], length)
    position = jnp.where(row < PF, length + row, length).astype(f32)
    lane = lax.broadcasted_iota(jnp.int32, (1, ROPE), 1)
    upper = lane >= ROPE // 2
    power = jnp.where(upper, lane - ROPE // 2, lane).astype(f32)
    angles = position * jnp.exp(power * (-2.0 / ROPE * math.log(rope_base)))
    cosines = jnp.cos(angles)
    sines = jnp.where(upper, 1.0, -1.0) * jnp.sin(angles)
    pl.semaphore_wait(barrier, 7)
    for i in range(1, 4):
        send(code_z(i)[0])

    def turn(v):
        half = ROPE // 2
        return v * cosines + jnp.concatenate([v[:, half:], v[:, :half]], axis=1) * sines

    dot = functools.partial(jnp.dot, preferred_element_type=f32)
    normed = rms_norm(tok[...].astype(f32), again[...]).astype(bf16)
    loads[4].wait()
    queries = dot(normed, wq[...])
    loads[5].wait()
    latent = nt(normed, wl[...])
    key_lat = rms_norm(latent[:, :LAT], lgain[...]).astype(bf16)
    key_rope = turn(latent[:, LAT:]).astype(bf16)
    loads[6].wait()
    entries, cache_len = cache.shape[0], cache.shape[2]
    rows_of = PF + decode.shape[0]
    spare = SLAB - PF
    factor = 1.0 / jnp.sqrt(jnp.float32(NOPE + ROPE))
    loads[7].wait()
    absorbed, ropes = [], []
    for h in range(heads):
        base = h * (NOPE + ROPE)
        q_nope = queries[:, base : base + NOPE].astype(bf16)
        ropes.append(turn(queries[:, base + NOPE : base + NOPE + ROPE]).astype(bf16))
        absorbed.append(nt(q_nope, ku[:, h * NOPE : (h + 1) * NOPE]).astype(bf16))

    def share(lo, hi, held, old_seen, new_seen):
        q_lat = jnp.concatenate([a[lo:hi] for a in absorbed], axis=0)
        q_rope = jnp.concatenate([r[lo:hi] for r in ropes], axis=0)
        old = [dot(q_lat, cache[e, :LAT, :]) + dot(q_rope, cache[e, LAT:, :]) for e in held]
        old = (old[0] if len(held) == 1 else jnp.concatenate(old, axis=1)) * factor
        new = (nt(q_lat, key_lat[lo:hi]) + nt(q_rope, key_rope[lo:hi])) * factor
        old = jnp.exp(jnp.where(old_seen, old, -jnp.inf))
        new = jnp.exp(jnp.where(new_seen, new, -jnp.inf))
        total = jnp.sum(old, axis=1, keepdims=True) + jnp.sum(new, axis=1, keepdims=True)
        old = (old / total).astype(bf16)
        new = (new / total).astype(bf16)
        context = dot(new, key_lat[lo:hi])
        for i, e in enumerate(held):
            context = context + nt(old[:, i * cache_len : (i + 1) * cache_len], cache[e, :LAT, :])
        return context.astype(bf16)

    stacked = lax.broadcasted_iota(jnp.int32, (heads * PF, 1), 0) % PF
    key = lax.broadcasted_iota(jnp.int32, (1, cache_len), 1)
    col = lax.broadcasted_iota(jnp.int32, (1, PF), 1)
    prefill_context = share(0, PF, [0], key < plen[0], col <= stacked)
    stacked = lax.broadcasted_iota(jnp.int32, (heads * spare, 1), 0) % spare
    held = list(range(1, entries))
    seen = jnp.zeros((heads * spare, 1), jnp.int32)
    for j in range(decode.shape[0]):
        seen = jnp.where(stacked == j, dlen[j], seen)
    start = stacked * cache_len
    key = lax.broadcasted_iota(jnp.int32, (1, len(held) * cache_len), 1)
    col = lax.broadcasted_iota(jnp.int32, (1, spare), 1)
    decode_context = share(PF, SLAB, held, (key >= start) & (key < start + seen), col == stacked)
    loads[8].wait()
    values = []
    for h in range(heads):
        context = jnp.concatenate(
            [prefill_context[h * PF : (h + 1) * PF], decode_context[h * spare : (h + 1) * spare]], axis=0
        )
        value = dot(context, vu[:, h * VD : (h + 1) * VD])
        values.append(jnp.where(row == rows_of, value[PF - 1 : PF], value).astype(bf16))
    values = jnp.concatenate(values, axis=1)
    loads[9].wait()
    part[:, cols(1 - y)] = dot(values, wo[:, cols(1 - y)]).astype(bf16)
    send(swap(0)[0])
    send(swap(1)[0])
    part[:, cols(y)] = dot(values, wo[:, cols(y)]).astype(bf16)

    def fold(rows):
        return jnp.concatenate([rows[:, : HALF // 2], rows[:, HALF // 2 :]], axis=0).astype(bf16)

    swap(0)[1].wait_recv()
    rows = part[PF:SLAB, cols(y)].astype(f32) + got[PF:SLAB, :].astype(f32)
    rows = tok[PF:SLAB, cols(y)].astype(f32) + rows
    rf[...] = rows[:FINAL].astype(bf16).astype(f32)
    fb[y, c, x, z] = fold(rows[:FINAL])
    for i in range(1, 4):
        send(first_z(i)[0])
    swap(1)[1].wait_recv()
    rows = part[0:PF, cols(y)].astype(f32) + got[0:PF, :].astype(f32)
    slab[z, c, x, y] = (tok[0:PF, cols(y)].astype(f32) + rows).astype(bf16)

    def take(pair):
        pair[1].wait_recv()

    def spread(i):
        if i > 0:
            take(gz(i))
        send(gx(i)[0])
        send(gy(i)[0])

    def corner(i):
        take(gx(i))
        send(dy(i)[0])
        take(gy(i))
        send(dx(i)[0])

    def close(i):
        take(dx(i))
        take(dy(i))
        send(gc(i)[0])

    width = 2 * HALF

    def normalize(top, blocks):
        total = sum(jnp.sum(b * b, axis=1, keepdims=True) for b in blocks)
        scale = lax.rsqrt(total * (1.0 / width) + epsilon)
        count, wide = blocks[0].shape
        for k, b in enumerate(blocks):
            lo = k * wide
            xn[top : top + count, lo : lo + wide] = (b * scale * gain[:, lo : lo + wide]).astype(bf16)

    def unfold(ref):
        rows = ref[...].astype(f32).reshape(2, 16, 2 * FINAL, HALF // 2)
        return [
            rows[yo, :, q * FINAL : (q + 1) * FINAL].reshape(16 * FINAL, HALF // 2) for yo in range(2) for q in range(2)
        ]

    def gates_of(co, xo, zo, first, count):
        block = cb[co, xo, zo].astype(f32)
        expert = lax.broadcasted_iota(jnp.int32, block.shape, 0)
        row = jnp.sum(jnp.where(expert == mine, block, 0.0), axis=0, keepdims=True)
        row = row[:, 0:128] + row[:, 128:256]
        lane = lax.broadcasted_iota(jnp.int32, (count, 128), 1)
        index = lax.broadcasted_iota(jnp.int32, (count, 128), 0)
        spot = index + first
        spot = jnp.where(spot == PF + decode.shape[0], PF - 1, spot)
        return jnp.sum(jnp.where(lane == spot, row, 0.0), axis=1, keepdims=True)

    units = wg.shape[0]

    def expand(count):
        lo = 0
        while lo < units:
            n = min(256, units - lo)
            gated = nt(xn[0:count, :], wg[lo : lo + n, :])
            upward = nt(xn[0:count, :], wu[lo : lo + n, :])
            hid[0:count, lo : lo + n] = (jax.nn.silu(gated) * upward).astype(bf16)
            lo += n

    def contract(count, gates, store):
        for lo in range(0, width, 512):
            result = jnp.dot(hid[0:count, :], wd[:, lo : lo + 512], preferred_element_type=f32) * gates
            store(lo, result.astype(bf16))

    def enter(i):
        zo = planes[i]
        for s, (co, xo) in enumerate([(0, 0), (0, 1), (1, 0), (1, 1)]):
            normalize(s * PF, [slab[zo, co, xo, h].astype(f32) for h in range(2)])
        expand(4 * PF)

    def leave(i):
        zo = planes[i]
        gates = jnp.concatenate([gates_of(co, xo, zo, 0, PF) for co in range(2) for xo in range(2)], axis=0)

        def store(lo, result):
            h, at_col = lo // HALF, lo % HALF
            for s in range(4):
                prod[zo, s // 2, s % 2, h, :, at_col : at_col + 512] = result[s * PF : (s + 1) * PF]

        contract(4 * PF, gates, store)

    def add(a, b):
        return (a.astype(f32) + b.astype(f32)).astype(bf16)

    def rc(i):
        zo = planes[i]
        a = prod.at[zo, 1 - c]
        p = remote(a, cin.at[i], r_s.at[0, i], r_r.at[0, i], to_c)
        return p, p

    def rx1(i):
        p = remote(prod.at[planes[i], c, 1 - x, :, 0:32], xin.at[i], r_s.at[1, i], r_r.at[1, i], to_x)
        return p, p

    def ry1(i):
        p = remote(prod.at[planes[i], c, :, 1 - y, 32:64], yin.at[i], r_s.at[2, i], r_r.at[2, i], to_y)
        return p, p

    def ry2(i):
        p = remote(t0.at[i, 1 - y], y2.at[i], r_s.at[3, i], r_r.at[3, i], to_y)
        return p, p

    def rx2(i):
        p = remote(t1.at[i, 1 - x], x2.at[i], r_s.at[4, i], r_r.at[4, i], to_x)
        return p, p

    def rz(i, k):
        zo = planes[i]
        return (
            remote(s3.at[i, 32 * k : 32 * k + 32], zin.at[z, 32 * k : 32 * k + 32], rz_s.at[k, i - 1], rz_r.at[k, z], along(zo)),
            remote(s3.at[i, 32 * k : 32 * k + 32], zin.at[zo, 32 * k : 32 * k + 32], rz_s.at[k, i - 1], rz_r.at[k, zo], along(zo)),
        )

    def r0(i):
        send(rc(i)[0])

    def r1(i):
        zo = planes[i]
        take(rc(i))
        for xo in range(2):
            for h in range(2):
                prod[zo, c, xo, h] = add(prod[zo, c, xo, h], cin[i, xo, h])
        send(rx1(i)[0])
        send(ry1(i)[0])

    def r2(i):
        zo = planes[i]
        take(rx1(i))
        for h in range(2):
            t0[i, h] = add(prod[zo, c, x, h, 0:32], xin[i, h])
        send(ry2(i)[0])
        take(ry1(i))
        for xo in range(2):
            t1[i, xo] = add(prod[zo, c, xo, y, 32:64], yin[i, xo])
        send(rx2(i)[0])

    def r3(i):
        take(ry2(i))
        s3[i, 0:32] = add(t0[i, y], y2[i])
        if i > 0:
            send(rz(i, 0)[0])
        take(rx2(i))
        s3[i, 32:64] = add(t1[i, x], x2[i])
        if i > 0:
            send(rz(i, 1)[0])

    def enter_last():
        normalize(0, unfold(fb))
        expand(16 * FINAL)

    def leave_last():
        gates = jnp.concatenate(
            [gates_of(co, xo, zo, PF, FINAL) for co in range(2) for xo in range(2) for zo in range(4)], axis=0
        )

        def store(lo, result):
            h, at_col = lo // HALF, lo % HALF
            for s in range(4):
                pf[s // 2, h, s % 2, :, at_col : at_col + 512] = result[s * 32 : (s + 1) * 32]

        contract(16 * FINAL, gates, store)

    def fr():
        p = remote(pf.at[1 - c], fcin, fr_s.at[0], fr_r.at[0], to_c)
        return p, p

    def fr_around():
        return [
            (p, p)
            for p in [
                remote(pf.at[c, yo, xo], fxin.at[j], fr_s.at[7 + j], fr_r.at[7 + j], to)
                for j, (xo, yo, to) in enumerate(square)
            ]
        ]

    def frz(i):
        zo = planes[i]
        return (
            remote(f3.at[zo], fzin.at[z], fr_s.at[2 + i], fr_r.at[3 + z], along(zo)),
            remote(f3.at[zo], fzin.at[zo], fr_s.at[2 + i], fr_r.at[3 + zo], along(zo)),
        )

    def f_core():
        take(fr())
        for h in range(2):
            for xo in range(2):
                pf[c, h, xo] = add(pf[c, h, xo], fcin[h, xo])
        for p in fr_around():
            send(p[0])

    def f_xy():
        total = pf[c, y, x].astype(f32)
        for j, p in enumerate(fr_around()):
            take(p)
            total = total + fxin[j].astype(f32)
        f3[...] = total.reshape(4, FINAL, HALF)
        for i in range(1, 4):
            send(frz(i)[0])

    def f_z():
        total = f3[z]
        for i in range(1, 4):
            take(frz(i))
            total = total + fzin[planes[i]]
        rows = rf[...] + total
        out[PF : out.shape[0], :] = rows[: out.shape[0] - PF].astype(bf16)
        fg[y, c, x, z] = fold(rows)
        for i in range(1, 4):
            send(lz(i)[0])

    def l_z():
        for i in range(1, 4):
            take(lz(i))
        for p in around(2, fg):
            send(p[0])

    def l_xy():
        for p in around(2, fg):
            take(p)
        send(lc()[0])

    def head_rows():
        take(lc())
        blocks = unfold(fg)
        total = sum(jnp.sum(b * b, axis=1, keepdims=True) for b in blocks)
        scale = lax.rsqrt(total * (1.0 / width) + epsilon)
        asked = order.shape[1]
        count = decode.shape[0]

        def spot(owner, row):
            return ((owner % 2 * 2 + owner // 2 % 2) * 4 + owner // 4) * FINAL + row

        last = spot(lax.broadcasted_iota(jnp.int32, (1, 16), 1), count)
        ordered = spot(order[...] // count, order[...] % count)
        picks = [
            jnp.where(lax.broadcasted_iota(jnp.int32, (16 * FINAL, n), 0) == s, 1.0, 0.0).astype(bf16)
            for s, n in [(last, 16), (ordered, asked)]
        ]
        tn = lambda a, b: lax.dot_general(a, b, (((0,), (0,)), ((), ())), preferred_element_type=f32)
        for k, b in enumerate(blocks):
            lo = k * (HALF // 2)
            normed = (b * scale * last_gain[:, lo : lo + HALF // 2]).astype(bf16)
            fn[0:16, lo : lo + HALF // 2] = tn(picks[0], normed).astype(bf16)
            fn[16 : 16 + asked, lo : lo + HALF // 2] = tn(picks[1], normed).astype(bf16)

    def head_columns():
        loads[3].wait()
        lo = 0
        while lo < hw.shape[0]:
            n = min(256, hw.shape[0] - lo)
            logits[:, lo : lo + n] = nt(fn[...], hw[lo : lo + n, :])
            lo += n

    spread(0)
    for i in range(1, 4):
        send(gz(i)[0])
    for i in range(1, 4):
        take(code_z(i))
    send(code_x()[0])
    for i in range(1, 4):
        take(first_z(i))
    for p in around(1, fb):
        send(p[0])
    take(code_x())
    send(code_c()[0])
    corner(0)
    spread(1)
    for p in around(1, fb):
        take(p)
    send(first_c()[0])
    close(0)
    spread(2)
    take(code_c())
    take(first_c())
    loads[0].wait()
    loads[1].wait()
    enter_last()
    corner(1)
    loads[2].wait()
    leave_last()
    send(fr()[0])
    spread(3)
    take(gc(0))
    enter(0)
    close(1)
    corner(2)
    leave(0)
    r0(0)
    take(gc(1))
    enter(1)
    close(2)
    corner(3)
    f_core()
    r1(0)
    leave(1)
    r0(1)
    take(gc(2))
    enter(2)
    r1(1)
    close(3)
    leave(2)
    r0(2)
    r2(0)
    r1(2)
    f_xy()
    take(gc(3))
    enter(3)
    r2(1)
    r3(0)
    leave(3)
    r0(3)
    r2(2)
    f_z()
    r1(3)
    r3(1)
    l_z()
    r3(2)
    r2(3)
    l_xy()
    r3(3)
    head_rows()
    head_columns()
    total = slab[z, c, x, y].astype(f32) + s3[0].astype(f32)
    for i in [1, 2, 3]:
        take(rz(i, 0))
        take(rz(i, 1))
        total = total + zin[planes[i]].astype(f32)
    out[0:PF, :] = total.astype(bf16)
    for copy in sent:
        copy.wait_send()


def layer(small, lengths, attn_weights, expert_weights, row_count):
    width = small[0].shape[1]
    units, vocab = expert_weights[0].shape[0], expert_weights[3].shape[0]
    slots = 16 + small[8].shape[1]
    heads = attn_weights[0].shape[1] // (NOPE + ROPE)
    dma = pltpu.SemaphoreType.DMA
    buf = lambda *shape: pltpu.VMEM(shape, jnp.bfloat16)
    wide = lambda *shape: pltpu.VMEM(shape, jnp.float32)
    vmem = pl.BlockSpec(memory_space=pltpu.VMEM)
    hbm = pl.BlockSpec(memory_space=pltpu.HBM)
    smem = pl.BlockSpec(memory_space=pltpu.SMEM)
    return pl.pallas_call(
        functools.partial(layer_kernel, heads),
        name="layer",
        out_shape=(
            pltpu.VMEM((row_count, HALF), jnp.bfloat16),
            pltpu.VMEM((slots, vocab), jnp.float32),
        ),
        in_specs=[vmem] * 9 + [smem] * 2 + [hbm] * 10,
        out_specs=(vmem,) * 2,
        scratch_shapes=[
            buf(units, width),
            buf(units, width),
            buf(units, width),
            buf(vocab, width),
            buf(SLAB, HALF),
            buf(4, 2, 2, 2, PF, HALF),
            buf(4, 2, 2, 2, PF, HALF),
            buf(4, 2, 2, PF, HALF),
            buf(4, 2, 32, HALF),
            buf(4, 2, 32, HALF),
            buf(4, 2, 32, HALF),
            buf(4, 2, 32, HALF),
            buf(4, 32, HALF),
            buf(4, 32, HALF),
            buf(4, PF, HALF),
            buf(4, PF, HALF),
            buf(4 * PF, width),
            buf(4 * PF, units),
            buf(2, 2, 2, 4, 2 * FINAL, HALF // 2),
            buf(2, 2, 4, 16, CODE),
            buf(2, 2, 2, 32, HALF),
            buf(2, 2, 32, HALF),
            buf(3, 32, HALF),
            wide(4, FINAL, HALF),
            wide(4, FINAL, HALF),
            buf(2, 2, 2, 4, 2 * FINAL, HALF // 2),
            wide(FINAL, HALF),
            buf(slots, width),
            dma((10,)),
            dma((2,)),
            dma((2,)),
            dma((3,)),
            dma((4,)),
            dma((5, 4)),
            dma((5, 4)),
            dma((5, 4)),
            dma((5, 4)),
            dma((2, 3)),
            dma((2, 4)),
            dma((10,)),
            dma((10,)),
            dma((3, 8)),
            dma((3, 8)),
        ]
        + [pltpu.VMEM(a.shape, a.dtype) for a in attn_weights]
        + [buf(SLAB, width), wide(SLAB - PF, width), buf(SLAB, width), wide(16, 128)],
        compiler_params=pltpu.CompilerParams(
            collective_id=0, has_side_effects=True, vmem_limit_bytes=60 * 1024 * 1024
        ),
    )(*small, *lengths, *attn_weights, *expert_weights)


def on_block(
    prefill_tokens,
    decode_tokens,
    request_order,
    prefill_lengths,
    decode_lengths,
    latent_cache,
    attn_gain,
    w_query,
    w_latent,
    latent_gain,
    key_up,
    value_up,
    w_out,
    ffn_gain,
    expert_ids,
    expert_weights,
    w_gate,
    w_up,
    w_down,
    final_gain,
    head_weight,
):
    width = prefill_tokens.shape[1]
    small = (
        prefill_tokens,
        decode_tokens,
        attn_gain.reshape(1, width),
        ffn_gain.reshape(1, width),
        final_gain.reshape(1, width),
        latent_gain.reshape(1, LAT),
        expert_ids.T,
        expert_weights.T,
        request_order.reshape(1, -1),
    )
    return layer(
        small,
        (prefill_lengths, decode_lengths),
        (w_query, w_latent.T, jnp.swapaxes(latent_cache, 1, 2), key_up, value_up, w_out),
        (w_gate[0].T, w_up[0].T, w_down[0], head_weight.T),
        prefill_tokens.shape[0] + decode_tokens.shape[0],
    )


def on_device(
    prefill_tokens,
    decode_tokens,
    request_order,
    prefill_lengths,
    decode_lengths,
    latent_cache,
    attn_gain,
    w_query,
    w_latent,
    latent_gain,
    key_up,
    value_up,
    w_out,
    ffn_gain,
    expert_ids,
    expert_weights,
    w_gate,
    w_up,
    w_down,
    final_gain,
    head_weight,
):
    owners = lax.axis_size("ep")
    shards = lax.axis_size("vp")
    partial_attn = attend(
        prefill_tokens,
        decode_tokens,
        latent_cache,
        prefill_lengths,
        decode_lengths,
        attn_gain,
        w_query,
        w_latent,
        latent_gain,
        key_up,
        value_up,
        w_out,
    )
    attn = lax.psum(partial_attn, "vp")
    tokens = jnp.concatenate([prefill_tokens, decode_tokens], axis=0)
    resid = (tokens.astype(jnp.float32) + attn).astype(jnp.bfloat16)
    ffn_in = rms_norm(resid.astype(jnp.float32), ffn_gain).astype(jnp.bfloat16)
    row_count = tokens.shape[0]
    model_width = tokens.shape[1]
    share_width = model_width // shards
    capacity = max(2, min(row_count, row_count * TOPK * 2 // owners))
    flat_ids = expert_ids.reshape(-1)
    onehot = (flat_ids[:, None] == jnp.arange(owners, dtype=jnp.int32)[None, :]).astype(jnp.float32)
    entry = jnp.arange(flat_ids.shape[0], dtype=jnp.int32)
    before = (entry[:, None] > entry[None, :]).astype(jnp.bfloat16)
    earlier = jnp.dot(before, onehot.astype(jnp.bfloat16), preferred_element_type=jnp.float32)
    slot_index = jnp.sum(earlier * onehot, axis=1).astype(jnp.int32)
    target = flat_ids * capacity + slot_index
    source_rows = jnp.arange(row_count * TOPK, dtype=jnp.int32) // TOPK
    outgoing = (
        jnp.zeros((owners * capacity, model_width), jnp.bfloat16)
        .at[target]
        .set(ffn_in[source_rows])
    )
    outgoing = outgoing.reshape(owners, capacity, model_width)
    arrived = lax.all_to_all(outgoing, "ep", split_axis=0, concat_axis=0, tiled=True)
    item_count = arrived.shape[1]
    flattened = arrived.reshape(owners * item_count, model_width)
    gated = jnp.dot(flattened, w_gate[0], preferred_element_type=jnp.float32)
    upward = jnp.dot(flattened, w_up[0], preferred_element_type=jnp.float32)
    hidden_act = (jax.nn.silu(gated) * upward).astype(jnp.bfloat16)
    result = jnp.dot(hidden_act, w_down[0], preferred_element_type=jnp.float32).reshape(
        owners, item_count, model_width
    )
    summed = lax.psum_scatter(result, "vp", scatter_dimension=2, tiled=True)
    sent_back = lax.all_to_all(summed, "ep", split_axis=0, concat_axis=0, tiled=True)
    picked = sent_back.reshape(owners * capacity, sent_back.shape[2])[target]
    picked = picked.reshape(row_count, TOPK, sent_back.shape[2])
    routed_sum = jnp.sum(expert_weights[:, :, None] * picked, axis=1)
    column = lax.axis_index("vp") * share_width
    resid_share = lax.dynamic_slice_in_dim(resid, column, share_width, 1)
    layer_out = (resid_share.astype(jnp.float32) + routed_sum).astype(jnp.bfloat16)
    prefill_count = prefill_tokens.shape[0]
    decode_count = decode_tokens.shape[0]
    own_rows = layer_out[prefill_count - 1 :]
    everyone = lax.all_gather(own_rows, ("ep", "vp"), axis=0, tiled=True)
    everyone = everyone.reshape(owners, shards, 1 + decode_count, share_width)
    everyone = jnp.transpose(everyone, (0, 2, 1, 3)).reshape(owners, 1 + decode_count, model_width)
    prefill_last = everyone[:, 0]
    decode_rows = everyone[:, 1:].reshape(owners * decode_count, model_width)[request_order]
    final_rows = jnp.concatenate([prefill_last, decode_rows], axis=0)
    final_normed = rms_norm(final_rows.astype(jnp.float32), final_gain).astype(jnp.bfloat16)
    logits = jnp.dot(final_normed, head_weight, preferred_element_type=jnp.float32)
    return (layer_out, logits)


def solution(mesh):
    block = mesh.shape["vp"] == 2 and mesh.shape["ep"] == 16
    return jax.shard_map(
        on_block if block else on_device,
        mesh=mesh,
        in_specs=(
            P("ep", None),
            P("ep", None),
            P(),
            P("ep"),
            P("ep"),
            P("ep", None, None),
            P(),
            P(None, "vp"),
            P(),
            P(),
            P(None, "vp"),
            P(None, "vp"),
            P("vp", None),
            P(),
            P("ep", None),
            P("ep", None),
            P("ep", None, "vp"),
            P("ep", None, "vp"),
            P("ep", "vp", None),
            P(),
            P(None, ("ep", "vp")),
        ),
        out_specs=(P("ep", "vp"), P(None, ("ep", "vp"))),
        check_vma=False,
    )
```

```python
import functools
import math

import jax
import jax.numpy as jnp
from jax import lax
from jax.experimental import pallas as pl
from jax.experimental.pallas import tpu as pltpu
from jax.sharding import PartitionSpec as P

NOPE = 128
ROPE = 64
VD = 128
LAT = 512
TOPK = 6


epsilon = 1e-06
rope_base = 10000.0


def rms_norm(values, gain):
    return values * lax.rsqrt(jnp.mean(values * values, axis=-1, keepdims=True) + epsilon) * gain


def rotate(values, positions):
    half_width = values.shape[-1] // 2
    frequency = rope_base ** (-jnp.arange(half_width, dtype=jnp.float32) * 2.0 / values.shape[-1])
    angles = positions.astype(jnp.float32)[..., None] * frequency
    cosines = jnp.cos(angles)
    sines = jnp.sin(angles)
    lower_half = values[..., :half_width]
    upper_half = values[..., half_width:]
    return jnp.concatenate(
        [lower_half * cosines - upper_half * sines, lower_half * sines + upper_half * cosines],
        axis=-1,
    )


def attend(
    prefill_rows,
    decode_rows,
    cached,
    prefill_len,
    decode_len,
    attn_gain,
    w_query,
    w_latent,
    latent_gain,
    key_up,
    value_up,
    w_out,
):
    tokens = jnp.concatenate([prefill_rows, decode_rows], axis=0)
    prefill_count = prefill_rows.shape[0]
    row_count = tokens.shape[0]
    head_count = w_query.shape[1] // (NOPE + ROPE)
    positions = jnp.concatenate(
        [prefill_len[0] + jnp.arange(prefill_count, dtype=jnp.int32), decode_len]
    )
    normed = rms_norm(tokens.astype(jnp.float32), attn_gain).astype(jnp.bfloat16)
    queries = jnp.dot(normed, w_query, preferred_element_type=jnp.float32).reshape(
        row_count, head_count, NOPE + ROPE
    )
    query_nope = queries[..., :NOPE].astype(jnp.bfloat16)
    query_rope = rotate(queries[..., NOPE:], positions[:, None]).astype(jnp.bfloat16)
    latent = jnp.dot(normed, w_latent, preferred_element_type=jnp.float32)
    latent_normed = rms_norm(latent[:, :LAT], latent_gain)
    new_keys = jnp.concatenate([latent_normed, rotate(latent[:, LAT:], positions)], axis=1).astype(
        jnp.bfloat16
    )
    key_heads = key_up.reshape(LAT, head_count, NOPE)
    absorbed = jnp.einsum(
        "rhn,lhn->rhl", query_nope, key_heads, preferred_element_type=jnp.float32
    ).astype(jnp.bfloat16)
    query_all = jnp.concatenate([absorbed, query_rope], axis=-1)
    factor = 1.0 / jnp.sqrt(jnp.float32(NOPE + ROPE))
    cache_len = cached.shape[1]
    prefill_keys = jnp.concatenate([cached[0], new_keys[:prefill_count]], axis=0)
    scores = (
        jnp.einsum(
            "chk,jk->chj",
            query_all[:prefill_count],
            prefill_keys,
            preferred_element_type=jnp.float32,
        )
        * factor
    )
    key_index = jnp.arange(cache_len + prefill_count, dtype=jnp.int32)
    row_index = jnp.arange(prefill_count, dtype=jnp.int32)
    visible = jnp.where(
        key_index[None, :] < cache_len,
        key_index[None, :] < prefill_len[0],
        key_index[None, :] - cache_len <= row_index[:, None],
    )
    expo = jnp.exp(jnp.where(visible[:, None, :], scores, -jnp.inf))
    attn_probs = (expo / jnp.sum(expo, axis=-1, keepdims=True)).astype(jnp.bfloat16)
    prefill_context = jnp.einsum(
        "chj,jl->chl", attn_probs, prefill_keys[:, :LAT], preferred_element_type=jnp.float32
    ).astype(jnp.bfloat16)
    decode_query = query_all[prefill_count:]
    decode_cache = cached[1:]
    own_keys = new_keys[prefill_count:]
    cache_scores = (
        jnp.einsum("dhk,dsk->dhs", decode_query, decode_cache, preferred_element_type=jnp.float32)
        * factor
    )
    self_scores = (
        jnp.einsum("dhk,dk->dh", decode_query, own_keys, preferred_element_type=jnp.float32)
        * factor
    )
    cache_visible = jnp.arange(cache_len, dtype=jnp.int32)[None, :] < decode_len[:, None]
    cache_expo = jnp.exp(jnp.where(cache_visible[:, None, :], cache_scores, -jnp.inf))
    self_expo = jnp.exp(self_scores)
    totals = jnp.sum(cache_expo, axis=-1) + self_expo
    cache_probs = (cache_expo / totals[..., None]).astype(jnp.bfloat16)
    self_probs = (self_expo / totals).astype(jnp.bfloat16)
    decode_context = jnp.einsum(
        "dhs,dsl->dhl", cache_probs, decode_cache[..., :LAT], preferred_element_type=jnp.float32
    )
    decode_context = (
        decode_context
        + self_probs.astype(jnp.float32)[..., None] * own_keys[:, None, :LAT].astype(jnp.float32)
    ).astype(jnp.bfloat16)
    context = jnp.concatenate([prefill_context, decode_context], axis=0)
    value_heads = value_up.reshape(LAT, head_count, VD)
    head_out = jnp.einsum(
        "rhl,lhv->rhv", context, value_heads, preferred_element_type=jnp.float32
    ).astype(jnp.bfloat16)
    return jnp.dot(
        head_out.reshape(row_count, head_count * VD), w_out, preferred_element_type=jnp.float32
    )


MESH = pl.DeviceIdType.MESH
SLAB = 80
PF = 64
FINAL = 8
HALF = 1024
CODE = 256


def place():
    e = lax.axis_index("ep")
    return e // 4, (e // 2) % 2, e % 2, lax.axis_index("vp")


def at(z, x, c, y):
    return {"ep": z * 4 + x * 2 + c, "vp": y}


def remote(src, dst, send, recv, target):
    return pltpu.make_async_remote_copy(
        src_ref=src, dst_ref=dst, send_sem=send, recv_sem=recv, device_id=target, device_id_type=MESH
    )


def layer_kernel(heads, prefill, decode, again, gain, last_gain, lgain, ids, mix, order, plen, dlen, wq_hbm, wl_hbm, cache_hbm, ku_hbm, vu_hbm, wo_hbm, wg_hbm, wu_hbm, wd_hbm, hw_hbm, out, logits, *scratch):
    (wg, wu, wd, hw, got, slab, prod, cin, xin, yin, t0, t1, y2, x2, s3, zin) = scratch[:16]
    (xn, hid, fb, cb, pf, fcin, fxin, f3, fzin, fg, rf, fn) = scratch[16:28]
    (w_sem, sw_s, sw_r, gz_s, gz_r, g_s, g_r) = scratch[28:35]
    (r_s, r_r, rz_s, rz_r, fr_s, fr_r, tree_s, tree_r) = scratch[35:43]
    (wq, wl, cache, ku, vu, wo, tok, tail, part, dense) = scratch[43:]
    f32, bf16 = jnp.float32, jnp.bfloat16
    nt = lambda a, b: lax.dot_general(a, b, (((1,), (1,)), ((), ())), preferred_element_type=f32)
    z, x, c, y = place()
    mine = z * 4 + x * 2 + c
    near = z + 1 - 2 * (z % 2)
    planes = [z, near, 3 - 3 * (z // 2), 2 - z // 2]
    to_x, to_y, to_c = at(z, 1 - x, c, y), at(z, x, c, 1 - y), at(z, x, 1 - c, y)
    to_d = at(z, 1 - x, c, 1 - y)
    square = [(1 - x, y, to_x), (x, 1 - y, to_y), (1 - x, 1 - y, to_d)]

    def along(zo):
        return at(zo, x, c, y)

    pairs = [(wg_hbm, wg), (wu_hbm, wu), (wd_hbm, wd), (hw_hbm, hw)]
    pairs += [(wq_hbm, wq), (wl_hbm, wl), (cache_hbm, cache), (ku_hbm, ku), (vu_hbm, vu), (wo_hbm, wo)]
    loads = [pltpu.make_async_copy(a, b, w_sem.at[i]) for i, (a, b) in enumerate(pairs)]
    for load in loads[4:] + loads[:4]:
        load.start()
    barrier = pltpu.get_barrier_semaphore()
    for target in [to_x, to_y, to_c, to_d] + [along(zo) for zo in planes[1:]]:
        pl.semaphore_signal(barrier, inc=1, device_id=target, device_id_type=MESH)
    sent = []

    def send(copy):
        copy.start()
        sent.append(copy)

    def cols(h):
        return pl.ds(pl.multiple_of(h * HALF, HALF), HALF)

    def swap(i):
        rows = pl.ds(PF, SLAB - PF) if i == 0 else pl.ds(0, PF)
        p = remote(part.at[rows, cols(1 - y)], got.at[rows, :], sw_s.at[i], sw_r.at[i], to_y)
        return p, p

    def same(ref_out, ref_in, s, r, target):
        return remote(ref_out, ref_out, s, r, target), remote(ref_in, ref_in, s, r, target)

    def gz(i):
        zo = planes[i]
        a, b = slab.at[z, c, x, y], slab.at[zo, c, x, y]
        return remote(a, a, gz_s.at[i - 1], gz_r.at[z], along(zo)), remote(b, b, gz_s.at[i - 1], gz_r.at[zo], along(zo))

    def gx(i):
        zo = planes[i]
        return same(slab.at[zo, c, x, y], slab.at[zo, c, 1 - x, y], g_s.at[0, i], g_r.at[0, i], to_x)

    def gy(i):
        zo = planes[i]
        return same(slab.at[zo, c, x, y], slab.at[zo, c, x, 1 - y], g_s.at[1, i], g_r.at[1, i], to_y)

    def dx(i):
        zo = planes[i]
        return same(
            slab.at[zo, c, x, 1 - y, 32:64], slab.at[zo, c, 1 - x, 1 - y, 32:64], g_s.at[2, i], g_r.at[2, i], to_x
        )

    def dy(i):
        zo = planes[i]
        return same(
            slab.at[zo, c, 1 - x, y, 0:32], slab.at[zo, c, 1 - x, 1 - y, 0:32], g_s.at[3, i], g_r.at[3, i], to_y
        )

    def gc(i):
        zo = planes[i]
        return same(slab.at[zo, c], slab.at[zo, 1 - c], g_s.at[4, i], g_r.at[4, i], to_c)

    def tree(k, block):
        def hop_z(i):
            zo = planes[i]
            return (
                remote(block(c, x, z), block(c, x, z), tree_s.at[k, i], tree_r.at[k, z], along(zo)),
                remote(block(c, x, zo), block(c, x, zo), tree_s.at[k, i], tree_r.at[k, zo], along(zo)),
            )

        return hop_z

    def hop(k, j, leaves, lands, target):
        return same(leaves, lands, tree_s.at[k, 4 + j], tree_r.at[k, 4 + j], target)

    code_z = tree(0, lambda co, xo, zo: cb.at[co, xo, zo])
    code_x = lambda: hop(0, 0, cb.at[c, x], cb.at[c, 1 - x], to_x)
    code_c = lambda: hop(0, 2, cb.at[c], cb.at[1 - c], to_c)
    first_z = tree(1, lambda co, xo, zo: fb.at[y, co, xo, zo])
    def around(k, ref):
        return [hop(k, j, ref.at[y, c, x], ref.at[yo, c, xo], to) for j, (xo, yo, to) in enumerate(square)]

    first_c = lambda: hop(1, 3, fb.at[:, c], fb.at[:, 1 - c], to_c)
    lz = tree(2, lambda co, xo, zo: fg.at[y, co, xo, zo])
    lc = lambda: hop(2, 3, fg.at[:, c], fg.at[:, 1 - c], to_c)

    tail[...] = jnp.zeros_like(tail)
    tail[0 : decode.shape[0], :] = decode[...].astype(f32)
    tail[decode.shape[0] : decode.shape[0] + 1, :] = prefill[PF - 16 : PF, :].astype(f32)[15:16]
    tok[0:PF, :] = prefill[...]
    tok[PF:SLAB, :] = tail[...].astype(bf16)
    dense[...] = jnp.zeros_like(dense)
    expert = lax.broadcasted_iota(jnp.int32, (16, ids.shape[1]), 0)
    named = jnp.zeros((16, ids.shape[1]), f32)
    for k in range(TOPK):
        named = named + jnp.where(ids[k : k + 1, :] == expert, mix[k : k + 1, :], 0.0)
    dense[:, 0 : ids.shape[1]] = named
    high = dense[...].astype(bf16)
    cb[c, x, z, :, 0:128] = high
    cb[c, x, z, :, 128:256] = (dense[...] - high.astype(f32)).astype(bf16)
    row = lax.broadcasted_iota(jnp.int32, (SLAB, 1), 0)
    length = jnp.where(row < PF, plen[0], 0)
    for j in range(decode.shape[0]):
        length = jnp.where(row == PF + j, dlen[j], length)
    position = jnp.where(row < PF, length + row, length).astype(f32)
    lane = lax.broadcasted_iota(jnp.int32, (1, ROPE), 1)
    upper = lane >= ROPE // 2
    power = jnp.where(upper, lane - ROPE // 2, lane).astype(f32)
    angles = position * jnp.exp(power * (-2.0 / ROPE * math.log(rope_base)))
    cosines = jnp.cos(angles)
    sines = jnp.where(upper, 1.0, -1.0) * jnp.sin(angles)
    pl.semaphore_wait(barrier, 7)
    for i in range(1, 4):
        send(code_z(i)[0])

    def turn(v):
        half = ROPE // 2
        return v * cosines + jnp.concatenate([v[:, half:], v[:, :half]], axis=1) * sines

    dot = functools.partial(jnp.dot, preferred_element_type=f32)
    normed = rms_norm(tok[...].astype(f32), again[...]).astype(bf16)
    loads[4].wait()
    queries = dot(normed, wq[...])
    loads[5].wait()
    latent = nt(normed, wl[...])
    key_lat = rms_norm(latent[:, :LAT], lgain[...]).astype(bf16)
    key_rope = turn(latent[:, LAT:]).astype(bf16)
    loads[6].wait()
    entries, cache_len = cache.shape[0], cache.shape[2]
    rows_of = PF + decode.shape[0]
    spare = SLAB - PF
    factor = 1.0 / jnp.sqrt(jnp.float32(NOPE + ROPE))
    loads[7].wait()
    absorbed, ropes = [], []
    for h in range(heads):
        base = h * (NOPE + ROPE)
        q_nope = queries[:, base : base + NOPE].astype(bf16)
        ropes.append(turn(queries[:, base + NOPE : base + NOPE + ROPE]).astype(bf16))
        absorbed.append(nt(q_nope, ku[:, h * NOPE : (h + 1) * NOPE]).astype(bf16))

    def share(lo, hi, held, old_seen, new_seen):
        q_lat = jnp.concatenate([a[lo:hi] for a in absorbed], axis=0)
        q_rope = jnp.concatenate([r[lo:hi] for r in ropes], axis=0)
        old = [dot(q_lat, cache[e, :LAT, :]) + dot(q_rope, cache[e, LAT:, :]) for e in held]
        old = (old[0] if len(held) == 1 else jnp.concatenate(old, axis=1)) * factor
        new = (nt(q_lat, key_lat[lo:hi]) + nt(q_rope, key_rope[lo:hi])) * factor
        old = jnp.exp(jnp.where(old_seen, old, -jnp.inf))
        new = jnp.exp(jnp.where(new_seen, new, -jnp.inf))
        total = jnp.sum(old, axis=1, keepdims=True) + jnp.sum(new, axis=1, keepdims=True)
        old = (old / total).astype(bf16)
        new = (new / total).astype(bf16)
        context = dot(new, key_lat[lo:hi])
        for i, e in enumerate(held):
            context = context + nt(old[:, i * cache_len : (i + 1) * cache_len], cache[e, :LAT, :])
        return context.astype(bf16)

    stacked = lax.broadcasted_iota(jnp.int32, (heads * PF, 1), 0) % PF
    key = lax.broadcasted_iota(jnp.int32, (1, cache_len), 1)
    col = lax.broadcasted_iota(jnp.int32, (1, PF), 1)
    prefill_context = share(0, PF, [0], key < plen[0], col <= stacked)
    stacked = lax.broadcasted_iota(jnp.int32, (heads * spare, 1), 0) % spare
    held = list(range(1, entries))
    seen = jnp.zeros((heads * spare, 1), jnp.int32)
    for j in range(decode.shape[0]):
        seen = jnp.where(stacked == j, dlen[j], seen)
    start = stacked * cache_len
    key = lax.broadcasted_iota(jnp.int32, (1, len(held) * cache_len), 1)
    col = lax.broadcasted_iota(jnp.int32, (1, spare), 1)
    decode_context = share(PF, SLAB, held, (key >= start) & (key < start + seen), col == stacked)
    loads[8].wait()
    values = []
    for h in range(heads):
        context = jnp.concatenate(
            [prefill_context[h * PF : (h + 1) * PF], decode_context[h * spare : (h + 1) * spare]], axis=0
        )
        value = dot(context, vu[:, h * VD : (h + 1) * VD])
        values.append(jnp.where(row == rows_of, value[PF - 1 : PF], value).astype(bf16))
    values = jnp.concatenate(values, axis=1)
    loads[9].wait()
    part[:, cols(1 - y)] = dot(values, wo[:, cols(1 - y)]).astype(bf16)
    send(swap(0)[0])
    send(swap(1)[0])
    part[:, cols(y)] = dot(values, wo[:, cols(y)]).astype(bf16)

    def fold(rows):
        return jnp.concatenate([rows[:, : HALF // 2], rows[:, HALF // 2 :]], axis=0).astype(bf16)

    swap(0)[1].wait_recv()
    rows = part[PF:SLAB, cols(y)].astype(f32) + got[PF:SLAB, :].astype(f32)
    rows = tok[PF:SLAB, cols(y)].astype(f32) + rows
    rf[...] = rows[:FINAL].astype(bf16).astype(f32)
    fb[y, c, x, z] = fold(rows[:FINAL])
    for i in range(1, 4):
        send(first_z(i)[0])
    swap(1)[1].wait_recv()
    rows = part[0:PF, cols(y)].astype(f32) + got[0:PF, :].astype(f32)
    slab[z, c, x, y] = (tok[0:PF, cols(y)].astype(f32) + rows).astype(bf16)

    def take(pair):
        pair[1].wait_recv()

    def spread(i):
        if i > 0:
            take(gz(i))
        send(gx(i)[0])
        send(gy(i)[0])

    def corner(i):
        take(gx(i))
        send(dy(i)[0])
        take(gy(i))
        send(dx(i)[0])

    def close(i):
        take(dx(i))
        take(dy(i))
        send(gc(i)[0])

    width = 2 * HALF

    def normalize(top, blocks):
        total = sum(jnp.sum(b * b, axis=1, keepdims=True) for b in blocks)
        scale = lax.rsqrt(total * (1.0 / width) + epsilon)
        count, wide = blocks[0].shape
        for k, b in enumerate(blocks):
            lo = k * wide
            xn[top : top + count, lo : lo + wide] = (b * scale * gain[:, lo : lo + wide]).astype(bf16)

    def unfold(ref):
        rows = ref[...].astype(f32).reshape(2, 16, 2 * FINAL, HALF // 2)
        return [
            rows[yo, :, q * FINAL : (q + 1) * FINAL].reshape(16 * FINAL, HALF // 2) for yo in range(2) for q in range(2)
        ]

    def gates_of(co, xo, zo, first, count):
        block = cb[co, xo, zo].astype(f32)
        expert = lax.broadcasted_iota(jnp.int32, block.shape, 0)
        row = jnp.sum(jnp.where(expert == mine, block, 0.0), axis=0, keepdims=True)
        row = row[:, 0:128] + row[:, 128:256]
        lane = lax.broadcasted_iota(jnp.int32, (count, 128), 1)
        index = lax.broadcasted_iota(jnp.int32, (count, 128), 0)
        spot = index + first
        spot = jnp.where(spot == PF + decode.shape[0], PF - 1, spot)
        return jnp.sum(jnp.where(lane == spot, row, 0.0), axis=1, keepdims=True)

    units = wg.shape[0]

    def expand(count):
        lo = 0
        while lo < units:
            n = min(256, units - lo)
            gated = nt(xn[0:count, :], wg[lo : lo + n, :])
            upward = nt(xn[0:count, :], wu[lo : lo + n, :])
            hid[0:count, lo : lo + n] = (jax.nn.silu(gated) * upward).astype(bf16)
            lo += n

    def contract(count, gates, store):
        for lo in range(0, width, 512):
            result = jnp.dot(hid[0:count, :], wd[:, lo : lo + 512], preferred_element_type=f32) * gates
            store(lo, result.astype(bf16))

    def enter(i):
        zo = planes[i]
        for s, (co, xo) in enumerate([(0, 0), (0, 1), (1, 0), (1, 1)]):
            normalize(s * PF, [slab[zo, co, xo, h].astype(f32) for h in range(2)])
        expand(4 * PF)

    def leave(i):
        zo = planes[i]
        gates = jnp.concatenate([gates_of(co, xo, zo, 0, PF) for co in range(2) for xo in range(2)], axis=0)

        def store(lo, result):
            h, at_col = lo // HALF, lo % HALF
            for s in range(4):
                prod[zo, s // 2, s % 2, h, :, at_col : at_col + 512] = result[s * PF : (s + 1) * PF]

        contract(4 * PF, gates, store)

    def add(a, b):
        return (a.astype(f32) + b.astype(f32)).astype(bf16)

    def rc(i):
        zo = planes[i]
        a = prod.at[zo, 1 - c]
        p = remote(a, cin.at[i], r_s.at[0, i], r_r.at[0, i], to_c)
        return p, p

    def rx1(i):
        p = remote(prod.at[planes[i], c, 1 - x, :, 0:32], xin.at[i], r_s.at[1, i], r_r.at[1, i], to_x)
        return p, p

    def ry1(i):
        p = remote(prod.at[planes[i], c, :, 1 - y, 32:64], yin.at[i], r_s.at[2, i], r_r.at[2, i], to_y)
        return p, p

    def ry2(i):
        p = remote(t0.at[i, 1 - y], y2.at[i], r_s.at[3, i], r_r.at[3, i], to_y)
        return p, p

    def rx2(i):
        p = remote(t1.at[i, 1 - x], x2.at[i], r_s.at[4, i], r_r.at[4, i], to_x)
        return p, p

    def rz(i, k):
        zo = planes[i]
        return (
            remote(s3.at[i, 32 * k : 32 * k + 32], zin.at[z, 32 * k : 32 * k + 32], rz_s.at[k, i - 1], rz_r.at[k, z], along(zo)),
            remote(s3.at[i, 32 * k : 32 * k + 32], zin.at[zo, 32 * k : 32 * k + 32], rz_s.at[k, i - 1], rz_r.at[k, zo], along(zo)),
        )

    def r0(i):
        send(rc(i)[0])

    def r1(i):
        zo = planes[i]
        take(rc(i))
        for xo in range(2):
            for h in range(2):
                prod[zo, c, xo, h] = add(prod[zo, c, xo, h], cin[i, xo, h])
        send(rx1(i)[0])
        send(ry1(i)[0])

    def r2(i):
        zo = planes[i]
        take(rx1(i))
        for h in range(2):
            t0[i, h] = add(prod[zo, c, x, h, 0:32], xin[i, h])
        send(ry2(i)[0])
        take(ry1(i))
        for xo in range(2):
            t1[i, xo] = add(prod[zo, c, xo, y, 32:64], yin[i, xo])
        send(rx2(i)[0])

    def r3(i):
        take(ry2(i))
        s3[i, 0:32] = add(t0[i, y], y2[i])
        if i > 0:
            send(rz(i, 0)[0])
        take(rx2(i))
        s3[i, 32:64] = add(t1[i, x], x2[i])
        if i > 0:
            send(rz(i, 1)[0])

    def enter_last():
        normalize(0, unfold(fb))
        expand(16 * FINAL)

    def leave_last():
        gates = jnp.concatenate(
            [gates_of(co, xo, zo, PF, FINAL) for co in range(2) for xo in range(2) for zo in range(4)], axis=0
        )

        def store(lo, result):
            h, at_col = lo // HALF, lo % HALF
            for s in range(4):
                pf[s // 2, h, s % 2, :, at_col : at_col + 512] = result[s * 32 : (s + 1) * 32]

        contract(16 * FINAL, gates, store)

    def fr():
        p = remote(pf.at[1 - c], fcin, fr_s.at[0], fr_r.at[0], to_c)
        return p, p

    def fr_around():
        return [
            (p, p)
            for p in [
                remote(pf.at[c, yo, xo], fxin.at[j], fr_s.at[7 + j], fr_r.at[7 + j], to)
                for j, (xo, yo, to) in enumerate(square)
            ]
        ]

    def frz(i):
        zo = planes[i]
        return (
            remote(f3.at[zo], fzin.at[z], fr_s.at[2 + i], fr_r.at[3 + z], along(zo)),
            remote(f3.at[zo], fzin.at[zo], fr_s.at[2 + i], fr_r.at[3 + zo], along(zo)),
        )

    def f_core():
        take(fr())
        for h in range(2):
            for xo in range(2):
                pf[c, h, xo] = add(pf[c, h, xo], fcin[h, xo])
        for p in fr_around():
            send(p[0])

    def f_xy():
        total = pf[c, y, x].astype(f32)
        for j, p in enumerate(fr_around()):
            take(p)
            total = total + fxin[j].astype(f32)
        f3[...] = total.reshape(4, FINAL, HALF)
        for i in range(1, 4):
            send(frz(i)[0])

    def f_z():
        total = f3[z]
        for i in range(1, 4):
            take(frz(i))
            total = total + fzin[planes[i]]
        rows = rf[...] + total
        out[PF : out.shape[0], :] = rows[: out.shape[0] - PF].astype(bf16)
        fg[y, c, x, z] = fold(rows)
        for i in range(1, 4):
            send(lz(i)[0])

    def l_z():
        for i in range(1, 4):
            take(lz(i))
        for p in around(2, fg):
            send(p[0])

    def l_xy():
        for p in around(2, fg):
            take(p)
        send(lc()[0])

    def head_rows():
        take(lc())
        blocks = unfold(fg)
        total = sum(jnp.sum(b * b, axis=1, keepdims=True) for b in blocks)
        scale = lax.rsqrt(total * (1.0 / width) + epsilon)
        asked = order.shape[1]
        count = decode.shape[0]

        def spot(owner, row):
            return ((owner % 2 * 2 + owner // 2 % 2) * 4 + owner // 4) * FINAL + row

        last = spot(lax.broadcasted_iota(jnp.int32, (1, 16), 1), count)
        ordered = spot(order[...] // count, order[...] % count)
        picks = [
            jnp.where(lax.broadcasted_iota(jnp.int32, (16 * FINAL, n), 0) == s, 1.0, 0.0).astype(bf16)
            for s, n in [(last, 16), (ordered, asked)]
        ]
        tn = lambda a, b: lax.dot_general(a, b, (((0,), (0,)), ((), ())), preferred_element_type=f32)
        for k, b in enumerate(blocks):
            lo = k * (HALF // 2)
            normed = (b * scale * last_gain[:, lo : lo + HALF // 2]).astype(bf16)
            fn[0:16, lo : lo + HALF // 2] = tn(picks[0], normed).astype(bf16)
            fn[16 : 16 + asked, lo : lo + HALF // 2] = tn(picks[1], normed).astype(bf16)

    def head_columns():
        loads[3].wait()
        lo = 0
        while lo < hw.shape[0]:
            n = min(256, hw.shape[0] - lo)
            logits[:, lo : lo + n] = nt(fn[...], hw[lo : lo + n, :])
            lo += n

    for i in range(1, 4):
        send(gz(i)[0])
    spread(0)
    for i in range(1, 4):
        take(code_z(i))
    send(code_x()[0])
    for i in range(1, 4):
        take(first_z(i))
    for p in around(1, fb):
        send(p[0])
    take(code_x())
    send(code_c()[0])
    corner(0)
    spread(1)
    for p in around(1, fb):
        take(p)
    send(first_c()[0])
    close(0)
    spread(2)
    take(code_c())
    take(first_c())
    loads[0].wait()
    loads[1].wait()
    enter_last()
    corner(1)
    loads[2].wait()
    leave_last()
    send(fr()[0])
    spread(3)
    take(gc(0))
    enter(0)
    close(1)
    corner(2)
    leave(0)
    r0(0)
    take(gc(1))
    r1(0)
    enter(1)
    close(2)
    corner(3)
    f_core()
    leave(1)
    r0(1)
    take(gc(2))
    enter(2)
    r1(1)
    close(3)
    leave(2)
    r0(2)
    r2(0)
    r1(2)
    f_xy()
    take(gc(3))
    enter(3)
    r2(1)
    r3(0)
    leave(3)
    r0(3)
    r2(2)
    f_z()
    r1(3)
    r3(1)
    l_z()
    r3(2)
    r2(3)
    l_xy()
    r3(3)
    head_rows()
    head_columns()
    total = slab[z, c, x, y].astype(f32) + s3[0].astype(f32)
    for i in [1, 2, 3]:
        take(rz(i, 0))
        take(rz(i, 1))
        total = total + zin[planes[i]].astype(f32)
    out[0:PF, :] = total.astype(bf16)
    for copy in sent:
        copy.wait_send()


def layer(small, lengths, attn_weights, expert_weights, row_count):
    width = small[0].shape[1]
    units, vocab = expert_weights[0].shape[0], expert_weights[3].shape[0]
    slots = 16 + small[8].shape[1]
    heads = attn_weights[0].shape[1] // (NOPE + ROPE)
    dma = pltpu.SemaphoreType.DMA
    buf = lambda *shape: pltpu.VMEM(shape, jnp.bfloat16)
    wide = lambda *shape: pltpu.VMEM(shape, jnp.float32)
    vmem = pl.BlockSpec(memory_space=pltpu.VMEM)
    hbm = pl.BlockSpec(memory_space=pltpu.HBM)
    smem = pl.BlockSpec(memory_space=pltpu.SMEM)
    return pl.pallas_call(
        functools.partial(layer_kernel, heads),
        name="layer",
        out_shape=(
            pltpu.VMEM((row_count, HALF), jnp.bfloat16),
            pltpu.VMEM((slots, vocab), jnp.float32),
        ),
        in_specs=[vmem] * 9 + [smem] * 2 + [hbm] * 10,
        out_specs=(vmem,) * 2,
        scratch_shapes=[
            buf(units, width),
            buf(units, width),
            buf(units, width),
            buf(vocab, width),
            buf(SLAB, HALF),
            buf(4, 2, 2, 2, PF, HALF),
            buf(4, 2, 2, 2, PF, HALF),
            buf(4, 2, 2, PF, HALF),
            buf(4, 2, 32, HALF),
            buf(4, 2, 32, HALF),
            buf(4, 2, 32, HALF),
            buf(4, 2, 32, HALF),
            buf(4, 32, HALF),
            buf(4, 32, HALF),
            buf(4, PF, HALF),
            buf(4, PF, HALF),
            buf(4 * PF, width),
            buf(4 * PF, units),
            buf(2, 2, 2, 4, 2 * FINAL, HALF // 2),
            buf(2, 2, 4, 16, CODE),
            buf(2, 2, 2, 32, HALF),
            buf(2, 2, 32, HALF),
            buf(3, 32, HALF),
            wide(4, FINAL, HALF),
            wide(4, FINAL, HALF),
            buf(2, 2, 2, 4, 2 * FINAL, HALF // 2),
            wide(FINAL, HALF),
            buf(slots, width),
            dma((10,)),
            dma((2,)),
            dma((2,)),
            dma((3,)),
            dma((4,)),
            dma((5, 4)),
            dma((5, 4)),
            dma((5, 4)),
            dma((5, 4)),
            dma((2, 3)),
            dma((2, 4)),
            dma((10,)),
            dma((10,)),
            dma((3, 8)),
            dma((3, 8)),
        ]
        + [pltpu.VMEM(a.shape, a.dtype) for a in attn_weights]
        + [buf(SLAB, width), wide(SLAB - PF, width), buf(SLAB, width), wide(16, 128)],
        compiler_params=pltpu.CompilerParams(
            collective_id=0, has_side_effects=True, vmem_limit_bytes=60 * 1024 * 1024
        ),
    )(*small, *lengths, *attn_weights, *expert_weights)


def on_block(
    prefill_tokens,
    decode_tokens,
    request_order,
    prefill_lengths,
    decode_lengths,
    latent_cache,
    attn_gain,
    w_query,
    w_latent,
    latent_gain,
    key_up,
    value_up,
    w_out,
    ffn_gain,
    expert_ids,
    expert_weights,
    w_gate,
    w_up,
    w_down,
    final_gain,
    head_weight,
):
    width = prefill_tokens.shape[1]
    small = (
        prefill_tokens,
        decode_tokens,
        attn_gain.reshape(1, width),
        ffn_gain.reshape(1, width),
        final_gain.reshape(1, width),
        latent_gain.reshape(1, LAT),
        expert_ids.T,
        expert_weights.T,
        request_order.reshape(1, -1),
    )
    return layer(
        small,
        (prefill_lengths, decode_lengths),
        (w_query, w_latent.T, jnp.swapaxes(latent_cache, 1, 2), key_up, value_up, w_out),
        (w_gate[0].T, w_up[0].T, w_down[0], head_weight.T),
        prefill_tokens.shape[0] + decode_tokens.shape[0],
    )


def on_device(
    prefill_tokens,
    decode_tokens,
    request_order,
    prefill_lengths,
    decode_lengths,
    latent_cache,
    attn_gain,
    w_query,
    w_latent,
    latent_gain,
    key_up,
    value_up,
    w_out,
    ffn_gain,
    expert_ids,
    expert_weights,
    w_gate,
    w_up,
    w_down,
    final_gain,
    head_weight,
):
    owners = lax.axis_size("ep")
    shards = lax.axis_size("vp")
    partial_attn = attend(
        prefill_tokens,
        decode_tokens,
        latent_cache,
        prefill_lengths,
        decode_lengths,
        attn_gain,
        w_query,
        w_latent,
        latent_gain,
        key_up,
        value_up,
        w_out,
    )
    attn = lax.psum(partial_attn, "vp")
    tokens = jnp.concatenate([prefill_tokens, decode_tokens], axis=0)
    resid = (tokens.astype(jnp.float32) + attn).astype(jnp.bfloat16)
    ffn_in = rms_norm(resid.astype(jnp.float32), ffn_gain).astype(jnp.bfloat16)
    row_count = tokens.shape[0]
    model_width = tokens.shape[1]
    share_width = model_width // shards
    capacity = max(2, min(row_count, row_count * TOPK * 2 // owners))
    flat_ids = expert_ids.reshape(-1)
    onehot = (flat_ids[:, None] == jnp.arange(owners, dtype=jnp.int32)[None, :]).astype(jnp.float32)
    entry = jnp.arange(flat_ids.shape[0], dtype=jnp.int32)
    before = (entry[:, None] > entry[None, :]).astype(jnp.bfloat16)
    earlier = jnp.dot(before, onehot.astype(jnp.bfloat16), preferred_element_type=jnp.float32)
    slot_index = jnp.sum(earlier * onehot, axis=1).astype(jnp.int32)
    target = flat_ids * capacity + slot_index
    source_rows = jnp.arange(row_count * TOPK, dtype=jnp.int32) // TOPK
    outgoing = (
        jnp.zeros((owners * capacity, model_width), jnp.bfloat16)
        .at[target]
        .set(ffn_in[source_rows])
    )
    outgoing = outgoing.reshape(owners, capacity, model_width)
    arrived = lax.all_to_all(outgoing, "ep", split_axis=0, concat_axis=0, tiled=True)
    item_count = arrived.shape[1]
    flattened = arrived.reshape(owners * item_count, model_width)
    gated = jnp.dot(flattened, w_gate[0], preferred_element_type=jnp.float32)
    upward = jnp.dot(flattened, w_up[0], preferred_element_type=jnp.float32)
    hidden_act = (jax.nn.silu(gated) * upward).astype(jnp.bfloat16)
    result = jnp.dot(hidden_act, w_down[0], preferred_element_type=jnp.float32).reshape(
        owners, item_count, model_width
    )
    summed = lax.psum_scatter(result, "vp", scatter_dimension=2, tiled=True)
    sent_back = lax.all_to_all(summed, "ep", split_axis=0, concat_axis=0, tiled=True)
    picked = sent_back.reshape(owners * capacity, sent_back.shape[2])[target]
    picked = picked.reshape(row_count, TOPK, sent_back.shape[2])
    routed_sum = jnp.sum(expert_weights[:, :, None] * picked, axis=1)
    column = lax.axis_index("vp") * share_width
    resid_share = lax.dynamic_slice_in_dim(resid, column, share_width, 1)
    layer_out = (resid_share.astype(jnp.float32) + routed_sum).astype(jnp.bfloat16)
    prefill_count = prefill_tokens.shape[0]
    decode_count = decode_tokens.shape[0]
    own_rows = layer_out[prefill_count - 1 :]
    everyone = lax.all_gather(own_rows, ("ep", "vp"), axis=0, tiled=True)
    everyone = everyone.reshape(owners, shards, 1 + decode_count, share_width)
    everyone = jnp.transpose(everyone, (0, 2, 1, 3)).reshape(owners, 1 + decode_count, model_width)
    prefill_last = everyone[:, 0]
    decode_rows = everyone[:, 1:].reshape(owners * decode_count, model_width)[request_order]
    final_rows = jnp.concatenate([prefill_last, decode_rows], axis=0)
    final_normed = rms_norm(final_rows.astype(jnp.float32), final_gain).astype(jnp.bfloat16)
    logits = jnp.dot(final_normed, head_weight, preferred_element_type=jnp.float32)
    return (layer_out, logits)


def solution(mesh):
    block = mesh.shape["vp"] == 2 and mesh.shape["ep"] == 16
    return jax.shard_map(
        on_block if block else on_device,
        mesh=mesh,
        in_specs=(
            P("ep", None),
            P("ep", None),
            P(),
            P("ep"),
            P("ep"),
            P("ep", None, None),
            P(),
            P(None, "vp"),
            P(),
            P(),
            P(None, "vp"),
            P(None, "vp"),
            P("vp", None),
            P(),
            P("ep", None),
            P("ep", None),
            P("ep", None, "vp"),
            P("ep", None, "vp"),
            P("ep", "vp", None),
            P(),
            P(None, ("ep", "vp")),
        ),
        out_specs=(P("ep", "vp"), P(None, ("ep", "vp"))),
        check_vma=False,
    )
```

```python
import functools
import math

import jax
import jax.numpy as jnp
from jax import lax
from jax.experimental import pallas as pl
from jax.experimental.pallas import tpu as pltpu
from jax.sharding import PartitionSpec as P

NOPE = 128
ROPE = 64
VD = 128
LAT = 512
TOPK = 6


epsilon = 1e-06
rope_base = 10000.0


def rms_norm(values, gain):
    return values * lax.rsqrt(jnp.mean(values * values, axis=-1, keepdims=True) + epsilon) * gain


def rotate(values, positions):
    half_width = values.shape[-1] // 2
    frequency = rope_base ** (-jnp.arange(half_width, dtype=jnp.float32) * 2.0 / values.shape[-1])
    angles = positions.astype(jnp.float32)[..., None] * frequency
    cosines = jnp.cos(angles)
    sines = jnp.sin(angles)
    lower_half = values[..., :half_width]
    upper_half = values[..., half_width:]
    return jnp.concatenate(
        [lower_half * cosines - upper_half * sines, lower_half * sines + upper_half * cosines],
        axis=-1,
    )


def attend(
    prefill_rows,
    decode_rows,
    cached,
    prefill_len,
    decode_len,
    attn_gain,
    w_query,
    w_latent,
    latent_gain,
    key_up,
    value_up,
    w_out,
):
    tokens = jnp.concatenate([prefill_rows, decode_rows], axis=0)
    prefill_count = prefill_rows.shape[0]
    row_count = tokens.shape[0]
    head_count = w_query.shape[1] // (NOPE + ROPE)
    positions = jnp.concatenate(
        [prefill_len[0] + jnp.arange(prefill_count, dtype=jnp.int32), decode_len]
    )
    normed = rms_norm(tokens.astype(jnp.float32), attn_gain).astype(jnp.bfloat16)
    queries = jnp.dot(normed, w_query, preferred_element_type=jnp.float32).reshape(
        row_count, head_count, NOPE + ROPE
    )
    query_nope = queries[..., :NOPE].astype(jnp.bfloat16)
    query_rope = rotate(queries[..., NOPE:], positions[:, None]).astype(jnp.bfloat16)
    latent = jnp.dot(normed, w_latent, preferred_element_type=jnp.float32)
    latent_normed = rms_norm(latent[:, :LAT], latent_gain)
    new_keys = jnp.concatenate([latent_normed, rotate(latent[:, LAT:], positions)], axis=1).astype(
        jnp.bfloat16
    )
    key_heads = key_up.reshape(LAT, head_count, NOPE)
    absorbed = jnp.einsum(
        "rhn,lhn->rhl", query_nope, key_heads, preferred_element_type=jnp.float32
    ).astype(jnp.bfloat16)
    query_all = jnp.concatenate([absorbed, query_rope], axis=-1)
    factor = 1.0 / jnp.sqrt(jnp.float32(NOPE + ROPE))
    cache_len = cached.shape[1]
    prefill_keys = jnp.concatenate([cached[0], new_keys[:prefill_count]], axis=0)
    scores = (
        jnp.einsum(
            "chk,jk->chj",
            query_all[:prefill_count],
            prefill_keys,
            preferred_element_type=jnp.float32,
        )
        * factor
    )
    key_index = jnp.arange(cache_len + prefill_count, dtype=jnp.int32)
    row_index = jnp.arange(prefill_count, dtype=jnp.int32)
    visible = jnp.where(
        key_index[None, :] < cache_len,
        key_index[None, :] < prefill_len[0],
        key_index[None, :] - cache_len <= row_index[:, None],
    )
    expo = jnp.exp(jnp.where(visible[:, None, :], scores, -jnp.inf))
    attn_probs = (expo / jnp.sum(expo, axis=-1, keepdims=True)).astype(jnp.bfloat16)
    prefill_context = jnp.einsum(
        "chj,jl->chl", attn_probs, prefill_keys[:, :LAT], preferred_element_type=jnp.float32
    ).astype(jnp.bfloat16)
    decode_query = query_all[prefill_count:]
    decode_cache = cached[1:]
    own_keys = new_keys[prefill_count:]
    cache_scores = (
        jnp.einsum("dhk,dsk->dhs", decode_query, decode_cache, preferred_element_type=jnp.float32)
        * factor
    )
    self_scores = (
        jnp.einsum("dhk,dk->dh", decode_query, own_keys, preferred_element_type=jnp.float32)
        * factor
    )
    cache_visible = jnp.arange(cache_len, dtype=jnp.int32)[None, :] < decode_len[:, None]
    cache_expo = jnp.exp(jnp.where(cache_visible[:, None, :], cache_scores, -jnp.inf))
    self_expo = jnp.exp(self_scores)
    totals = jnp.sum(cache_expo, axis=-1) + self_expo
    cache_probs = (cache_expo / totals[..., None]).astype(jnp.bfloat16)
    self_probs = (self_expo / totals).astype(jnp.bfloat16)
    decode_context = jnp.einsum(
        "dhs,dsl->dhl", cache_probs, decode_cache[..., :LAT], preferred_element_type=jnp.float32
    )
    decode_context = (
        decode_context
        + self_probs.astype(jnp.float32)[..., None] * own_keys[:, None, :LAT].astype(jnp.float32)
    ).astype(jnp.bfloat16)
    context = jnp.concatenate([prefill_context, decode_context], axis=0)
    value_heads = value_up.reshape(LAT, head_count, VD)
    head_out = jnp.einsum(
        "rhl,lhv->rhv", context, value_heads, preferred_element_type=jnp.float32
    ).astype(jnp.bfloat16)
    return jnp.dot(
        head_out.reshape(row_count, head_count * VD), w_out, preferred_element_type=jnp.float32
    )


MESH = pl.DeviceIdType.MESH
SLAB = 80
PF = 64
FINAL = 8
HALF = 1024
CODE = 256


def place():
    e = lax.axis_index("ep")
    return e // 4, (e // 2) % 2, e % 2, lax.axis_index("vp")


def at(z, x, c, y):
    return {"ep": z * 4 + x * 2 + c, "vp": y}


def remote(src, dst, send, recv, target):
    return pltpu.make_async_remote_copy(
        src_ref=src, dst_ref=dst, send_sem=send, recv_sem=recv, device_id=target, device_id_type=MESH
    )


def layer_kernel(heads, prefill, decode, again, gain, last_gain, lgain, ids, mix, order, plen, dlen, wq_hbm, wl_hbm, cache_hbm, ku_hbm, vu_hbm, wo_hbm, wg_hbm, wu_hbm, wd_hbm, hw_hbm, out, logits, *scratch):
    (wg, wu, wd, hw, got, slab, prod, cin, xin, yin, t0, t1, y2, x2, s3, zin) = scratch[:16]
    (xn, hid, fb, cb, pf, fcin, fxin, f3, fzin, fg, rf, fn) = scratch[16:28]
    (w_sem, sw_s, sw_r, gz_s, gz_r, g_s, g_r) = scratch[28:35]
    (r_s, r_r, rz_s, rz_r, fr_s, fr_r, tree_s, tree_r) = scratch[35:43]
    (wq, wl, cache, ku, vu, wo, tok, tail, part, dense) = scratch[43:]
    f32, bf16 = jnp.float32, jnp.bfloat16
    nt = lambda a, b: lax.dot_general(a, b, (((1,), (1,)), ((), ())), preferred_element_type=f32)
    z, x, c, y = place()
    mine = z * 4 + x * 2 + c
    near = z + 1 - 2 * (z % 2)
    planes = [z, near, 3 - 3 * (z // 2), 2 - z // 2]
    to_x, to_y, to_c = at(z, 1 - x, c, y), at(z, x, c, 1 - y), at(z, x, 1 - c, y)
    to_d = at(z, 1 - x, c, 1 - y)
    square = [(1 - x, y, to_x), (x, 1 - y, to_y), (1 - x, 1 - y, to_d)]

    def along(zo):
        return at(zo, x, c, y)

    pairs = [(wg_hbm, wg), (wu_hbm, wu), (wd_hbm, wd), (hw_hbm, hw)]
    pairs += [(wq_hbm, wq), (wl_hbm, wl), (cache_hbm, cache), (ku_hbm, ku), (vu_hbm, vu), (wo_hbm, wo)]
    loads = [pltpu.make_async_copy(a, b, w_sem.at[i]) for i, (a, b) in enumerate(pairs)]
    for load in loads[4:] + loads[:4]:
        load.start()
    barrier = pltpu.get_barrier_semaphore()
    for target in [to_x, to_y, to_c, to_d] + [along(zo) for zo in planes[1:]]:
        pl.semaphore_signal(barrier, inc=1, device_id=target, device_id_type=MESH)
    sent = []

    def send(copy):
        copy.start()
        sent.append(copy)

    def cols(h):
        return pl.ds(pl.multiple_of(h * HALF, HALF), HALF)

    def swap(i):
        rows = pl.ds(PF, SLAB - PF) if i == 0 else pl.ds(0, PF)
        p = remote(part.at[rows, cols(1 - y)], got.at[rows, :], sw_s.at[i], sw_r.at[i], to_y)
        return p, p

    def same(ref_out, ref_in, s, r, target):
        return remote(ref_out, ref_out, s, r, target), remote(ref_in, ref_in, s, r, target)

    def gz(i):
        zo = planes[i]
        a, b = slab.at[z, c, x, y], slab.at[zo, c, x, y]
        return remote(a, a, gz_s.at[i - 1], gz_r.at[z], along(zo)), remote(b, b, gz_s.at[i - 1], gz_r.at[zo], along(zo))

    def gx(i):
        zo = planes[i]
        return same(slab.at[zo, c, x, y], slab.at[zo, c, 1 - x, y], g_s.at[0, i], g_r.at[0, i], to_x)

    def gy(i):
        zo = planes[i]
        return same(slab.at[zo, c, x, y], slab.at[zo, c, x, 1 - y], g_s.at[1, i], g_r.at[1, i], to_y)

    def dx(i):
        zo = planes[i]
        return same(
            slab.at[zo, c, x, 1 - y, 32:64], slab.at[zo, c, 1 - x, 1 - y, 32:64], g_s.at[2, i], g_r.at[2, i], to_x
        )

    def dy(i):
        zo = planes[i]
        return same(
            slab.at[zo, c, 1 - x, y, 0:32], slab.at[zo, c, 1 - x, 1 - y, 0:32], g_s.at[3, i], g_r.at[3, i], to_y
        )

    def gc(i):
        zo = planes[i]
        return same(slab.at[zo, c], slab.at[zo, 1 - c], g_s.at[4, i], g_r.at[4, i], to_c)

    def tree(k, block):
        def hop_z(i):
            zo = planes[i]
            return (
                remote(block(c, x, z), block(c, x, z), tree_s.at[k, i], tree_r.at[k, z], along(zo)),
                remote(block(c, x, zo), block(c, x, zo), tree_s.at[k, i], tree_r.at[k, zo], along(zo)),
            )

        return hop_z

    def hop(k, j, leaves, lands, target):
        return same(leaves, lands, tree_s.at[k, 4 + j], tree_r.at[k, 4 + j], target)

    code_z = tree(0, lambda co, xo, zo: cb.at[co, xo, zo])
    code_x = lambda: hop(0, 0, cb.at[c, x], cb.at[c, 1 - x], to_x)
    code_c = lambda: hop(0, 2, cb.at[c], cb.at[1 - c], to_c)
    first_z = tree(1, lambda co, xo, zo: fb.at[y, co, xo, zo])
    def around(k, ref):
        return [hop(k, j, ref.at[y, c, x], ref.at[yo, c, xo], to) for j, (xo, yo, to) in enumerate(square)]

    first_c = lambda: hop(1, 3, fb.at[:, c], fb.at[:, 1 - c], to_c)
    lz = tree(2, lambda co, xo, zo: fg.at[y, co, xo, zo])
    lc = lambda: hop(2, 3, fg.at[:, c], fg.at[:, 1 - c], to_c)

    tail[...] = jnp.zeros_like(tail)
    tail[0 : decode.shape[0], :] = decode[...].astype(f32)
    tail[decode.shape[0] : decode.shape[0] + 1, :] = prefill[PF - 16 : PF, :].astype(f32)[15:16]
    tok[0:PF, :] = prefill[...]
    tok[PF:SLAB, :] = tail[...].astype(bf16)
    dense[...] = jnp.zeros_like(dense)
    expert = lax.broadcasted_iota(jnp.int32, (16, ids.shape[1]), 0)
    named = jnp.zeros((16, ids.shape[1]), f32)
    for k in range(TOPK):
        named = named + jnp.where(ids[k : k + 1, :] == expert, mix[k : k + 1, :], 0.0)
    dense[:, 0 : ids.shape[1]] = named
    high = dense[...].astype(bf16)
    cb[c, x, z, :, 0:128] = high
    cb[c, x, z, :, 128:256] = (dense[...] - high.astype(f32)).astype(bf16)
    row = lax.broadcasted_iota(jnp.int32, (SLAB, 1), 0)
    length = jnp.where(row < PF, plen[0], 0)
    for j in range(decode.shape[0]):
        length = jnp.where(row == PF + j, dlen[j], length)
    position = jnp.where(row < PF, length + row, length).astype(f32)
    lane = lax.broadcasted_iota(jnp.int32, (1, ROPE), 1)
    upper = lane >= ROPE // 2
    power = jnp.where(upper, lane - ROPE // 2, lane).astype(f32)
    angles = position * jnp.exp(power * (-2.0 / ROPE * math.log(rope_base)))
    cosines = jnp.cos(angles)
    sines = jnp.where(upper, 1.0, -1.0) * jnp.sin(angles)
    pl.semaphore_wait(barrier, 7)
    for i in range(1, 4):
        send(code_z(i)[0])

    def turn(v):
        half = ROPE // 2
        return v * cosines + jnp.concatenate([v[:, half:], v[:, :half]], axis=1) * sines

    dot = functools.partial(jnp.dot, preferred_element_type=f32)
    normed = rms_norm(tok[...].astype(f32), again[...]).astype(bf16)
    loads[4].wait()
    queries = dot(normed, wq[...])
    loads[5].wait()
    latent = nt(normed, wl[...])
    key_lat = rms_norm(latent[:, :LAT], lgain[...]).astype(bf16)
    key_rope = turn(latent[:, LAT:]).astype(bf16)
    loads[6].wait()
    entries, cache_len = cache.shape[0], cache.shape[2]
    rows_of = PF + decode.shape[0]
    spare = SLAB - PF
    factor = 1.0 / jnp.sqrt(jnp.float32(NOPE + ROPE))
    loads[7].wait()
    absorbed, ropes = [], []
    for h in range(heads):
        base = h * (NOPE + ROPE)
        q_nope = queries[:, base : base + NOPE].astype(bf16)
        ropes.append(turn(queries[:, base + NOPE : base + NOPE + ROPE]).astype(bf16))
        absorbed.append(nt(q_nope, ku[:, h * NOPE : (h + 1) * NOPE]).astype(bf16))

    def share(lo, hi, held, old_seen, new_seen):
        q_lat = jnp.concatenate([a[lo:hi] for a in absorbed], axis=0)
        q_rope = jnp.concatenate([r[lo:hi] for r in ropes], axis=0)
        old = [dot(q_lat, cache[e, :LAT, :]) + dot(q_rope, cache[e, LAT:, :]) for e in held]
        old = (old[0] if len(held) == 1 else jnp.concatenate(old, axis=1)) * factor
        new = (nt(q_lat, key_lat[lo:hi]) + nt(q_rope, key_rope[lo:hi])) * factor
        old = jnp.exp(jnp.where(old_seen, old, -jnp.inf))
        new = jnp.exp(jnp.where(new_seen, new, -jnp.inf))
        total = jnp.sum(old, axis=1, keepdims=True) + jnp.sum(new, axis=1, keepdims=True)
        old = (old / total).astype(bf16)
        new = (new / total).astype(bf16)
        context = dot(new, key_lat[lo:hi])
        for i, e in enumerate(held):
            context = context + nt(old[:, i * cache_len : (i + 1) * cache_len], cache[e, :LAT, :])
        return context.astype(bf16)

    stacked = lax.broadcasted_iota(jnp.int32, (heads * PF, 1), 0) % PF
    key = lax.broadcasted_iota(jnp.int32, (1, cache_len), 1)
    col = lax.broadcasted_iota(jnp.int32, (1, PF), 1)
    prefill_context = share(0, PF, [0], key < plen[0], col <= stacked)
    stacked = lax.broadcasted_iota(jnp.int32, (heads * spare, 1), 0) % spare
    held = list(range(1, entries))
    seen = jnp.zeros((heads * spare, 1), jnp.int32)
    for j in range(decode.shape[0]):
        seen = jnp.where(stacked == j, dlen[j], seen)
    start = stacked * cache_len
    key = lax.broadcasted_iota(jnp.int32, (1, len(held) * cache_len), 1)
    col = lax.broadcasted_iota(jnp.int32, (1, spare), 1)
    decode_context = share(PF, SLAB, held, (key >= start) & (key < start + seen), col == stacked)
    loads[8].wait()
    values = []
    for h in range(heads):
        context = jnp.concatenate(
            [prefill_context[h * PF : (h + 1) * PF], decode_context[h * spare : (h + 1) * spare]], axis=0
        )
        value = dot(context, vu[:, h * VD : (h + 1) * VD])
        values.append(jnp.where(row == rows_of, value[PF - 1 : PF], value).astype(bf16))
    values = jnp.concatenate(values, axis=1)
    loads[9].wait()
    part[:, cols(1 - y)] = dot(values, wo[:, cols(1 - y)]).astype(bf16)
    send(swap(0)[0])
    send(swap(1)[0])
    part[:, cols(y)] = dot(values, wo[:, cols(y)]).astype(bf16)

    def fold(rows):
        return jnp.concatenate([rows[:, : HALF // 2], rows[:, HALF // 2 :]], axis=0).astype(bf16)

    swap(0)[1].wait_recv()
    rows = part[PF:SLAB, cols(y)].astype(f32) + got[PF:SLAB, :].astype(f32)
    rows = tok[PF:SLAB, cols(y)].astype(f32) + rows
    rf[...] = rows[:FINAL].astype(bf16).astype(f32)
    fb[y, c, x, z] = fold(rows[:FINAL])
    for i in range(1, 4):
        send(first_z(i)[0])
    swap(1)[1].wait_recv()
    rows = part[0:PF, cols(y)].astype(f32) + got[0:PF, :].astype(f32)
    slab[z, c, x, y] = (tok[0:PF, cols(y)].astype(f32) + rows).astype(bf16)

    def take(pair):
        pair[1].wait_recv()

    def spread(i):
        if i > 0:
            take(gz(i))
        send(gx(i)[0])
        send(gy(i)[0])

    def corner(i):
        take(gx(i))
        send(dy(i)[0])
        take(gy(i))
        send(dx(i)[0])

    def close(i):
        take(dx(i))
        take(dy(i))
        send(gc(i)[0])

    width = 2 * HALF

    def normalize(top, blocks):
        total = sum(jnp.sum(b * b, axis=1, keepdims=True) for b in blocks)
        scale = lax.rsqrt(total * (1.0 / width) + epsilon)
        count, wide = blocks[0].shape
        for k, b in enumerate(blocks):
            lo = k * wide
            xn[top : top + count, lo : lo + wide] = (b * scale * gain[:, lo : lo + wide]).astype(bf16)

    def unfold(ref):
        rows = ref[...].astype(f32).reshape(2, 16, 2 * FINAL, HALF // 2)
        return [
            rows[yo, :, q * FINAL : (q + 1) * FINAL].reshape(16 * FINAL, HALF // 2) for yo in range(2) for q in range(2)
        ]

    def gates_of(co, xo, zo, first, count):
        block = cb[co, xo, zo].astype(f32)
        expert = lax.broadcasted_iota(jnp.int32, block.shape, 0)
        row = jnp.sum(jnp.where(expert == mine, block, 0.0), axis=0, keepdims=True)
        row = row[:, 0:128] + row[:, 128:256]
        lane = lax.broadcasted_iota(jnp.int32, (count, 128), 1)
        index = lax.broadcasted_iota(jnp.int32, (count, 128), 0)
        spot = index + first
        spot = jnp.where(spot == PF + decode.shape[0], PF - 1, spot)
        return jnp.sum(jnp.where(lane == spot, row, 0.0), axis=1, keepdims=True)

    units = wg.shape[0]

    def expand(count):
        lo = 0
        while lo < units:
            n = min(256, units - lo)
            gated = nt(xn[0:count, :], wg[lo : lo + n, :])
            upward = nt(xn[0:count, :], wu[lo : lo + n, :])
            hid[0:count, lo : lo + n] = (jax.nn.silu(gated) * upward).astype(bf16)
            lo += n

    def contract(count, gates, store):
        for lo in range(0, width, 512):
            result = jnp.dot(hid[0:count, :], wd[:, lo : lo + 512], preferred_element_type=f32) * gates
            store(lo, result.astype(bf16))

    def enter(i):
        zo = planes[i]
        for s, (co, xo) in enumerate([(0, 0), (0, 1), (1, 0), (1, 1)]):
            normalize(s * PF, [slab[zo, co, xo, h].astype(f32) for h in range(2)])
        expand(4 * PF)

    def leave(i):
        zo = planes[i]
        gates = jnp.concatenate([gates_of(co, xo, zo, 0, PF) for co in range(2) for xo in range(2)], axis=0)

        def store(lo, result):
            h, at_col = lo // HALF, lo % HALF
            for s in range(4):
                prod[zo, s // 2, s % 2, h, :, at_col : at_col + 512] = result[s * PF : (s + 1) * PF]

        contract(4 * PF, gates, store)

    def add(a, b):
        return (a.astype(f32) + b.astype(f32)).astype(bf16)

    def rc(i):
        zo = planes[i]
        a = prod.at[zo, 1 - c]
        p = remote(a, cin.at[i], r_s.at[0, i], r_r.at[0, i], to_c)
        return p, p

    def rx1(i):
        p = remote(prod.at[planes[i], c, 1 - x, :, 0:32], xin.at[i], r_s.at[1, i], r_r.at[1, i], to_x)
        return p, p

    def ry1(i):
        p = remote(prod.at[planes[i], c, :, 1 - y, 32:64], yin.at[i], r_s.at[2, i], r_r.at[2, i], to_y)
        return p, p

    def ry2(i):
        p = remote(t0.at[i, 1 - y], y2.at[i], r_s.at[3, i], r_r.at[3, i], to_y)
        return p, p

    def rx2(i):
        p = remote(t1.at[i, 1 - x], x2.at[i], r_s.at[4, i], r_r.at[4, i], to_x)
        return p, p

    def rz(i, k):
        zo = planes[i]
        return (
            remote(s3.at[i, 32 * k : 32 * k + 32], zin.at[z, 32 * k : 32 * k + 32], rz_s.at[k, i - 1], rz_r.at[k, z], along(zo)),
            remote(s3.at[i, 32 * k : 32 * k + 32], zin.at[zo, 32 * k : 32 * k + 32], rz_s.at[k, i - 1], rz_r.at[k, zo], along(zo)),
        )

    def r0(i):
        send(rc(i)[0])

    def r1(i):
        zo = planes[i]
        take(rc(i))
        for xo in range(2):
            for h in range(2):
                prod[zo, c, xo, h] = add(prod[zo, c, xo, h], cin[i, xo, h])
        send(rx1(i)[0])
        send(ry1(i)[0])

    def r2(i):
        zo = planes[i]
        take(rx1(i))
        for h in range(2):
            t0[i, h] = add(prod[zo, c, x, h, 0:32], xin[i, h])
        send(ry2(i)[0])
        take(ry1(i))
        for xo in range(2):
            t1[i, xo] = add(prod[zo, c, xo, y, 32:64], yin[i, xo])
        send(rx2(i)[0])

    def r3(i):
        take(ry2(i))
        s3[i, 0:32] = add(t0[i, y], y2[i])
        if i > 0:
            send(rz(i, 0)[0])
        take(rx2(i))
        s3[i, 32:64] = add(t1[i, x], x2[i])
        if i > 0:
            send(rz(i, 1)[0])

    def enter_last():
        normalize(0, unfold(fb))
        expand(16 * FINAL)

    def leave_last():
        gates = jnp.concatenate(
            [gates_of(co, xo, zo, PF, FINAL) for co in range(2) for xo in range(2) for zo in range(4)], axis=0
        )

        def store(lo, result):
            h, at_col = lo // HALF, lo % HALF
            for s in range(4):
                pf[s // 2, h, s % 2, :, at_col : at_col + 512] = result[s * 32 : (s + 1) * 32]

        contract(16 * FINAL, gates, store)

    def fr():
        p = remote(pf.at[1 - c], fcin, fr_s.at[0], fr_r.at[0], to_c)
        return p, p

    def fr_around():
        return [
            (p, p)
            for p in [
                remote(pf.at[c, yo, xo], fxin.at[j], fr_s.at[7 + j], fr_r.at[7 + j], to)
                for j, (xo, yo, to) in enumerate(square)
            ]
        ]

    def frz(i):
        zo = planes[i]
        return (
            remote(f3.at[zo], fzin.at[z], fr_s.at[2 + i], fr_r.at[3 + z], along(zo)),
            remote(f3.at[zo], fzin.at[zo], fr_s.at[2 + i], fr_r.at[3 + zo], along(zo)),
        )

    def f_core():
        take(fr())
        for h in range(2):
            for xo in range(2):
                pf[c, h, xo] = add(pf[c, h, xo], fcin[h, xo])
        for p in fr_around():
            send(p[0])

    def f_xy():
        total = pf[c, y, x].astype(f32)
        for j, p in enumerate(fr_around()):
            take(p)
            total = total + fxin[j].astype(f32)
        f3[...] = total.reshape(4, FINAL, HALF)
        for i in range(1, 4):
            send(frz(i)[0])

    def f_z():
        total = f3[z]
        for i in range(1, 4):
            take(frz(i))
            total = total + fzin[planes[i]]
        rows = rf[...] + total
        out[PF : out.shape[0], :] = rows[: out.shape[0] - PF].astype(bf16)
        fg[y, c, x, z] = fold(rows)
        for i in range(1, 4):
            send(lz(i)[0])

    def l_z():
        for i in range(1, 4):
            take(lz(i))
        for p in around(2, fg):
            send(p[0])

    def l_xy():
        for p in around(2, fg):
            take(p)
        send(lc()[0])

    def head_rows():
        take(lc())
        blocks = unfold(fg)
        total = sum(jnp.sum(b * b, axis=1, keepdims=True) for b in blocks)
        scale = lax.rsqrt(total * (1.0 / width) + epsilon)
        asked = order.shape[1]
        count = decode.shape[0]

        def spot(owner, row):
            return ((owner % 2 * 2 + owner // 2 % 2) * 4 + owner // 4) * FINAL + row

        last = spot(lax.broadcasted_iota(jnp.int32, (1, 16), 1), count)
        ordered = spot(order[...] // count, order[...] % count)
        picks = [
            jnp.where(lax.broadcasted_iota(jnp.int32, (16 * FINAL, n), 0) == s, 1.0, 0.0).astype(bf16)
            for s, n in [(last, 16), (ordered, asked)]
        ]
        tn = lambda a, b: lax.dot_general(a, b, (((0,), (0,)), ((), ())), preferred_element_type=f32)
        for k, b in enumerate(blocks):
            lo = k * (HALF // 2)
            normed = (b * scale * last_gain[:, lo : lo + HALF // 2]).astype(bf16)
            fn[0:16, lo : lo + HALF // 2] = tn(picks[0], normed).astype(bf16)
            fn[16 : 16 + asked, lo : lo + HALF // 2] = tn(picks[1], normed).astype(bf16)

    def head_columns():
        loads[3].wait()
        lo = 0
        while lo < hw.shape[0]:
            n = min(256, hw.shape[0] - lo)
            logits[:, lo : lo + n] = nt(fn[...], hw[lo : lo + n, :])
            lo += n

    for i in range(1, 4):
        send(gz(i)[0])
    spread(0)
    for i in range(1, 4):
        take(first_z(i))
    for p in around(1, fb):
        send(p[0])
    for i in range(1, 4):
        take(code_z(i))
    send(code_x()[0])
    corner(0)
    spread(1)
    take(code_x())
    send(code_c()[0])
    for p in around(1, fb):
        take(p)
    send(first_c()[0])
    close(0)
    spread(2)
    take(code_c())
    take(first_c())
    loads[0].wait()
    loads[1].wait()
    enter_last()
    corner(1)
    loads[2].wait()
    leave_last()
    send(fr()[0])
    spread(3)
    take(gc(0))
    enter(0)
    close(1)
    corner(2)
    leave(0)
    r0(0)
    take(gc(1))
    r1(0)
    enter(1)
    f_core()
    close(2)
    corner(3)
    leave(1)
    r0(1)
    take(gc(2))
    enter(2)
    r1(1)
    close(3)
    leave(2)
    r0(2)
    r2(0)
    r1(2)
    f_xy()
    take(gc(3))
    enter(3)
    r2(1)
    r3(0)
    leave(3)
    r0(3)
    r2(2)
    f_z()
    r1(3)
    r3(1)
    l_z()
    r3(2)
    r2(3)
    l_xy()
    r3(3)
    head_rows()
    head_columns()
    total = slab[z, c, x, y].astype(f32) + s3[0].astype(f32)
    for i in [1, 2, 3]:
        take(rz(i, 0))
        take(rz(i, 1))
        total = total + zin[planes[i]].astype(f32)
    out[0:PF, :] = total.astype(bf16)
    for copy in sent:
        copy.wait_send()


def layer(small, lengths, attn_weights, expert_weights, row_count):
    width = small[0].shape[1]
    units, vocab = expert_weights[0].shape[0], expert_weights[3].shape[0]
    slots = 16 + small[8].shape[1]
    heads = attn_weights[0].shape[1] // (NOPE + ROPE)
    dma = pltpu.SemaphoreType.DMA
    buf = lambda *shape: pltpu.VMEM(shape, jnp.bfloat16)
    wide = lambda *shape: pltpu.VMEM(shape, jnp.float32)
    vmem = pl.BlockSpec(memory_space=pltpu.VMEM)
    hbm = pl.BlockSpec(memory_space=pltpu.HBM)
    smem = pl.BlockSpec(memory_space=pltpu.SMEM)
    return pl.pallas_call(
        functools.partial(layer_kernel, heads),
        name="layer",
        out_shape=(
            pltpu.VMEM((row_count, HALF), jnp.bfloat16),
            pltpu.VMEM((slots, vocab), jnp.float32),
        ),
        in_specs=[vmem] * 9 + [smem] * 2 + [hbm] * 10,
        out_specs=(vmem,) * 2,
        scratch_shapes=[
            buf(units, width),
            buf(units, width),
            buf(units, width),
            buf(vocab, width),
            buf(SLAB, HALF),
            buf(4, 2, 2, 2, PF, HALF),
            buf(4, 2, 2, 2, PF, HALF),
            buf(4, 2, 2, PF, HALF),
            buf(4, 2, 32, HALF),
            buf(4, 2, 32, HALF),
            buf(4, 2, 32, HALF),
            buf(4, 2, 32, HALF),
            buf(4, 32, HALF),
            buf(4, 32, HALF),
            buf(4, PF, HALF),
            buf(4, PF, HALF),
            buf(4 * PF, width),
            buf(4 * PF, units),
            buf(2, 2, 2, 4, 2 * FINAL, HALF // 2),
            buf(2, 2, 4, 16, CODE),
            buf(2, 2, 2, 32, HALF),
            buf(2, 2, 32, HALF),
            buf(3, 32, HALF),
            wide(4, FINAL, HALF),
            wide(4, FINAL, HALF),
            buf(2, 2, 2, 4, 2 * FINAL, HALF // 2),
            wide(FINAL, HALF),
            buf(slots, width),
            dma((10,)),
            dma((2,)),
            dma((2,)),
            dma((3,)),
            dma((4,)),
            dma((5, 4)),
            dma((5, 4)),
            dma((5, 4)),
            dma((5, 4)),
            dma((2, 3)),
            dma((2, 4)),
            dma((10,)),
            dma((10,)),
            dma((3, 8)),
            dma((3, 8)),
        ]
        + [pltpu.VMEM(a.shape, a.dtype) for a in attn_weights]
        + [buf(SLAB, width), wide(SLAB - PF, width), buf(SLAB, width), wide(16, 128)],
        compiler_params=pltpu.CompilerParams(
            collective_id=0, has_side_effects=True, vmem_limit_bytes=60 * 1024 * 1024
        ),
    )(*small, *lengths, *attn_weights, *expert_weights)


def on_block(
    prefill_tokens,
    decode_tokens,
    request_order,
    prefill_lengths,
    decode_lengths,
    latent_cache,
    attn_gain,
    w_query,
    w_latent,
    latent_gain,
    key_up,
    value_up,
    w_out,
    ffn_gain,
    expert_ids,
    expert_weights,
    w_gate,
    w_up,
    w_down,
    final_gain,
    head_weight,
):
    width = prefill_tokens.shape[1]
    small = (
        prefill_tokens,
        decode_tokens,
        attn_gain.reshape(1, width),
        ffn_gain.reshape(1, width),
        final_gain.reshape(1, width),
        latent_gain.reshape(1, LAT),
        expert_ids.T,
        expert_weights.T,
        request_order.reshape(1, -1),
    )
    return layer(
        small,
        (prefill_lengths, decode_lengths),
        (w_query, w_latent.T, jnp.swapaxes(latent_cache, 1, 2), key_up, value_up, w_out),
        (w_gate[0].T, w_up[0].T, w_down[0], head_weight.T),
        prefill_tokens.shape[0] + decode_tokens.shape[0],
    )


def on_device(
    prefill_tokens,
    decode_tokens,
    request_order,
    prefill_lengths,
    decode_lengths,
    latent_cache,
    attn_gain,
    w_query,
    w_latent,
    latent_gain,
    key_up,
    value_up,
    w_out,
    ffn_gain,
    expert_ids,
    expert_weights,
    w_gate,
    w_up,
    w_down,
    final_gain,
    head_weight,
):
    owners = lax.axis_size("ep")
    shards = lax.axis_size("vp")
    partial_attn = attend(
        prefill_tokens,
        decode_tokens,
        latent_cache,
        prefill_lengths,
        decode_lengths,
        attn_gain,
        w_query,
        w_latent,
        latent_gain,
        key_up,
        value_up,
        w_out,
    )
    attn = lax.psum(partial_attn, "vp")
    tokens = jnp.concatenate([prefill_tokens, decode_tokens], axis=0)
    resid = (tokens.astype(jnp.float32) + attn).astype(jnp.bfloat16)
    ffn_in = rms_norm(resid.astype(jnp.float32), ffn_gain).astype(jnp.bfloat16)
    row_count = tokens.shape[0]
    model_width = tokens.shape[1]
    share_width = model_width // shards
    capacity = max(2, min(row_count, row_count * TOPK * 2 // owners))
    flat_ids = expert_ids.reshape(-1)
    onehot = (flat_ids[:, None] == jnp.arange(owners, dtype=jnp.int32)[None, :]).astype(jnp.float32)
    entry = jnp.arange(flat_ids.shape[0], dtype=jnp.int32)
    before = (entry[:, None] > entry[None, :]).astype(jnp.bfloat16)
    earlier = jnp.dot(before, onehot.astype(jnp.bfloat16), preferred_element_type=jnp.float32)
    slot_index = jnp.sum(earlier * onehot, axis=1).astype(jnp.int32)
    target = flat_ids * capacity + slot_index
    source_rows = jnp.arange(row_count * TOPK, dtype=jnp.int32) // TOPK
    outgoing = (
        jnp.zeros((owners * capacity, model_width), jnp.bfloat16)
        .at[target]
        .set(ffn_in[source_rows])
    )
    outgoing = outgoing.reshape(owners, capacity, model_width)
    arrived = lax.all_to_all(outgoing, "ep", split_axis=0, concat_axis=0, tiled=True)
    item_count = arrived.shape[1]
    flattened = arrived.reshape(owners * item_count, model_width)
    gated = jnp.dot(flattened, w_gate[0], preferred_element_type=jnp.float32)
    upward = jnp.dot(flattened, w_up[0], preferred_element_type=jnp.float32)
    hidden_act = (jax.nn.silu(gated) * upward).astype(jnp.bfloat16)
    result = jnp.dot(hidden_act, w_down[0], preferred_element_type=jnp.float32).reshape(
        owners, item_count, model_width
    )
    summed = lax.psum_scatter(result, "vp", scatter_dimension=2, tiled=True)
    sent_back = lax.all_to_all(summed, "ep", split_axis=0, concat_axis=0, tiled=True)
    picked = sent_back.reshape(owners * capacity, sent_back.shape[2])[target]
    picked = picked.reshape(row_count, TOPK, sent_back.shape[2])
    routed_sum = jnp.sum(expert_weights[:, :, None] * picked, axis=1)
    column = lax.axis_index("vp") * share_width
    resid_share = lax.dynamic_slice_in_dim(resid, column, share_width, 1)
    layer_out = (resid_share.astype(jnp.float32) + routed_sum).astype(jnp.bfloat16)
    prefill_count = prefill_tokens.shape[0]
    decode_count = decode_tokens.shape[0]
    own_rows = layer_out[prefill_count - 1 :]
    everyone = lax.all_gather(own_rows, ("ep", "vp"), axis=0, tiled=True)
    everyone = everyone.reshape(owners, shards, 1 + decode_count, share_width)
    everyone = jnp.transpose(everyone, (0, 2, 1, 3)).reshape(owners, 1 + decode_count, model_width)
    prefill_last = everyone[:, 0]
    decode_rows = everyone[:, 1:].reshape(owners * decode_count, model_width)[request_order]
    final_rows = jnp.concatenate([prefill_last, decode_rows], axis=0)
    final_normed = rms_norm(final_rows.astype(jnp.float32), final_gain).astype(jnp.bfloat16)
    logits = jnp.dot(final_normed, head_weight, preferred_element_type=jnp.float32)
    return (layer_out, logits)


def solution(mesh):
    block = mesh.shape["vp"] == 2 and mesh.shape["ep"] == 16
    return jax.shard_map(
        on_block if block else on_device,
        mesh=mesh,
        in_specs=(
            P("ep", None),
            P("ep", None),
            P(),
            P("ep"),
            P("ep"),
            P("ep", None, None),
            P(),
            P(None, "vp"),
            P(),
            P(),
            P(None, "vp"),
            P(None, "vp"),
            P("vp", None),
            P(),
            P("ep", None),
            P("ep", None),
            P("ep", None, "vp"),
            P("ep", None, "vp"),
            P("ep", "vp", None),
            P(),
            P(None, ("ep", "vp")),
        ),
        out_specs=(P("ep", "vp"), P(None, ("ep", "vp"))),
        check_vma=False,
    )
```
